32 devices in a mesh: cell: 2 (over x), ap: 8 (over z, y), sc: 2 (over core).
Axes of the slice: x: 2, y: 2, z: 4, core: 2. Of those that a mesh axis runs over, the one named last changes fastest.
Arguments:
- unsmoothed_link_guesses: bfloat16 [32, 4, 2, 128, 2048], P(('cell', 'ap'), None, None, None, 'sc'), parts along dimension 0, may hold values from -24 to 24
- received: bfloat16 [32, 4, 2, 4, 2048], P(('cell', 'ap'), None, None, None, 'sc'), parts along dimension 0, may hold values from -6 to 6
- user_power: float32 [256], P('cell'), parts along dimension 0, may hold values from 0.25 to 4
- noise_power: float32 [32], P(('cell', 'ap')), parts along dimension 0, may hold values from 0.1 to 1
- ap_gain: float32 [32, 128], P(('cell', 'ap')), parts along dimension 0, may hold values from 0.5 to 4
- user_cluster: int32 [256], P('cell'), parts along dimension 0, may hold values from 0 to 15, as said below
- serving: int32 [32, 16], P('cell'), parts along dimension 0, may hold values from 0 to 1, as said below
- cluster_owner: int32 [32, 1], P('cell'), parts along dimension 0, may hold values from 0 to 7, as said below
Outputs:
- estimates: float32 [64, 8, 4, 2, 2048], P(('cell', 'ap'), None, None, None, 'sc'), parts along dimension 0
The draws below stay inside these ranges and needn't reach their ends.
There are 2 independent parts, one for each index of `cell`. The reference program is written for one: setup_inputs(seed, part) draws one part's arguments, and reference() takes and returns one part's arrays. A program takes and returns all parts, laid end to end along the dimension named above; each array names one. Nothing has to cross between parts.
Inputs may be any that keep to these rules, and one draw needn't show every extreme that they name: `user_cluster`: each of the 16 clusters holds exactly 8 users. `serving`: column a belongs to index a // 2 of ap. Where a cluster is served by an index of ap, at least one of its access points serves it. Of the clusters that one index of ap serves, at most 2 have the same owner; in every draw some owner has exactly 2 of its clusters served by every index of ap. `cluster_owner`: at most 4 clusters have the same owner, and some owner has exactly 4.
All inputs are finite; a program needn't handle non-finite values.
Results may differ from the reference program's by a relative error of at most 0.017.
Values may be sent and summed in bfloat16 or wider, within the bound.
A program may use at most 128 MiB of HBM per device.

```python
import math
import jax
import jax.numpy as jnp
from jax import lax

AP_DEV = 2
ANTENNA_COUNT = 4
TONE_NUMBER = 2048
TAPS = 64
DATA_SYMBOLS = 4
CU = 8
OWN_MAX = 4
PEER_MAX = 2
ACCESS_POINTS = 16
CLUSTERS = 16
USER_TOTAL = 128
SLOTS = 32
N_AP = 8


def owner_and_serving(key):
    base_key = jax.random.fold_in(key, 11)
    subkeys = jax.random.split(base_key, 6)
    devices = ACCESS_POINTS // AP_DEV
    slot_count = devices * OWN_MAX
    heavy_owner = jax.random.randint(subkeys[0], (), 0, devices)
    slot_ids = jnp.arange(slot_count, dtype=jnp.int32)
    scores = jax.random.randint(subkeys[1], (slot_count,), 0, 1 << 16) * slot_count + slot_ids
    scores = jnp.where(slot_ids // OWN_MAX == heavy_owner, slot_ids - slot_count, scores)
    slot_order = jnp.argsort(scores)
    chosen = (slot_order[:CLUSTERS] // OWN_MAX).astype(jnp.int32)
    shuffled = jax.random.permutation(subkeys[2], CLUSTERS)
    owner_map = jnp.zeros((CLUSTERS,), jnp.int32).at[shuffled].set(chosen)
    cluster_ids = jnp.arange(CLUSTERS, dtype=jnp.int32)
    same_owner = owner_map[:, None] == owner_map[None, :]
    earlier = cluster_ids[None, :] < cluster_ids[:, None]
    cluster_rank = jnp.sum(same_owner & earlier, axis=1).astype(jnp.int32)
    coins = jax.random.randint(subkeys[3], (devices, CLUSTERS), 0, 2)
    before = jnp.sum(coins[:, None, :] * (same_owner & earlier).astype(jnp.int32)[None], axis=2)
    served = (coins == 1) & (before < PEER_MAX)
    device_ids = jnp.arange(devices, dtype=jnp.int32)
    turn_index = (cluster_rank[None, :] - device_ids[:, None]) % OWN_MAX
    forced = turn_index < PEER_MAX
    served = jnp.where((owner_map == heavy_owner)[None, :], forced, served)
    first_ap = jax.random.randint(subkeys[4], (devices, CLUSTERS), 0, AP_DEV)
    extra_bits = jax.random.randint(subkeys[5], (devices, CLUSTERS, AP_DEV), 0, 2)
    members = (extra_bits == 1) | (jnp.arange(AP_DEV, dtype=jnp.int32)[None, None, :] == first_ap[:, :, None])
    serving = (served[:, :, None] & members).astype(jnp.int32)
    serving = jnp.transpose(serving, (1, 0, 2)).reshape(CLUSTERS, ACCESS_POINTS)
    return (owner_map, serving)


def draw_cluster_owner(key, part):
    owner_map, serving = owner_and_serving(key)
    return owner_map[:, None].astype(jnp.int32)


def draw_serving(key, part):
    owner_map, serving = owner_and_serving(key)
    return serving.astype(jnp.int32)


def draw_user_cluster(key, part):
    shuffled = jax.random.permutation(jax.random.fold_in(key, 3), USER_TOTAL)
    return (shuffled // CU).astype(jnp.int32)


def level_of(stream_key, extent, cuts, smallest, top_value):
    gain, own = 1.0, jax.random.fold_in(stream_key, 6)
    for dim, shards_of in cuts:
        steps = jnp.exp(jax.random.uniform(jax.random.fold_in(own, dim), (shards_of,), jnp.float32, smallest / len(cuts), top_value / len(cuts)))
        gain = gain * jnp.repeat(steps, extent[dim] // shards_of).reshape([-1 if axis == dim else 1 for axis in range(len(extent))])
    return gain


def gaussian(stream_key, dims, deviation, most, shards=(), held_as=jnp.bfloat16):
    values = deviation * jax.random.normal(stream_key, dims, jnp.float32)
    if shards:
        values = values * level_of(stream_key, dims, shards, -0.22, 0.18)
    return jnp.clip(values, -most, most).astype(held_as)


def setup_inputs(seed: int = 0, part: int = 0) -> dict:
    seeds = jax.random.split(jax.random.key(seed), 9)
    part_keys = jax.random.split(jax.random.fold_in(seeds[8], part), 9)
    return {
        "unsmoothed_link_guesses": gaussian(part_keys[0], (ACCESS_POINTS, ANTENNA_COUNT, 2, USER_TOTAL, TONE_NUMBER), 4.0, 24.0, ((0, 8), (4, 2))),
        "received": gaussian(part_keys[1], (ACCESS_POINTS, ANTENNA_COUNT, 2, DATA_SYMBOLS, TONE_NUMBER), 1.0, 6.0, ((0, 8), (4, 2))),
        "user_power": jnp.clip(jnp.exp(jax.random.uniform(part_keys[2], (USER_TOTAL,), jnp.float32, math.log(0.25), math.log(4.0))), 0.25, 4.0),
        "noise_power": jnp.clip(jnp.exp(math.log(1.0) - 2.3025851 * jax.random.uniform(part_keys[3], (ACCESS_POINTS,), jnp.float32) ** level_of(part_keys[3], (ACCESS_POINTS,), ((0, 8),), -0.2, 0.2)), 0.1, 1.0),
        "ap_gain": jnp.clip(jnp.exp(math.log(4.0) - 2.0794415 * jax.random.uniform(part_keys[4], (ACCESS_POINTS, USER_TOTAL), jnp.float32) ** level_of(part_keys[4], (ACCESS_POINTS, USER_TOTAL), ((0, 8),), -0.2, 0.2)), 0.5, 4.0),
        "user_cluster": draw_user_cluster(jax.random.fold_in(jax.random.fold_in(seeds[8], part), 71), part),
        "serving": draw_serving(jax.random.fold_in(jax.random.fold_in(seeds[8], part), 71), part),
        "cluster_owner": draw_cluster_owner(jax.random.fold_in(jax.random.fold_in(seeds[8], part), 71), part),
    }


def complex_times(left_factor, right_factor):
    return (left_factor[0] * right_factor[0] - left_factor[1] * right_factor[1], left_factor[0] * right_factor[1] + left_factor[1] * right_factor[0])

def times_conj(left_factor, right_factor):
    return (left_factor[0] * right_factor[0] + left_factor[1] * right_factor[1], left_factor[1] * right_factor[0] - left_factor[0] * right_factor[1])

def hermitian_solve(cov_re, cov_im, right_re, right_im):
    dimension = cov_re.shape[0]
    factor = {}
    pivots = []
    for j in range(dimension):
        pivot_root = cov_re[j, j]
        for k in range(j):
            element = factor[j, k]
            pivot_root = pivot_root - (element[0] * element[0] + element[1] * element[1])
        pivot_root = jnp.sqrt(pivot_root)
        pivots.append(pivot_root)
        for i in range(j + 1, dimension):
            running = (cov_re[i, j], cov_im[i, j])
            for k in range(j):
                product = times_conj(factor[i, k], factor[j, k])
                running = (running[0] - product[0], running[1] - product[1])
            factor[i, j] = (running[0] / pivot_root, running[1] / pivot_root)
    forward = []
    for i in range(dimension):
        running = (right_re[i], right_im[i])
        for k in range(i):
            product = complex_times(factor[i, k], forward[k])
            running = (running[0] - product[0], running[1] - product[1])
        forward.append((running[0] / pivots[i], running[1] / pivots[i]))
    result = [None] * dimension
    for i in range(dimension - 1, -1, -1):
        running = forward[i]
        for k in range(i + 1, dimension):
            product = times_conj(result[k], factor[k, i])
            running = (running[0] - product[0], running[1] - product[1])
        result[i] = (running[0] / pivots[i], running[1] / pivots[i])
    return result

def lag_fourier_matrices(lowest_tone_hertz, tone_quantity):
    tone_hertz_values = lowest_tone_hertz + jnp.arange(tone_quantity, dtype=jnp.int32)
    lag_seconds = jnp.arange(TAPS, dtype=jnp.int32)
    rotation_angles = tone_hertz_values[:, None] * lag_seconds[None, :] % TONE_NUMBER
    angles = rotation_angles.astype(jnp.float32) * (2.0 * math.pi / TONE_NUMBER)
    return jnp.concatenate([jnp.cos(angles), jnp.sin(angles)], axis=1).astype(jnp.bfloat16)

def smoothing(h_group, lag_fourier_matrix):
    dims_shape = h_group.shape
    products = jnp.dot(h_group.reshape(-1, dims_shape[-1]), lag_fourier_matrix, preferred_element_type=jnp.float32)
    products = products.reshape(dims_shape[:-1] + (2 * TAPS,))
    coef_re = (products[:, :, 0, :, :TAPS] - products[:, :, 1, :, TAPS:]) / TONE_NUMBER
    coef_im = (products[:, :, 0, :, TAPS:] + products[:, :, 1, :, :TAPS]) / TONE_NUMBER
    return jnp.stack([coef_re, coef_im], axis=2)

def rebuild(coefficients, lag_fourier_matrix):
    coef_b = coefficients.astype(jnp.bfloat16)
    real_rows = jnp.concatenate([coef_b[:, :, 0], coef_b[:, :, 1]], axis=-1)
    imag_rows = jnp.concatenate([coef_b[:, :, 1], -coef_b[:, :, 0]], axis=-1)
    stacked = jnp.stack([real_rows, imag_rows], axis=2)
    dims_shape = stacked.shape
    smooth = jnp.dot(stacked.reshape(-1, 2 * TAPS), lag_fourier_matrix.T, preferred_element_type=jnp.float32)
    return smooth.reshape(dims_shape[:-1] + (lag_fourier_matrix.shape[0],))

def local_estimates(smooth, power_row, noise_level, right_side, weight_row):
    antennas = smooth.shape[0]
    scaled = smooth * (power_row / smooth.shape[2])[None, None, :, None]
    gram_sums = jnp.einsum('icuf,jduf->icjdf', scaled, smooth, precision=lax.Precision.HIGHEST)
    cov_re = gram_sums[:, 0, :, 0] + gram_sums[:, 1, :, 1] + noise_level * jnp.eye(antennas, dtype=smooth.dtype)[:, :, None]
    cov_im = gram_sums[:, 1, :, 0] - gram_sums[:, 0, :, 1]
    signal = right_side.astype(jnp.float32)
    solved = hermitian_solve(cov_re, cov_im, signal[:, 0], signal[:, 1])
    est_re = smooth[0, 0][:, None, :] * solved[0][0][None] + smooth[0, 1][:, None, :] * solved[0][1][None]
    est_im = smooth[0, 0][:, None, :] * solved[0][1][None] - smooth[0, 1][:, None, :] * solved[0][0][None]
    for i in range(1, antennas):
        est_re = est_re + smooth[i, 0][:, None, :] * solved[i][0][None] + smooth[i, 1][:, None, :] * solved[i][1][None]
        est_im = est_im + smooth[i, 0][:, None, :] * solved[i][1][None] - smooth[i, 1][:, None, :] * solved[i][0][None]
    return weight_row[:, None, None, None] * jnp.stack([est_re, est_im], axis=2)

def reference(unsmoothed_link_guesses, received, user_power, noise_power, ap_gain, user_cluster, serving, cluster_owner):
    lag_fourier_matrix = lag_fourier_matrices(0, TONE_NUMBER)
    cluster_ids = jnp.arange(CLUSTERS, dtype=jnp.int32)
    onehot = (user_cluster[:, None] == cluster_ids[None, :]).astype(jnp.float32)
    serve_user = jnp.dot(onehot, serving.astype(jnp.float32), precision=lax.Precision.HIGHEST)
    weights = serve_user.T * ap_gain
    totals = lax.optimization_barrier(jnp.sum(weights, axis=0))

    def group_step(carry, inputs):
        h_group, right_group, noise_group, weight_group = inputs
        smooth = rebuild(smoothing(h_group, lag_fourier_matrix), lag_fourier_matrix)
        partial_value = local_estimates(smooth[0], user_power, noise_group[0], right_group[0], weight_group[0])
        for station in range(1, AP_DEV):
            partial_value = partial_value + local_estimates(smooth[station], user_power, noise_group[station], right_group[station], weight_group[station])
        rounded = lax.optimization_barrier(partial_value.astype(jnp.bfloat16))
        return (carry + rounded.astype(jnp.float32), None)
    inputs = (unsmoothed_link_guesses.reshape((N_AP, AP_DEV) + unsmoothed_link_guesses.shape[1:]), received.reshape((N_AP, AP_DEV) + received.shape[1:]), noise_power.reshape(N_AP, AP_DEV), weights.reshape(N_AP, AP_DEV, USER_TOTAL))
    initial = jnp.zeros((USER_TOTAL, DATA_SYMBOLS, 2, TONE_NUMBER), jnp.float32)
    numerator, _ = lax.scan(group_step, initial, inputs)
    decoded = numerator / (1.0 + totals)[:, None, None, None]
    owner_map = cluster_owner[:, 0]
    cluster_rank = lax.optimization_barrier(jnp.sum((owner_map[:, None] == owner_map[None, :]) & (cluster_ids[None, :] < cluster_ids[:, None]), axis=1)).astype(jnp.int32)
    user_ids = jnp.arange(USER_TOTAL, dtype=jnp.int32)
    position = lax.optimization_barrier(jnp.sum((user_cluster[:, None] == user_cluster[None, :]) & (user_ids[None, :] < user_ids[:, None]), axis=1)).astype(jnp.int32)
    slot_index = (owner_map[user_cluster] * OWN_MAX + cluster_rank[user_cluster]).astype(jnp.int32)
    estimates = jnp.zeros((SLOTS, CU, DATA_SYMBOLS, 2, TONE_NUMBER), jnp.float32).at[slot_index, position].set(decoded)
    return estimates
```

```python
import functools
import math

import jax
import jax.numpy as jnp
import numpy as np
from jax import lax
from jax.experimental import pallas as pl
from jax.experimental.pallas import tpu as pltpu
from jax.sharding import PartitionSpec as P

TONE_NUMBER = 2048
TAPS = 64
CU = 8
OWN_MAX = 4
PEER_MAX = 2
COARSE = 2 * TAPS
MESH = pl.DeviceIdType.MESH
LANES = 128
VMEM_BYTES = 67043328


def complex_times(left_factor, right_factor):
    return (
        left_factor[0] * right_factor[0] - left_factor[1] * right_factor[1],
        left_factor[0] * right_factor[1] + left_factor[1] * right_factor[0],
    )


def times_conj(left_factor, right_factor):
    return (
        left_factor[0] * right_factor[0] + left_factor[1] * right_factor[1],
        left_factor[1] * right_factor[0] - left_factor[0] * right_factor[1],
    )


def hermitian_solve(cov_re, cov_im, right):
    dimension = len(cov_re)
    factor = {}
    inverses = []
    for j in range(dimension):
        pivot = cov_re[j][j]
        for k in range(j):
            element = factor[j, k]
            pivot = pivot - (element[0] * element[0] + element[1] * element[1])
        inverse = 1.0 / jnp.sqrt(pivot)
        inverses.append(inverse)
        for i in range(j + 1, dimension):
            running = (cov_re[i][j], cov_im[i][j])
            for k in range(j):
                product = times_conj(factor[i, k], factor[j, k])
                running = (running[0] - product[0], running[1] - product[1])
            factor[i, j] = (running[0] * inverse, running[1] * inverse)
    forward = []
    for i in range(dimension):
        running = right[i]
        for k in range(i):
            product = complex_times(factor[i, k], forward[k])
            running = (running[0] - product[0], running[1] - product[1])
        forward.append((running[0] * inverses[i], running[1] * inverses[i]))
    result = [None] * dimension
    for i in range(dimension - 1, -1, -1):
        running = forward[i]
        for k in range(i + 1, dimension):
            product = times_conj(result[k], factor[k, i])
            running = (running[0] - product[0], running[1] - product[1])
        result[i] = (running[0] * inverses[i], running[1] * inverses[i])
    return result


def angles_of(values):
    rotation = np.arange(TAPS, dtype=np.int32)[:, None] * values[None, :] % TONE_NUMBER
    return rotation.astype(np.float32) * np.float32(2.0 * math.pi / TONE_NUMBER)


def wave_table(values):
    cosine, sine = np.cos(angles_of(values)), np.sin(angles_of(values))
    return np.concatenate([cosine, sine], axis=0), np.concatenate([-sine, cosine], axis=0)


def tap_tables(parts, tones):
    made = []
    for part in range(parts):
        real, imag = wave_table(part * tones + np.arange(tones, dtype=np.int32))
        made.append(np.concatenate([real.T, imag.T], axis=0))
    return np.stack(made).astype(jnp.bfloat16)


def tone_tables(parts, tones):
    made = []
    for part in range(parts):
        real, imag = wave_table(part * tones + np.arange(tones, dtype=np.int32))
        pair = np.stack(
            [real.reshape(2 * TAPS, -1, LANES), imag.reshape(2 * TAPS, -1, LANES)], axis=2
        )
        made.append(pair.reshape(2 * TAPS, 2 * tones))
    return np.stack(made).astype(jnp.bfloat16)


def coarse_table():
    step = TONE_NUMBER // COARSE
    real, imag = wave_table(step * np.arange(COARSE, dtype=np.int32))
    return np.concatenate([real, imag], axis=1).astype(jnp.bfloat16)


def spread_tables(parts, tones):
    step = TONE_NUMBER // COARSE
    made = []
    for part in range(parts):
        values = part * tones + np.arange(tones, dtype=np.int64)
        gap = values[None, :] - step * np.arange(COARSE, dtype=np.int64)[:, None]
        kernel = np.ones(gap.shape, np.float64)
        for d in range(1, COARSE // 2 + 1):
            share = 2.0 if d < COARSE // 2 else 1.0
            kernel += share * np.cos(2.0 * math.pi / TONE_NUMBER * (d * gap % TONE_NUMBER))
        kernel /= COARSE
        high = kernel.astype(np.float32).astype(jnp.bfloat16)
        low = (kernel - high.astype(np.float64)).astype(np.float32).astype(jnp.bfloat16)
        made.append(np.concatenate([high, low], axis=0))
    return np.stack(made)


def exact_dot(left, right, dims):
    return lax.dot_general(
        left.astype(jnp.bfloat16),
        right.astype(jnp.bfloat16),
        (dims, ((), ())),
        preferred_element_type=jnp.float32,
    )


def iota(shape, dim):
    return lax.broadcasted_iota(jnp.int32, shape, dim).astype(jnp.float32)


def user_tables(user_cluster, serving, owner, clusters, users, group, n):
    onehot = (iota((clusters, users), 0) == user_cluster.astype(jnp.float32)).astype(jnp.float32)
    owner_row = owner.astype(jnp.float32)
    square = (clusters, clusters)
    rows, cols = iota(square, 0), iota(square, 1)
    owner_col = jnp.sum(jnp.where(rows == cols, owner_row, 0.0), axis=1, keepdims=True)
    same = owner_col == owner_row
    earlier = jnp.where(same & (cols < rows), 1.0, 0.0)
    serve = serving.astype(jnp.float32)
    pair = jnp.where(
        jnp.floor((iota((group * n, n), 0) + 0.5) * (1.0 / group)) == iota((group * n, n), 1),
        1.0,
        0.0,
    )
    served = jnp.where(exact_dot(serve, pair, ((1,), (0,))) > 0.5, 1.0, 0.0)
    before = exact_dot(earlier, served, ((1,), (0,)))
    rank = jnp.sum(earlier, axis=1, keepdims=True)
    owner_u = jnp.sum(onehot * owner_col, axis=0, keepdims=True)
    rank_u = jnp.sum(onehot * rank, axis=0, keepdims=True)
    served_u = exact_dot(served, onehot, ((0,), (0,)))
    before_u = exact_dot(before, onehot, ((0,), (0,)))
    serve_u = exact_dot(serve, onehot, ((0,), (0,)))
    equal = exact_dot(onehot, onehot, ((0,), (0,)))
    both = (users, users)
    position = jnp.sum(
        jnp.where(iota(both, 0) < iota(both, 1), equal, 0.0), axis=0, keepdims=True
    )
    return owner_u, rank_u, served_u, before_u, serve_u, position


def uplink_kernel(
    n,
    chunks,
    ring_of,
    guess_hbm,
    received_hbm,
    power_hbm,
    noise_hbm,
    gain_hbm,
    cluster_hbm,
    serving_hbm,
    owner_hbm,
    taps_hbm,
    table_hbm,
    coarse_hbm,
    spread_hbm,
    out_ref,
    coef_all,
    solved_all,
    received_ref,
    power_ref,
    noise_ref,
    gain_ref,
    cluster_ref,
    serving_ref,
    owner_ref,
    solved_wide,
    guess,
    taps,
    table,
    coarse,
    spread,
    half,
    other,
    coef_send,
    coef_b,
    gains,
    pick,
    pick_weight,
    power_wide,
    sampled,
    samples,
    cov,
    smooth,
    own,
    share,
    guess_sem,
    table_sem,
    half_send_sem,
    half_recv_sem,
    gain_send_sem,
    gain_recv_sem,
    coef_send_sem,
    coef_recv_sem,
    ring_send_sem,
    ring_recv_sem,
    local_sem,
    small_sem,
    relay_send_sem,
    relay_recv_sem,
):
    stations, antennas, _, users, tones = guess.shape
    pieces = stations * antennas
    block = PEER_MAX * CU
    clusters = serving_ref.shape[0]
    me = lax.axis_index("ap")
    part = lax.axis_index("sc")
    node, place = ring_of
    spot = place(me)
    right = node(lax.rem(spot + 1, n))
    left = node(lax.rem(spot + n - 1, n))

    table_copies = []
    for source, into in (
        (taps_hbm.at[part], taps),
        (coarse_hbm, coarse),
        (spread_hbm.at[part], spread),
        (table_hbm.at[part], table),
    ):
        table_copies.append(
            pltpu.make_async_copy(source, into, table_sem.at[len(table_copies)])
        )
    table_copies[0].start()
    guess_copies = []
    for q in range(pieces):
        a, i = q // antennas, q % antennas
        copy = pltpu.make_async_copy(guess_hbm.at[a, i], guess.at[a, i], guess_sem.at[q])
        copy.start()
        guess_copies.append(copy)
    small_copies = []
    for source, into in (
        (cluster_hbm, cluster_ref),
        (serving_hbm, serving_ref),
        (owner_hbm, owner_ref),
        (power_hbm, power_ref),
        (gain_hbm, gain_ref),
        (noise_hbm, noise_ref),
        (received_hbm, received_ref),
    ):
        copy = pltpu.make_async_copy(source, into, small_sem.at[len(small_copies)])
        copy.start()
        small_copies.append(copy)
    for copy in table_copies[1:]:
        copy.start()

    barrier = pltpu.get_barrier_semaphore()
    pl.semaphore_signal(barrier, inc=1, device_id={"sc": 1 - part}, device_id_type=MESH)
    for k in range(1, n):
        pl.semaphore_signal(
            barrier, inc=1, device_id={"ap": lax.rem(me + k, n)}, device_id_type=MESH
        )

    table_copies[0].wait()
    half_copies = []
    for q in range(pieces):
        a, i = q // antennas, q % antennas
        guess_copies[q].wait()
        sums = jnp.dot(
            guess[a, i, 0], taps[:tones, :], preferred_element_type=jnp.float32
        ) + jnp.dot(guess[a, i, 1], taps[tones:, :], preferred_element_type=jnp.float32)
        half[q] = (sums * (1.0 / TONE_NUMBER)).astype(jnp.bfloat16)
        if q == 0:
            pl.semaphore_wait(barrier, n)
        copy = pltpu.make_async_remote_copy(
            src_ref=half.at[q],
            dst_ref=other.at[q],
            send_sem=half_send_sem.at[q],
            recv_sem=half_recv_sem.at[q],
            device_id={"sc": 1 - part},
            device_id_type=MESH,
        )
        copy.start()
        half_copies.append(copy)

    for copy in small_copies:
        copy.wait()
    gain_copies = []
    for k in range(1, n):
        peer = lax.rem(me + k, n)
        copy = pltpu.make_async_remote_copy(
            src_ref=gain_ref,
            dst_ref=gains.at[me],
            send_sem=gain_send_sem.at[k],
            recv_sem=gain_recv_sem.at[n - k],
            device_id={"ap": peer},
            device_id_type=MESH,
        )
        copy.start()
        gain_copies.append(copy)
    gains[me] = gain_ref[...]
    owner_u, rank_u, served_u, before_u, serve_u, position = user_tables(
        cluster_ref[...], serving_ref[...], owner_ref[...], clusters, users, stations, n
    )
    mef = me.astype(jnp.float32)
    mine = iota((n, users), 0) == mef
    served_me = jnp.sum(jnp.where(mine, served_u, 0.0), axis=0, keepdims=True)
    before_me = jnp.sum(jnp.where(mine, before_u, 0.0), axis=0, keepdims=True)
    target = jnp.where(
        served_me > 0.5, owner_u * block + before_me * CU + position, -1.0
    )
    chosen_user = iota((n * block, users), 0) == target
    pick[...] = jnp.where(chosen_user, 1.0, 0.0).astype(jnp.bfloat16)
    for a in range(stations):
        row_here = iota((n * stations, users), 0) == mef * stations + a
        weight = jnp.sum(jnp.where(row_here, serve_u, 0.0), axis=0, keepdims=True)
        weight = weight * gain_ref[a : a + 1, :]
        column = jnp.sum(jnp.where(chosen_user, weight, 0.0), axis=1, keepdims=True)
        pick_weight[a] = jnp.broadcast_to(column, (n * block, LANES))
    wide = jnp.broadcast_to(power_ref[...] * (1.0 / users), (LANES, users))
    power_wide[...] = jnp.transpose(wide)

    for q in range(pieces):
        half_copies[q].wait_recv()
        total = (half[q].astype(jnp.float32) + other[q].astype(jnp.float32)).astype(jnp.bfloat16)
        coef_b[pl.ds(q * users, users), :] = total
        chosen = jnp.dot(pick[...], total, preferred_element_type=jnp.float32)
        chosen = chosen * pick_weight[q // antennas]
        coef_send[:, q] = chosen.astype(jnp.bfloat16).reshape(n, block, 2 * TAPS)
    coef_copies = []
    mine_half = pl.ds(part * (pieces // 2), pieces // 2)
    for k in range(1, n):
        peer = lax.rem(me + k, n)
        copy = pltpu.make_async_remote_copy(
            src_ref=coef_send.at[peer, mine_half],
            dst_ref=coef_all.at[me, mine_half],
            send_sem=coef_send_sem.at[k],
            recv_sem=coef_recv_sem.at[n - k],
            device_id={"ap": peer},
            device_id_type=MESH,
        )
        copy.start()
        coef_copies.append(copy)
    own_coef = pltpu.make_async_copy(coef_send.at[me], coef_all.at[me], local_sem)
    own_coef.start()

    width = tones // chunks
    lane_tiles = width // LANES
    symbols = received_ref.shape[3]
    rows = stations * symbols
    ring_copies = {}
    reach = {}
    for c in range(chunks):
        far, near = n // 2, n - 1 - n // 2
        reach[c] = (far, near) if c % 2 == 0 else (near, far)

    ready = []

    def origin_of(direction, step):
        back = lax.rem(spot + n - step, n) if direction == 0 else lax.rem(spot + step, n)
        return node(back)

    def ring_start(c, direction, step):
        if step > reach[c][direction]:
            return False
        origin = origin_of(direction, step)
        source = own.at[c]
        if step > 0:
            ring_copies[c, direction, step - 1].wait_recv()
            source = solved_all.at[origin, c]
            ready.append((origin, c, source))
        if step == reach[c][direction]:
            return True
        copy = pltpu.make_async_remote_copy(
            src_ref=source,
            dst_ref=solved_all.at[origin, c],
            send_sem=ring_send_sem.at[direction, c, step],
            recv_sem=ring_recv_sem.at[direction, c, step],
            device_id={"ap": right if direction == 0 else left},
            device_id_type=MESH,
        )
        copy.start()
        ring_copies[c, direction, step] = copy
        return True

    steps = max(max(r) for r in reach.values())
    entries = [(i, j) for i in range(antennas) for j in range(i + 1)]
    noise = jnp.concatenate(
        [
            jnp.broadcast_to(noise_ref[0:1, a : a + 1], (symbols, 1))
            for a in range(stations)
        ],
        axis=0,
    )

    for copy in table_copies[1:]:
        copy.wait()
    both = jnp.dot(coef_b[...], coarse[...], preferred_element_type=jnp.float32)
    for reim in range(2):
        sampled[reim] = both[:, reim * COARSE : (reim + 1) * COARSE]
    for a in range(stations):

        def body(step, sums, a=a):
            sums = list(sums)
            for w in range(2):
                row = (step * 2 + w) * 8
                scale = power_wide[pl.ds(pl.multiple_of(row, 8), 8), :]
                re, im = [], []
                for i in range(antennas):
                    at = pl.multiple_of((a * antennas + i) * users + row, 8)
                    re.append(sampled[0, pl.ds(at, 8), :])
                    im.append(sampled[1, pl.ds(at, 8), :])
                at = 0
                for i in range(antennas):
                    sre, sim = re[i] * scale, im[i] * scale
                    for j in range(i + 1):
                        sums[at] = sums[at] + (sre * re[j] + sim * im[j])
                        at += 1
                        if j < i:
                            sums[at] = sums[at] + (sim * re[j] - sre * im[j])
                            at += 1
            return tuple(sums)

        zero = jnp.zeros((8, COARSE), jnp.float32)
        sums = lax.fori_loop(0, users // 16, body, (zero,) * (antennas * antennas))
        for e in range(antennas * antennas):
            value = jnp.sum(sums[e], axis=0, keepdims=True)
            samples[pl.ds(e * rows + a * symbols, symbols), :] = jnp.broadcast_to(
                value, (symbols, COARSE)
            )
    high = samples[...].astype(jnp.bfloat16)
    low = (samples[...] - high.astype(jnp.float32)).astype(jnp.bfloat16)
    cov[...] = (
        jnp.dot(
            jnp.concatenate([high, high], axis=1),
            spread[...],
            preferred_element_type=jnp.float32,
        )
        + jnp.dot(low, spread[:COARSE, :], preferred_element_type=jnp.float32)
    )
    for c in range(chunks):
        base = c * width
        lanes = slice(base, base + width)
        cov_re = [[None] * antennas for _ in range(antennas)]
        cov_im = [[None] * antennas for _ in range(antennas)]
        at = 0
        for i, j in entries:
            cov_re[i][j] = cov[at * rows : (at + 1) * rows, lanes]
            at += 1
            if i == j:
                cov_re[i][j] = cov_re[i][j] + noise
            else:
                cov_im[i][j] = cov[at * rows : (at + 1) * rows, lanes]
                at += 1
        signal = []
        for i in range(antennas):
            signal.append(
                tuple(
                    jnp.concatenate(
                        [
                            received_ref[a, i, reim, :, lanes].astype(jnp.float32)
                            for a in range(stations)
                        ],
                        axis=0,
                    )
                    for reim in range(2)
                )
            )
        solved = hermitian_solve(cov_re, cov_im, signal)
        for i in range(antennas):
            joined = jnp.concatenate([solved[i][0], solved[i][1]], axis=0)
            own[c, pl.ds(i * 2 * rows, 2 * rows), :] = joined.astype(jnp.bfloat16)
        ready.append((me, c, own.at[c]))
        for d in range(c + 1):
            for direction in range(2):
                ring_start(d, direction, c - d)

    for copy in gain_copies:
        copy.wait_recv()
    totals = jnp.zeros((1, users), jnp.float32)
    for p in range(n):
        for a in range(stations):
            row = serve_u[p * stations + a : p * stations + a + 1] * gains[p, a : a + 1, :]
            totals = totals + row
    scale = 1.0 / (1.0 + totals)
    held = owner_u == mef
    slot_user = iota((OWN_MAX * CU, users), 0) == jnp.where(held, rank_u * CU + position, -1.0)
    slot_rows = jnp.where(slot_user, 1.0, 0.0)
    slot_scale = jnp.sum(jnp.where(slot_user, scale, 0.0), axis=1, keepdims=True)
    slot_scale = jnp.broadcast_to(slot_scale, (OWN_MAX * CU, LANES))
    hits = []
    for p in range(n):
        goal = jnp.where(
            held & (served_u[p : p + 1] > 0.5), before_u[p : p + 1] * CU + position, -1.0
        )
        hits.append(jnp.where(iota((block, users), 0) == goal, 1.0, 0.0))
    placement = exact_dot(slot_rows, jnp.concatenate(hits, axis=0), ((1,), (1,)))
    placement = placement.astype(jnp.bfloat16)

    relay_copies = []
    for k in range(1, n):
        coef_copies[n - k - 1].wait_recv()
        origin = lax.rem(me + n - (n - k), n)
        copy = pltpu.make_async_remote_copy(
            src_ref=coef_all.at[origin, mine_half],
            dst_ref=coef_all.at[origin, mine_half],
            send_sem=relay_send_sem.at[k],
            recv_sem=relay_recv_sem.at[k],
            device_id={"sc": 1 - part},
            device_id_type=MESH,
        )
        copy.start()
        relay_copies.append(copy)
    own_coef.wait()

    def combine(origin, c, source):
        wide = source[...].astype(jnp.float32)
        for i in range(antennas):
            re = wide[i * 2 * rows : i * 2 * rows + rows]
            im = wide[i * 2 * rows + rows : (i + 1) * 2 * rows]
            solved_wide[i, 0] = re
            solved_wide[i, 1] = im
            solved_wide[i, 2] = re + im
        coefs = coef_all[origin].reshape(pieces * block, 2 * TAPS)
        for l in range(lane_tiles):
            columns = pl.ds((c * lane_tiles + l) * 2 * LANES, 2 * LANES)
            smooth[l] = jnp.dot(coefs, table[:, columns], preferred_element_type=jnp.float32)
        for l in range(lane_tiles):
            lanes = pl.ds(l * LANES, LANES)
            sums = [[None] * symbols for _ in range(PEER_MAX)]
            for a in range(stations):
                for i in range(antennas):
                    re, im, gap = [], [], []
                    for k in range(PEER_MAX):
                        at = (a * antennas + i) * block + k * CU
                        re.append(smooth[l, pl.ds(at, CU), :LANES])
                        im.append(smooth[l, pl.ds(at, CU), LANES:])
                        gap.append(re[k] - im[k])
                    for s in range(symbols):
                        row = pl.ds(a * symbols + s, 1)
                        sre = solved_wide[i, 0, row, lanes]
                        sim = solved_wide[i, 1, row, lanes]
                        ssum = solved_wide[i, 2, row, lanes]
                        for k in range(PEER_MAX):
                            new = (re[k] * sre, im[k] * sim, gap[k] * ssum)
                            old = sums[k][s]
                            if old is not None:
                                new = tuple(x + y for x, y in zip(old, new))
                            sums[k][s] = new
            at = pl.ds(pl.multiple_of(origin * block, block), block)
            for s in range(symbols):
                first = [sums[k][s][0] + sums[k][s][1] for k in range(PEER_MAX)]
                second = [
                    sums[k][s][2] - (sums[k][s][0] - sums[k][s][1]) for k in range(PEER_MAX)
                ]
                for reim, values in ((0, first), (1, second)):
                    share[s * 2 + reim, at, pl.ds(c * width + l * LANES, LANES)] = (
                        jnp.concatenate(values, axis=0).astype(jnp.bfloat16)
                    )

    def drain(most):
        for _ in range(most):
            if ready:
                combine(*ready.pop(0))

    drain(1)
    waited = False
    for late in range(chunks, chunks + steps):
        for d in range(chunks):
            for direction in range(2):
                if late - d > 0 and ring_start(d, direction, late - d):
                    if not waited and len(ready) and ready[0][0] is not me:
                        for copy in relay_copies:
                            copy.wait_recv()
                        waited = True
                    drain(1)
    if not waited:
        for copy in relay_copies:
            copy.wait_recv()
    drain(len(ready))

    tiles = tones // LANES
    for s in range(symbols):
        for reim in range(2):
            placed = jnp.dot(placement, share[s * 2 + reim], preferred_element_type=jnp.float32)
            for l in range(tiles):
                for r in range(OWN_MAX):
                    value = placed[r * CU : (r + 1) * CU, l * LANES : (l + 1) * LANES]
                    first = r * CU * symbols * tiles * 2 + (s * tiles + l) * 2 + reim
                    out_ref[pl.ds(first, CU, stride=symbols * tiles * 2), :] = (
                        value * slot_scale[r * CU : (r + 1) * CU]
                    )

    for copy in relay_copies:
        copy.wait_send()
    for copy in half_copies:
        copy.wait_send()
    for copy in gain_copies:
        copy.wait_send()
    for copy in coef_copies:
        copy.wait_send()
    for copy in ring_copies.values():
        copy.wait_send()


def ring_functions(mesh):
    n = mesh.shape["ap"]
    half = n // 2

    def plain(q):
        return q

    def node(q):
        upper = q // half
        return (1 - upper) * 2 * q + upper * (2 * (n - q) - 1)

    def place(d):
        odd = d % 2
        return (1 - odd) * (d // 2) + odd * (n - (d + 1) // 2)

    if n % 2:
        return plain, plain
    try:
        axes = list(mesh.axis_names)
        line = np.moveaxis(mesh.devices, axes.index("ap"), 0).reshape(n, -1)[:, 0]
        spots = [tuple(d.coords) for d in line]
        sizes = [max(s[x] for s in spots) + 1 for x in range(3)]

        def length(order):
            far = 0
            for q in range(n):
                one, two = spots[order(q)], spots[order((q + 1) % n)]
                far += sum(
                    min(abs(one[x] - two[x]), sizes[x] - abs(one[x] - two[x])) for x in range(3)
                )
            return far

        if length(plain) < length(node):
            return plain, plain
    except (AttributeError, TypeError):
        pass
    return node, place


def local(
    n,
    parts,
    ring_of,
    unsmoothed_link_guesses,
    received,
    user_power,
    noise_power,
    ap_gain,
    user_cluster,
    serving,
    cluster_owner,
):
    stations, antennas, _, users, tones = unsmoothed_link_guesses.shape
    symbols = received.shape[3]
    pieces = stations * antennas
    block = PEER_MAX * CU
    rows = stations * symbols
    chunks = 2
    width = tones // chunks
    steps = n // 2
    vmem = pl.BlockSpec(memory_space=pltpu.VMEM)
    dma = pltpu.SemaphoreType.DMA
    bf16, f32 = jnp.bfloat16, jnp.float32
    hbm = pl.BlockSpec(memory_space=pltpu.HBM)
    tiles = tones // LANES
    lines = OWN_MAX * CU * symbols * tiles * 2
    placed = pl.pallas_call(
        functools.partial(uplink_kernel, n, chunks, ring_of),
        out_shape=jax.ShapeDtypeStruct((lines, LANES), f32),
        in_specs=[hbm] * 12,
        out_specs=vmem,
        scratch_shapes=[
            pltpu.VMEM((n, pieces, block, 2 * TAPS), bf16),
            pltpu.VMEM((n, chunks, antennas * 2 * rows, width), bf16),
            pltpu.VMEM(received.shape, bf16),
            pltpu.VMEM((1, users), f32),
            pltpu.VMEM((1, stations), f32),
            pltpu.VMEM((stations, users), f32),
            pltpu.VMEM((1, users), jnp.int32),
            pltpu.VMEM(serving.shape, jnp.int32),
            pltpu.VMEM((1, serving.shape[0]), jnp.int32),
            pltpu.VMEM((antennas, 3, rows, width), f32),
            pltpu.VMEM((stations, antennas, 2, users, tones), bf16),
            pltpu.VMEM((2 * tones, 2 * TAPS), bf16),
            pltpu.VMEM((2 * TAPS, 2 * tones), bf16),
            pltpu.VMEM((2 * TAPS, 2 * COARSE), bf16),
            pltpu.VMEM((2 * COARSE, tones), bf16),
            pltpu.VMEM((pieces, users, 2 * TAPS), bf16),
            pltpu.VMEM((pieces, users, 2 * TAPS), bf16),
            pltpu.VMEM((n, pieces, block, 2 * TAPS), bf16),
            pltpu.VMEM((pieces * users, 2 * TAPS), bf16),
            pltpu.VMEM((n, stations, users), f32),
            pltpu.VMEM((n * block, users), bf16),
            pltpu.VMEM((stations, n * block, LANES), f32),
            pltpu.VMEM((users, LANES), f32),
            pltpu.VMEM((2, pieces * users, COARSE), f32),
            pltpu.VMEM((antennas * antennas * rows, COARSE), f32),
            pltpu.VMEM((antennas * antennas * rows, tones), f32),
            pltpu.VMEM((width // LANES, pieces * block, 2 * LANES), f32),
            pltpu.VMEM((chunks, antennas * 2 * rows, width), bf16),
            pltpu.VMEM((symbols * 2, n * block, tones), bf16),
            dma((pieces,)),
            dma((4,)),
            dma((pieces,)),
            dma((pieces,)),
            dma((n,)),
            dma((n,)),
            dma((n,)),
            dma((n,)),
            dma((2, chunks, steps)),
            dma((2, chunks, steps)),
            dma,
            dma((7,)),
            dma((n,)),
            dma((n,)),
        ],
        compiler_params=pltpu.CompilerParams(
            collective_id=0, has_side_effects=True, vmem_limit_bytes=VMEM_BYTES
        ),
        name="uplink",
    )(
        unsmoothed_link_guesses,
        received,
        user_power.reshape(1, users),
        noise_power.reshape(1, stations),
        ap_gain,
        user_cluster.reshape(1, users),
        serving,
        cluster_owner.reshape(1, -1),
        jnp.asarray(tap_tables(parts, tones)),
        jnp.asarray(tone_tables(parts, tones)),
        jnp.asarray(coarse_table()),
        jnp.asarray(spread_tables(parts, tones)),
    )
    placed = placed.reshape(OWN_MAX, CU, symbols, tiles, 2, LANES)
    placed = jnp.transpose(placed, (0, 1, 2, 4, 3, 5))
    return placed.reshape(OWN_MAX, CU, symbols, 2, tones)


def solution(mesh):
    placed = (
        P(("cell", "ap"), None, None, None, "sc"),
        P(("cell", "ap"), None, None, None, "sc"),
        P("cell"),
        P(("cell", "ap")),
        P(("cell", "ap"), None),
        P("cell"),
        P("cell", None),
        P("cell", None),
    )
    return jax.shard_map(
        functools.partial(local, mesh.shape["ap"], mesh.shape["sc"], ring_functions(mesh)),
        mesh=mesh,
        in_specs=placed,
        out_specs=P(("cell", "ap"), None, None, None, "sc"),
        check_vma=False,
    )
```

```python
import functools
import math

import jax
import jax.numpy as jnp
import numpy as np
from jax import lax
from jax.experimental import pallas as pl
from jax.experimental.pallas import tpu as pltpu
from jax.sharding import PartitionSpec as P

TONE_NUMBER = 2048
TAPS = 64
CU = 8
OWN_MAX = 4
PEER_MAX = 2
COARSE = 2 * TAPS
MESH = pl.DeviceIdType.MESH
LANES = 128
VMEM_BYTES = 67043328


def complex_times(left_factor, right_factor):
    return (
        left_factor[0] * right_factor[0] - left_factor[1] * right_factor[1],
        left_factor[0] * right_factor[1] + left_factor[1] * right_factor[0],
    )


def times_conj(left_factor, right_factor):
    return (
        left_factor[0] * right_factor[0] + left_factor[1] * right_factor[1],
        left_factor[1] * right_factor[0] - left_factor[0] * right_factor[1],
    )


def hermitian_solve(cov_re, cov_im, right):
    dimension = len(cov_re)
    factor = {}
    inverses = []
    for j in range(dimension):
        pivot = cov_re[j][j]
        for k in range(j):
            element = factor[j, k]
            pivot = pivot - (element[0] * element[0] + element[1] * element[1])
        inverse = 1.0 / jnp.sqrt(pivot)
        inverses.append(inverse)
        for i in range(j + 1, dimension):
            running = (cov_re[i][j], cov_im[i][j])
            for k in range(j):
                product = times_conj(factor[i, k], factor[j, k])
                running = (running[0] - product[0], running[1] - product[1])
            factor[i, j] = (running[0] * inverse, running[1] * inverse)
    forward = []
    for i in range(dimension):
        running = right[i]
        for k in range(i):
            product = complex_times(factor[i, k], forward[k])
            running = (running[0] - product[0], running[1] - product[1])
        forward.append((running[0] * inverses[i], running[1] * inverses[i]))
    result = [None] * dimension
    for i in range(dimension - 1, -1, -1):
        running = forward[i]
        for k in range(i + 1, dimension):
            product = times_conj(result[k], factor[k, i])
            running = (running[0] - product[0], running[1] - product[1])
        result[i] = (running[0] * inverses[i], running[1] * inverses[i])
    return result


def angles_of(values):
    rotation = np.arange(TAPS, dtype=np.int32)[:, None] * values[None, :] % TONE_NUMBER
    return rotation.astype(np.float32) * np.float32(2.0 * math.pi / TONE_NUMBER)


def wave_table(values):
    cosine, sine = np.cos(angles_of(values)), np.sin(angles_of(values))
    return np.concatenate([cosine, sine], axis=0), np.concatenate([-sine, cosine], axis=0)


def tap_tables(parts, tones):
    made = []
    for part in range(parts):
        real, _ = wave_table(part * tones + np.arange(tones, dtype=np.int32))
        made.append(real.T)
    return np.stack(made).astype(jnp.bfloat16)


def tone_tables(parts, tones):
    made = []
    for part in range(parts):
        real, imag = wave_table(part * tones + np.arange(tones, dtype=np.int32))
        pair = np.stack(
            [real.reshape(2 * TAPS, -1, LANES), imag.reshape(2 * TAPS, -1, LANES)], axis=2
        )
        made.append(pair.reshape(2 * TAPS, 2 * tones))
    return np.stack(made).astype(jnp.bfloat16)


def coarse_table():
    step = TONE_NUMBER // COARSE
    real, imag = wave_table(step * np.arange(COARSE, dtype=np.int32))
    return np.concatenate([real, imag], axis=1).astype(jnp.bfloat16)


def spread_tables(parts, tones):
    step = TONE_NUMBER // COARSE
    made = []
    for part in range(parts):
        values = part * tones + np.arange(tones, dtype=np.int64)
        gap = values[None, :] - step * np.arange(COARSE, dtype=np.int64)[:, None]
        kernel = np.ones(gap.shape, np.float64)
        for d in range(1, COARSE // 2 + 1):
            share = 2.0 if d < COARSE // 2 else 1.0
            kernel += share * np.cos(2.0 * math.pi / TONE_NUMBER * (d * gap % TONE_NUMBER))
        kernel /= COARSE
        high = kernel.astype(np.float32).astype(jnp.bfloat16)
        low = (kernel - high.astype(np.float64)).astype(np.float32).astype(jnp.bfloat16)
        made.append(np.concatenate([high, low], axis=0))
    return np.stack(made)


def exact_dot(left, right, dims):
    return lax.dot_general(
        left.astype(jnp.bfloat16),
        right.astype(jnp.bfloat16),
        (dims, ((), ())),
        preferred_element_type=jnp.float32,
    )


def iota(shape, dim):
    return lax.broadcasted_iota(jnp.int32, shape, dim).astype(jnp.float32)


def user_tables(user_cluster, serving, owner, clusters, users, group, n):
    onehot = (iota((clusters, users), 0) == user_cluster.astype(jnp.float32)).astype(jnp.float32)
    owner_row = owner.astype(jnp.float32)
    square = (clusters, clusters)
    rows, cols = iota(square, 0), iota(square, 1)
    owner_col = jnp.sum(jnp.where(rows == cols, owner_row, 0.0), axis=1, keepdims=True)
    same = owner_col == owner_row
    earlier = jnp.where(same & (cols < rows), 1.0, 0.0)
    serve = serving.astype(jnp.float32)
    pair = jnp.where(
        jnp.floor((iota((group * n, n), 0) + 0.5) * (1.0 / group)) == iota((group * n, n), 1),
        1.0,
        0.0,
    )
    served = jnp.where(exact_dot(serve, pair, ((1,), (0,))) > 0.5, 1.0, 0.0)
    before = exact_dot(earlier, served, ((1,), (0,)))
    rank = jnp.sum(earlier, axis=1, keepdims=True)
    owner_u = jnp.sum(onehot * owner_col, axis=0, keepdims=True)
    rank_u = jnp.sum(onehot * rank, axis=0, keepdims=True)
    served_u = exact_dot(served, onehot, ((0,), (0,)))
    before_u = exact_dot(before, onehot, ((0,), (0,)))
    serve_u = exact_dot(serve, onehot, ((0,), (0,)))
    equal = exact_dot(onehot, onehot, ((0,), (0,)))
    both = (users, users)
    position = jnp.sum(
        jnp.where(iota(both, 0) < iota(both, 1), equal, 0.0), axis=0, keepdims=True
    )
    return owner_u, rank_u, served_u, before_u, serve_u, position


def uplink_kernel(
    n,
    chunks,
    ring_of,
    guess_hbm,
    received_hbm,
    power_hbm,
    noise_hbm,
    gain_hbm,
    cluster_hbm,
    serving_hbm,
    owner_hbm,
    taps_hbm,
    table_hbm,
    coarse_hbm,
    spread_hbm,
    share_hbm,
    place_ref,
    scale_ref,
    coef_all,
    solved_all,
    received_ref,
    power_ref,
    noise_ref,
    gain_ref,
    cluster_ref,
    serving_ref,
    owner_ref,
    solved_wide,
    guess,
    taps,
    table,
    coarse,
    spread,
    half,
    other,
    coef_send,
    coef_b,
    gains,
    pick,
    pick_weight,
    power_wide,
    sampled,
    samples,
    cov,
    smooth,
    own,
    share,
    guess_sem,
    table_sem,
    half_send_sem,
    half_recv_sem,
    gain_send_sem,
    gain_recv_sem,
    coef_send_sem,
    coef_recv_sem,
    ring_send_sem,
    ring_recv_sem,
    local_sem,
    small_sem,
    relay_send_sem,
    relay_recv_sem,
    share_sem,
):
    stations, antennas, _, users, tones = guess.shape
    pieces = stations * antennas
    block = PEER_MAX * CU
    clusters = serving_ref.shape[0]
    me = lax.axis_index("ap")
    part = lax.axis_index("sc")
    node, place = ring_of
    spot = place(me)
    right = node(lax.rem(spot + 1, n))
    left = node(lax.rem(spot + n - 1, n))

    table_copies = []
    for source, into in (
        (taps_hbm.at[part], taps),
        (coarse_hbm, coarse),
        (spread_hbm.at[part], spread),
        (table_hbm.at[part], table),
    ):
        table_copies.append(
            pltpu.make_async_copy(source, into, table_sem.at[len(table_copies)])
        )
    table_copies[0].start()
    guess_copies = []
    for q in range(pieces):
        a, i = q // antennas, q % antennas
        copy = pltpu.make_async_copy(guess_hbm.at[a, i], guess.at[a, i], guess_sem.at[q])
        guess_copies.append(copy)
    for copy in guess_copies[: pieces // 2]:
        copy.start()
    barrier = pltpu.get_barrier_semaphore()
    pl.semaphore_signal(barrier, inc=1, device_id={"sc": 1 - part}, device_id_type=MESH)
    for k in range(1, n):
        pl.semaphore_signal(
            barrier, inc=1, device_id={"ap": lax.rem(me + k, n)}, device_id_type=MESH
        )

    table_copies[0].wait()
    for copy in guess_copies[pieces // 2 :]:
        copy.start()
    small_copies = []
    for source, into in (
        (cluster_hbm, cluster_ref),
        (serving_hbm, serving_ref),
        (owner_hbm, owner_ref),
        (power_hbm, power_ref),
        (gain_hbm, gain_ref),
        (noise_hbm, noise_ref),
        (received_hbm, received_ref),
    ):
        copy = pltpu.make_async_copy(source, into, small_sem.at[len(small_copies)])
        copy.start()
        small_copies.append(copy)
    for copy in table_copies[1:]:
        copy.start()

    half_copies = []
    together = 2
    lower = lax.broadcasted_iota(jnp.int32, (users, 2 * TAPS), 1) < TAPS
    for first in range(0, pieces, together):
        group = range(first, first + together)
        for q in group:
            guess_copies[q].wait()
        a, i = first // antennas, first % antennas
        products = jnp.dot(
            guess[a, i : i + together].reshape(together * 2 * users, tones),
            taps[...],
            preferred_element_type=jnp.float32,
        )
        for q in group:
            at = (q - first) * 2 * users
            turned = pltpu.roll(products[at + users : at + 2 * users], TAPS, axis=1)
            sums = products[at : at + users] + jnp.where(lower, -turned, turned)
            half[q] = (sums * (1.0 / TONE_NUMBER)).astype(jnp.bfloat16)
        if first == 0:
            pl.semaphore_wait(barrier, n)
        for q in group:
            copy = pltpu.make_async_remote_copy(
                src_ref=half.at[q],
                dst_ref=other.at[q],
                send_sem=half_send_sem.at[q],
                recv_sem=half_recv_sem.at[q],
                device_id={"sc": 1 - part},
                device_id_type=MESH,
            )
            copy.start()
            half_copies.append(copy)

    for copy in small_copies:
        copy.wait()
    gain_copies = []
    for k in range(1, n):
        peer = lax.rem(me + k, n)
        copy = pltpu.make_async_remote_copy(
            src_ref=gain_ref,
            dst_ref=gains.at[me],
            send_sem=gain_send_sem.at[k],
            recv_sem=gain_recv_sem.at[n - k],
            device_id={"ap": peer},
            device_id_type=MESH,
        )
        copy.start()
        gain_copies.append(copy)
    gains[me] = gain_ref[...]
    owner_u, rank_u, served_u, before_u, serve_u, position = user_tables(
        cluster_ref[...], serving_ref[...], owner_ref[...], clusters, users, stations, n
    )
    mef = me.astype(jnp.float32)
    mine = iota((n, users), 0) == mef
    served_me = jnp.sum(jnp.where(mine, served_u, 0.0), axis=0, keepdims=True)
    before_me = jnp.sum(jnp.where(mine, before_u, 0.0), axis=0, keepdims=True)
    target = jnp.where(
        served_me > 0.5, owner_u * block + before_me * CU + position, -1.0
    )
    chosen_user = iota((n * block, users), 0) == target
    pick[...] = jnp.where(chosen_user, 1.0, 0.0).astype(jnp.bfloat16)
    for a in range(stations):
        row_here = iota((n * stations, users), 0) == mef * stations + a
        weight = jnp.sum(jnp.where(row_here, serve_u, 0.0), axis=0, keepdims=True)
        weight = weight * gain_ref[a : a + 1, :]
        column = jnp.sum(jnp.where(chosen_user, weight, 0.0), axis=1, keepdims=True)
        pick_weight[a] = jnp.broadcast_to(column, (n * block, LANES))
    wide = jnp.broadcast_to(power_ref[...] * (1.0 / users), (LANES, users))
    power_wide[...] = jnp.transpose(wide)

    for q in range(pieces):
        half_copies[q].wait_recv()
        total = (half[q].astype(jnp.float32) + other[q].astype(jnp.float32)).astype(jnp.bfloat16)
        coef_b[pl.ds(q * users, users), :] = total
        chosen = jnp.dot(pick[...], total, preferred_element_type=jnp.float32)
        chosen = chosen * pick_weight[q // antennas]
        coef_send[:, q] = chosen.astype(jnp.bfloat16).reshape(n, block, 2 * TAPS)
    coef_copies = []
    mine_half = pl.ds(part * (pieces // 2), pieces // 2)
    for k in range(1, n):
        peer = lax.rem(me + k, n)
        copy = pltpu.make_async_remote_copy(
            src_ref=coef_send.at[peer, mine_half],
            dst_ref=coef_all.at[me, mine_half],
            send_sem=coef_send_sem.at[k],
            recv_sem=coef_recv_sem.at[n - k],
            device_id={"ap": peer},
            device_id_type=MESH,
        )
        copy.start()
        coef_copies.append(copy)
    own_coef = pltpu.make_async_copy(coef_send.at[me], coef_all.at[me], local_sem)
    own_coef.start()

    width = tones // chunks
    lane_tiles = width // LANES
    symbols = received_ref.shape[3]
    rows = stations * symbols
    ring_copies = {}
    reach = {}
    for c in range(chunks):
        far, near = n // 2, n - 1 - n // 2
        reach[c] = (far, near) if c % 2 == 0 else (near, far)

    ready = []

    def origin_of(direction, step):
        back = lax.rem(spot + n - step, n) if direction == 0 else lax.rem(spot + step, n)
        return node(back)

    def ring_start(c, direction, step):
        if step > reach[c][direction]:
            return False
        origin = origin_of(direction, step)
        source = own.at[c]
        if step > 0:
            ring_copies[c, direction, step - 1].wait_recv()
            source = solved_all.at[origin, c]
            ready.append((origin, c, source))
        if step == reach[c][direction]:
            return True
        copy = pltpu.make_async_remote_copy(
            src_ref=source,
            dst_ref=solved_all.at[origin, c],
            send_sem=ring_send_sem.at[direction, c, step],
            recv_sem=ring_recv_sem.at[direction, c, step],
            device_id={"ap": right if direction == 0 else left},
            device_id_type=MESH,
        )
        copy.start()
        ring_copies[c, direction, step] = copy
        return True

    steps = max(max(r) for r in reach.values())
    entries = [(i, j) for i in range(antennas) for j in range(i + 1)]
    noise = jnp.concatenate(
        [
            jnp.broadcast_to(noise_ref[0:1, a : a + 1], (symbols, 1))
            for a in range(stations)
        ],
        axis=0,
    )

    for copy in table_copies[1:]:
        copy.wait()
    both = jnp.dot(coef_b[...], coarse[...], preferred_element_type=jnp.float32)
    for reim in range(2):
        sampled[reim] = both[:, reim * COARSE : (reim + 1) * COARSE]
    for a in range(stations):

        def body(step, sums, a=a):
            sums = list(sums)
            for w in range(2):
                row = (step * 2 + w) * 8
                scale = power_wide[pl.ds(pl.multiple_of(row, 8), 8), :]
                re, im = [], []
                for i in range(antennas):
                    at = pl.multiple_of((a * antennas + i) * users + row, 8)
                    re.append(sampled[0, pl.ds(at, 8), :])
                    im.append(sampled[1, pl.ds(at, 8), :])
                at = 0
                for i in range(antennas):
                    sre, sim = re[i] * scale, im[i] * scale
                    for j in range(i + 1):
                        sums[at] = sums[at] + (sre * re[j] + sim * im[j])
                        at += 1
                        if j < i:
                            sums[at] = sums[at] + (sim * re[j] - sre * im[j])
                            at += 1
            return tuple(sums)

        zero = jnp.zeros((8, COARSE), jnp.float32)
        sums = lax.fori_loop(0, users // 16, body, (zero,) * (antennas * antennas))
        for e in range(antennas * antennas):
            value = jnp.sum(sums[e], axis=0, keepdims=True)
            samples[pl.ds(e * rows + a * symbols, symbols), :] = jnp.broadcast_to(
                value, (symbols, COARSE)
            )
    high = samples[...].astype(jnp.bfloat16)
    low = (samples[...] - high.astype(jnp.float32)).astype(jnp.bfloat16)
    cov[...] = (
        jnp.dot(
            jnp.concatenate([high, high], axis=1),
            spread[...],
            preferred_element_type=jnp.float32,
        )
        + jnp.dot(low, spread[:COARSE, :], preferred_element_type=jnp.float32)
    )
    for c in range(chunks):
        base = c * width
        lanes = slice(base, base + width)
        cov_re = [[None] * antennas for _ in range(antennas)]
        cov_im = [[None] * antennas for _ in range(antennas)]
        at = 0
        for i, j in entries:
            cov_re[i][j] = cov[at * rows : (at + 1) * rows, lanes]
            at += 1
            if i == j:
                cov_re[i][j] = cov_re[i][j] + noise
            else:
                cov_im[i][j] = cov[at * rows : (at + 1) * rows, lanes]
                at += 1
        signal = []
        for i in range(antennas):
            signal.append(
                tuple(
                    jnp.concatenate(
                        [
                            received_ref[a, i, reim, :, lanes].astype(jnp.float32)
                            for a in range(stations)
                        ],
                        axis=0,
                    )
                    for reim in range(2)
                )
            )
        solved = hermitian_solve(cov_re, cov_im, signal)
        for i in range(antennas):
            joined = jnp.concatenate([solved[i][0], solved[i][1]], axis=0)
            own[c, pl.ds(i * 2 * rows, 2 * rows), :] = joined.astype(jnp.bfloat16)
        ready.append((me, c, own.at[c]))
        for direction in range(2):
            ring_start(c, direction, 0)

    for copy in gain_copies:
        copy.wait_recv()
    totals = jnp.zeros((1, users), jnp.float32)
    for p in range(n):
        for a in range(stations):
            row = serve_u[p * stations + a : p * stations + a + 1] * gains[p, a : a + 1, :]
            totals = totals + row
    scale = 1.0 / (1.0 + totals)
    held = owner_u == mef
    slot_user = iota((OWN_MAX * CU, users), 0) == jnp.where(held, rank_u * CU + position, -1.0)
    slot_rows = jnp.where(slot_user, 1.0, 0.0)
    slot_scale = jnp.sum(jnp.where(slot_user, scale, 0.0), axis=1, keepdims=True)
    scale_ref[...] = jnp.broadcast_to(slot_scale, (OWN_MAX * CU, LANES))
    hits = []
    for p in range(n):
        goal = jnp.where(
            held & (served_u[p : p + 1] > 0.5), before_u[p : p + 1] * CU + position, -1.0
        )
        hits.append(jnp.where(iota((block, users), 0) == goal, 1.0, 0.0))
    placement = exact_dot(slot_rows, jnp.concatenate(hits, axis=0), ((1,), (1,)))
    place_ref[...] = placement.astype(jnp.bfloat16)

    relay_copies = []
    for k in range(1, n):
        coef_copies[n - k - 1].wait_recv()
        origin = lax.rem(me + n - (n - k), n)
        copy = pltpu.make_async_remote_copy(
            src_ref=coef_all.at[origin, mine_half],
            dst_ref=coef_all.at[origin, mine_half],
            send_sem=relay_send_sem.at[k],
            recv_sem=relay_recv_sem.at[k],
            device_id={"sc": 1 - part},
            device_id_type=MESH,
        )
        copy.start()
        relay_copies.append(copy)
    own_coef.wait()

    def combine(origin, c, source):
        wide = source[...].astype(jnp.float32)
        for i in range(antennas):
            re = wide[i * 2 * rows : i * 2 * rows + rows]
            im = wide[i * 2 * rows + rows : (i + 1) * 2 * rows]
            solved_wide[i, 0] = re
            solved_wide[i, 1] = im
            solved_wide[i, 2] = re + im
        coefs = coef_all[origin].reshape(pieces * block, 2 * TAPS)
        for l in range(lane_tiles):
            columns = pl.ds((c * lane_tiles + l) * 2 * LANES, 2 * LANES)
            smooth[l] = jnp.dot(coefs, table[:, columns], preferred_element_type=jnp.float32)
        for l in range(lane_tiles):
            lanes = pl.ds(l * LANES, LANES)
            sums = [[None] * symbols for _ in range(PEER_MAX)]
            for a in range(stations):
                for i in range(antennas):
                    re, im, gap = [], [], []
                    for k in range(PEER_MAX):
                        at = (a * antennas + i) * block + k * CU
                        re.append(smooth[l, pl.ds(at, CU), :LANES])
                        im.append(smooth[l, pl.ds(at, CU), LANES:])
                        gap.append(re[k] - im[k])
                    for s in range(symbols):
                        row = pl.ds(a * symbols + s, 1)
                        sre = solved_wide[i, 0, row, lanes]
                        sim = solved_wide[i, 1, row, lanes]
                        ssum = solved_wide[i, 2, row, lanes]
                        for k in range(PEER_MAX):
                            new = (re[k] * sre, im[k] * sim, gap[k] * ssum)
                            old = sums[k][s]
                            if old is not None:
                                new = tuple(x + y for x, y in zip(old, new))
                            sums[k][s] = new
            at = pl.ds(pl.multiple_of(origin * block, block), block)
            for s in range(symbols):
                first = [sums[k][s][0] + sums[k][s][1] for k in range(PEER_MAX)]
                second = [
                    sums[k][s][2] - (sums[k][s][0] - sums[k][s][1]) for k in range(PEER_MAX)
                ]
                for reim, values in ((0, first), (1, second)):
                    share[s * 2 + reim, at, pl.ds(c * width + l * LANES, LANES)] = (
                        jnp.concatenate(values, axis=0).astype(jnp.bfloat16)
                    )
        at = pl.ds(pl.multiple_of(origin * block, block), block)
        lanes = pl.ds(c * width, width)
        copy = pltpu.make_async_copy(
            share.at[:, at, lanes], share_hbm.at[:, at, lanes], share_sem.at[len(share_copies)]
        )
        copy.start()
        share_copies.append(copy)

    share_copies = []

    def drain(most):
        for _ in range(most):
            if ready:
                combine(*ready.pop(0))

    drain(1)
    waited = False
    for step in range(1, steps + 1):
        for c in range(chunks):
            for direction in range(2):
                if not ring_start(c, direction, step):
                    continue
                if not waited and len(ready) and ready[0][0] is not me:
                    for copy in relay_copies:
                        copy.wait_recv()
                    waited = True
                drain(1)
    drain(len(ready))
    for copy in share_copies:
        copy.wait()
    for copy in relay_copies:
        copy.wait_send()
    for copy in half_copies:
        copy.wait_send()
    for copy in gain_copies:
        copy.wait_send()
    for copy in coef_copies:
        copy.wait_send()
    for copy in ring_copies.values():
        copy.wait_send()


def place_kernel(
    place_hbm, scale_hbm, share_hbm, out_hbm, place_ref, scale_ref, share, lines, small_sem, in_sem, out_sem
):
    kinds, _, tones = share.shape
    smalls = []
    for source, into in ((place_hbm, place_ref), (scale_hbm, scale_ref)):
        copy = pltpu.make_async_copy(source, into, small_sem.at[len(smalls)])
        copy.start()
        smalls.append(copy)
    symbols, tiles = kinds // 2, tones // LANES
    arrivals = []
    for kind in range(kinds):
        copy = pltpu.make_async_copy(share_hbm.at[kind], share.at[kind], in_sem.at[kind])
        copy.start()
        arrivals.append(copy)
    for copy in smalls:
        copy.wait()
    copies = []
    for s in range(symbols):
        for reim in range(2):
            arrivals[s * 2 + reim].wait()
            placed = jnp.dot(
                place_ref[...], share[s * 2 + reim], preferred_element_type=jnp.float32
            )
            for l in range(tiles):
                for r in range(OWN_MAX):
                    rows = slice(r * CU, (r + 1) * CU)
                    value = placed[rows, l * LANES : (l + 1) * LANES] * scale_ref[rows]
                    lines[s, pl.ds(r * CU * 2 * tiles + l * 2 + reim, CU, stride=2 * tiles), :] = value
        height = 2 * tiles
        copy = pltpu.make_async_copy(
            lines.at[s].reshape(OWN_MAX * CU, height, LANES), out_hbm.at[:, s], out_sem.at[s]
        )
        copy.start()
        copies.append(copy)
    for copy in copies:
        copy.wait()


def ring_functions(mesh):
    n = mesh.shape["ap"]
    half = n // 2

    def plain(q):
        return q

    def node(q):
        upper = q // half
        return (1 - upper) * 2 * q + upper * (2 * (n - q) - 1)

    def place(d):
        odd = d % 2
        return (1 - odd) * (d // 2) + odd * (n - (d + 1) // 2)

    if n % 2:
        return plain, plain
    try:
        axes = list(mesh.axis_names)
        line = np.moveaxis(mesh.devices, axes.index("ap"), 0).reshape(n, -1)[:, 0]
        spots = [tuple(d.coords) for d in line]
        sizes = [max(s[x] for s in spots) + 1 for x in range(3)]

        def length(order):
            far = 0
            for q in range(n):
                one, two = spots[order(q)], spots[order((q + 1) % n)]
                far += sum(
                    min(abs(one[x] - two[x]), sizes[x] - abs(one[x] - two[x])) for x in range(3)
                )
            return far

        if length(plain) < length(node):
            return plain, plain
    except (AttributeError, TypeError):
        pass
    return node, place


def local(
    n,
    parts,
    ring_of,
    unsmoothed_link_guesses,
    received,
    user_power,
    noise_power,
    ap_gain,
    user_cluster,
    serving,
    cluster_owner,
):
    stations, antennas, _, users, tones = unsmoothed_link_guesses.shape
    symbols = received.shape[3]
    pieces = stations * antennas
    block = PEER_MAX * CU
    rows = stations * symbols
    chunks = 2
    width = tones // chunks
    steps = n // 2
    vmem = pl.BlockSpec(memory_space=pltpu.VMEM)
    dma = pltpu.SemaphoreType.DMA
    bf16, f32 = jnp.bfloat16, jnp.float32
    hbm = pl.BlockSpec(memory_space=pltpu.HBM)
    tiles = tones // LANES
    slots = OWN_MAX * CU
    share, place, scale = pl.pallas_call(
        functools.partial(uplink_kernel, n, chunks, ring_of),
        out_shape=(
            jax.ShapeDtypeStruct((symbols * 2, n * block, tones), bf16),
            jax.ShapeDtypeStruct((slots, n * block), bf16),
            jax.ShapeDtypeStruct((slots, LANES), f32),
        ),
        in_specs=[hbm] * 12,
        out_specs=(hbm, vmem, vmem),
        scratch_shapes=[
            pltpu.VMEM((n, pieces, block, 2 * TAPS), bf16),
            pltpu.VMEM((n, chunks, antennas * 2 * rows, width), bf16),
            pltpu.VMEM(received.shape, bf16),
            pltpu.VMEM((1, users), f32),
            pltpu.VMEM((1, stations), f32),
            pltpu.VMEM((stations, users), f32),
            pltpu.VMEM((1, users), jnp.int32),
            pltpu.VMEM(serving.shape, jnp.int32),
            pltpu.VMEM((1, serving.shape[0]), jnp.int32),
            pltpu.VMEM((antennas, 3, rows, width), f32),
            pltpu.VMEM((stations, antennas, 2, users, tones), bf16),
            pltpu.VMEM((tones, 2 * TAPS), bf16),
            pltpu.VMEM((2 * TAPS, 2 * tones), bf16),
            pltpu.VMEM((2 * TAPS, 2 * COARSE), bf16),
            pltpu.VMEM((2 * COARSE, tones), bf16),
            pltpu.VMEM((pieces, users, 2 * TAPS), bf16),
            pltpu.VMEM((pieces, users, 2 * TAPS), bf16),
            pltpu.VMEM((n, pieces, block, 2 * TAPS), bf16),
            pltpu.VMEM((pieces * users, 2 * TAPS), bf16),
            pltpu.VMEM((n, stations, users), f32),
            pltpu.VMEM((n * block, users), bf16),
            pltpu.VMEM((stations, n * block, LANES), f32),
            pltpu.VMEM((users, LANES), f32),
            pltpu.VMEM((2, pieces * users, COARSE), f32),
            pltpu.VMEM((antennas * antennas * rows, COARSE), f32),
            pltpu.VMEM((antennas * antennas * rows, tones), f32),
            pltpu.VMEM((width // LANES, pieces * block, 2 * LANES), f32),
            pltpu.VMEM((chunks, antennas * 2 * rows, width), bf16),
            pltpu.VMEM((symbols * 2, n * block, tones), bf16),
            dma((pieces,)),
            dma((4,)),
            dma((pieces,)),
            dma((pieces,)),
            dma((n,)),
            dma((n,)),
            dma((n,)),
            dma((n,)),
            dma((2, chunks, steps)),
            dma((2, chunks, steps)),
            dma,
            dma((7,)),
            dma((n,)),
            dma((n,)),
            dma((n * chunks,)),
        ],
        compiler_params=pltpu.CompilerParams(
            collective_id=0, has_side_effects=True, vmem_limit_bytes=VMEM_BYTES
        ),
        name="uplink",
    )(
        unsmoothed_link_guesses,
        received,
        user_power.reshape(1, users),
        noise_power.reshape(1, stations),
        ap_gain,
        user_cluster.reshape(1, users),
        serving,
        cluster_owner.reshape(1, -1),
        jnp.asarray(tap_tables(parts, tones)),
        jnp.asarray(tone_tables(parts, tones)),
        jnp.asarray(coarse_table()),
        jnp.asarray(spread_tables(parts, tones)),
    )
    placed = pl.pallas_call(
        place_kernel,
        out_shape=jax.ShapeDtypeStruct((slots, symbols, tiles * 2, LANES), f32),
        in_specs=[hbm, hbm, hbm],
        out_specs=hbm,
        scratch_shapes=[
            pltpu.VMEM((slots, n * block), bf16),
            pltpu.VMEM((slots, LANES), f32),
            pltpu.VMEM((symbols * 2, n * block, tones), bf16),
            pltpu.VMEM((symbols, slots * tiles * 2, LANES), f32),
            dma((2,)),
            dma((symbols * 2,)),
            dma((symbols,)),
        ],
        compiler_params=pltpu.CompilerParams(vmem_limit_bytes=VMEM_BYTES),
        name="place",
    )(place, scale, share)
    placed = placed.reshape(OWN_MAX, CU, symbols, tiles, 2, LANES)
    placed = jnp.transpose(placed, (0, 1, 2, 4, 3, 5))
    return placed.reshape(OWN_MAX, CU, symbols, 2, tones)


def solution(mesh):
    placed = (
        P(("cell", "ap"), None, None, None, "sc"),
        P(("cell", "ap"), None, None, None, "sc"),
        P("cell"),
        P(("cell", "ap")),
        P(("cell", "ap"), None),
        P("cell"),
        P("cell", None),
        P("cell", None),
    )
    return jax.shard_map(
        functools.partial(local, mesh.shape["ap"], mesh.shape["sc"], ring_functions(mesh)),
        mesh=mesh,
        in_specs=placed,
        out_specs=P(("cell", "ap"), None, None, None, "sc"),
        check_vma=False,
    )
```

```python
import functools
import math

import jax
import jax.numpy as jnp
import numpy as np
from jax import lax
from jax.experimental import pallas as pl
from jax.experimental.pallas import tpu as pltpu
from jax.sharding import PartitionSpec as P

TONE_NUMBER = 2048
TAPS = 64
CU = 8
OWN_MAX = 4
PEER_MAX = 2
COARSE = 2 * TAPS
MESH = pl.DeviceIdType.MESH
LANES = 128
VMEM_BYTES = 67043328


def complex_times(left_factor, right_factor):
    return (
        left_factor[0] * right_factor[0] - left_factor[1] * right_factor[1],
        left_factor[0] * right_factor[1] + left_factor[1] * right_factor[0],
    )


def times_conj(left_factor, right_factor):
    return (
        left_factor[0] * right_factor[0] + left_factor[1] * right_factor[1],
        left_factor[1] * right_factor[0] - left_factor[0] * right_factor[1],
    )


def hermitian_solve(cov_re, cov_im, right):
    dimension = len(cov_re)
    factor = {}
    inverses = []
    for j in range(dimension):
        pivot = cov_re[j][j]
        for k in range(j):
            element = factor[j, k]
            pivot = pivot - (element[0] * element[0] + element[1] * element[1])
        inverse = 1.0 / jnp.sqrt(pivot)
        inverses.append(inverse)
        for i in range(j + 1, dimension):
            running = (cov_re[i][j], cov_im[i][j])
            for k in range(j):
                product = times_conj(factor[i, k], factor[j, k])
                running = (running[0] - product[0], running[1] - product[1])
            factor[i, j] = (running[0] * inverse, running[1] * inverse)
    forward = []
    for i in range(dimension):
        running = right[i]
        for k in range(i):
            product = complex_times(factor[i, k], forward[k])
            running = (running[0] - product[0], running[1] - product[1])
        forward.append((running[0] * inverses[i], running[1] * inverses[i]))
    result = [None] * dimension
    for i in range(dimension - 1, -1, -1):
        running = forward[i]
        for k in range(i + 1, dimension):
            product = times_conj(result[k], factor[k, i])
            running = (running[0] - product[0], running[1] - product[1])
        result[i] = (running[0] * inverses[i], running[1] * inverses[i])
    return result


def angles_of(values):
    rotation = np.arange(TAPS, dtype=np.int32)[:, None] * values[None, :] % TONE_NUMBER
    return rotation.astype(np.float32) * np.float32(2.0 * math.pi / TONE_NUMBER)


def wave_table(values):
    cosine, sine = np.cos(angles_of(values)), np.sin(angles_of(values))
    return np.concatenate([cosine, sine], axis=0), np.concatenate([-sine, cosine], axis=0)


def tap_tables(parts, tones):
    made = []
    for part in range(parts):
        real, _ = wave_table(part * tones + np.arange(tones, dtype=np.int32))
        made.append(real.T)
    return np.stack(made).astype(jnp.bfloat16)


def tone_tables(parts, tones):
    made = []
    for part in range(parts):
        real, imag = wave_table(part * tones + np.arange(tones, dtype=np.int32))
        pair = np.stack(
            [real.reshape(2 * TAPS, -1, LANES), imag.reshape(2 * TAPS, -1, LANES)], axis=2
        )
        made.append(pair.reshape(2 * TAPS, 2 * tones))
    return np.stack(made).astype(jnp.bfloat16)


def coarse_table():
    step = TONE_NUMBER // COARSE
    real, imag = wave_table(step * np.arange(COARSE, dtype=np.int32))
    return np.concatenate([real, imag], axis=1).astype(jnp.bfloat16)


def spread_tables(parts, tones):
    step = TONE_NUMBER // COARSE
    made = []
    for part in range(parts):
        values = part * tones + np.arange(tones, dtype=np.int64)
        gap = values[None, :] - step * np.arange(COARSE, dtype=np.int64)[:, None]
        kernel = np.ones(gap.shape, np.float64)
        for d in range(1, COARSE // 2 + 1):
            share = 2.0 if d < COARSE // 2 else 1.0
            kernel += share * np.cos(2.0 * math.pi / TONE_NUMBER * (d * gap % TONE_NUMBER))
        kernel /= COARSE
        high = kernel.astype(np.float32).astype(jnp.bfloat16)
        low = (kernel - high.astype(np.float64)).astype(np.float32).astype(jnp.bfloat16)
        made.append(np.concatenate([high, low], axis=0))
    return np.stack(made)


def exact_dot(left, right, dims):
    return lax.dot_general(
        left.astype(jnp.bfloat16),
        right.astype(jnp.bfloat16),
        (dims, ((), ())),
        preferred_element_type=jnp.float32,
    )


def iota(shape, dim):
    return lax.broadcasted_iota(jnp.int32, shape, dim).astype(jnp.float32)


def user_tables(user_cluster, serving, owner, clusters, users, group, n):
    onehot = (iota((clusters, users), 0) == user_cluster.astype(jnp.float32)).astype(jnp.float32)
    owner_row = owner.astype(jnp.float32)
    square = (clusters, clusters)
    rows, cols = iota(square, 0), iota(square, 1)
    owner_col = jnp.sum(jnp.where(rows == cols, owner_row, 0.0), axis=1, keepdims=True)
    same = owner_col == owner_row
    earlier = jnp.where(same & (cols < rows), 1.0, 0.0)
    serve = serving.astype(jnp.float32)
    pair = jnp.where(
        jnp.floor((iota((group * n, n), 0) + 0.5) * (1.0 / group)) == iota((group * n, n), 1),
        1.0,
        0.0,
    )
    served = jnp.where(exact_dot(serve, pair, ((1,), (0,))) > 0.5, 1.0, 0.0)
    before = exact_dot(earlier, served, ((1,), (0,)))
    rank = jnp.sum(earlier, axis=1, keepdims=True)
    owner_u = jnp.sum(onehot * owner_col, axis=0, keepdims=True)
    rank_u = jnp.sum(onehot * rank, axis=0, keepdims=True)
    served_u = exact_dot(served, onehot, ((0,), (0,)))
    before_u = exact_dot(before, onehot, ((0,), (0,)))
    serve_u = exact_dot(serve, onehot, ((0,), (0,)))
    equal = exact_dot(onehot, onehot, ((0,), (0,)))
    both = (users, users)
    position = jnp.sum(
        jnp.where(iota(both, 0) < iota(both, 1), equal, 0.0), axis=0, keepdims=True
    )
    return owner_u, rank_u, served_u, before_u, serve_u, position


def uplink_kernel(
    n,
    ring_of,
    guess_hbm,
    received_hbm,
    power_hbm,
    noise_hbm,
    gain_hbm,
    cluster_hbm,
    serving_hbm,
    owner_hbm,
    taps_hbm,
    table_hbm,
    coarse_hbm,
    spread_hbm,
    share_hbm,
    place_hbm,
    scale_hbm,
    packet_all,
    signal_all,
    received_ref,
    power_ref,
    noise_ref,
    gain_ref,
    cluster_ref,
    serving_ref,
    owner_ref,
    guess,
    taps,
    table,
    coarse,
    spread,
    half,
    other,
    packet_send,
    coef_b,
    gains,
    pick,
    pick_weight,
    power_wide,
    sampled,
    samples,
    cov,
    solved,
    smooth,
    share,
    place_ref,
    scale_ref,
    guess_sem,
    table_sem,
    half_send_sem,
    half_recv_sem,
    gain_send_sem,
    gain_recv_sem,
    packet_send_sem,
    packet_recv_sem,
    ring_send_sem,
    ring_recv_sem,
    small_sem,
    relay_send_sem,
    relay_recv_sem,
    share_sem,
    place_sem,
):
    stations, antennas, _, users, tones = guess.shape
    pieces = stations * antennas
    block = PEER_MAX * CU
    clusters = serving_ref.shape[0]
    me = lax.axis_index("ap")
    part = lax.axis_index("sc")
    node, place = ring_of
    spot = place(me)
    right = node(lax.rem(spot + 1, n))
    left = node(lax.rem(spot + n - 1, n))

    table_copies = []
    for source, into in (
        (taps_hbm.at[part], taps),
        (coarse_hbm, coarse),
        (spread_hbm.at[part], spread),
        (table_hbm.at[part], table),
    ):
        table_copies.append(
            pltpu.make_async_copy(source, into, table_sem.at[len(table_copies)])
        )
    received_copy = pltpu.make_async_copy(received_hbm, received_ref, place_sem.at[0])
    received_copy.start()
    table_copies[0].start()
    guess_copies = []
    for q in range(pieces):
        a, i = q // antennas, q % antennas
        copy = pltpu.make_async_copy(guess_hbm.at[a, i], guess.at[a, i], guess_sem.at[q])
        guess_copies.append(copy)
    for copy in guess_copies[: pieces // 2]:
        copy.start()
    barrier = pltpu.get_barrier_semaphore()
    pl.semaphore_signal(barrier, inc=1, device_id={"sc": 1 - part}, device_id_type=MESH)
    for k in range(1, n):
        pl.semaphore_signal(
            barrier, inc=1, device_id={"ap": lax.rem(me + k, n)}, device_id_type=MESH
        )

    ring_copies = {}
    reach = {}
    for c in range(stations):
        far, near = n // 2, n - 1 - n // 2
        reach[c] = (far, near) if c % 2 == 0 else (near, far)
    steps = max(max(r) for r in reach.values())

    def origin_of(direction, step):
        back = lax.rem(spot + n - step, n) if direction == 0 else lax.rem(spot + step, n)
        return node(back)

    def ring_step(c, step):
        for direction in range(2):
            if step > reach[c][direction]:
                continue
            origin = origin_of(direction, step)
            source = received_ref.at[c]
            if step > 0:
                ring_copies[c, direction, step - 1].wait_recv()
                source = signal_all.at[origin, c]
            if step == reach[c][direction]:
                continue
            copy = pltpu.make_async_remote_copy(
                src_ref=source,
                dst_ref=signal_all.at[origin, c],
                send_sem=ring_send_sem.at[direction, c, step],
                recv_sem=ring_recv_sem.at[direction, c, step],
                device_id={"ap": right if direction == 0 else left},
                device_id_type=MESH,
            )
            copy.start()
            ring_copies[c, direction, step] = copy

    table_copies[0].wait()
    for copy in guess_copies[pieces // 2 :]:
        copy.start()
    small_copies = []
    for source, into in (
        (cluster_hbm, cluster_ref),
        (serving_hbm, serving_ref),
        (owner_hbm, owner_ref),
        (power_hbm, power_ref),
        (gain_hbm, gain_ref),
        (noise_hbm, noise_ref),
    ):
        copy = pltpu.make_async_copy(source, into, small_sem.at[len(small_copies)])
        copy.start()
        small_copies.append(copy)
    for copy in table_copies[1:]:
        copy.start()

    half_copies = []
    together = 2
    lower = lax.broadcasted_iota(jnp.int32, (users, 2 * TAPS), 1) < TAPS
    for first in range(0, pieces, together):
        group = range(first, first + together)
        for q in group:
            guess_copies[q].wait()
        a, i = first // antennas, first % antennas
        products = jnp.dot(
            guess[a, i : i + together].reshape(together * 2 * users, tones),
            taps[...],
            preferred_element_type=jnp.float32,
        )
        for q in group:
            at = (q - first) * 2 * users
            turned = pltpu.roll(products[at + users : at + 2 * users], TAPS, axis=1)
            sums = products[at : at + users] + jnp.where(lower, -turned, turned)
            half[q] = (sums * (1.0 / TONE_NUMBER)).astype(jnp.bfloat16)
        if first == 0:
            pl.semaphore_wait(barrier, n)
            received_copy.wait()
            for c in range(stations):
                ring_step(c, 0)
        for q in group:
            copy = pltpu.make_async_remote_copy(
                src_ref=half.at[q],
                dst_ref=other.at[q],
                send_sem=half_send_sem.at[q],
                recv_sem=half_recv_sem.at[q],
                device_id={"sc": 1 - part},
                device_id_type=MESH,
            )
            copy.start()
            half_copies.append(copy)

    for copy in small_copies:
        copy.wait()
    gain_copies = []
    for k in range(1, n):
        peer = lax.rem(me + k, n)
        copy = pltpu.make_async_remote_copy(
            src_ref=gain_ref,
            dst_ref=gains.at[me],
            send_sem=gain_send_sem.at[k],
            recv_sem=gain_recv_sem.at[n - k],
            device_id={"ap": peer},
            device_id_type=MESH,
        )
        copy.start()
        gain_copies.append(copy)
    gains[me] = gain_ref[...]
    owner_u, rank_u, served_u, before_u, serve_u, position = user_tables(
        cluster_ref[...], serving_ref[...], owner_ref[...], clusters, users, stations, n
    )
    mef = me.astype(jnp.float32)
    mine = iota((n, users), 0) == mef
    served_me = jnp.sum(jnp.where(mine, served_u, 0.0), axis=0, keepdims=True)
    before_me = jnp.sum(jnp.where(mine, before_u, 0.0), axis=0, keepdims=True)
    target = jnp.where(
        served_me > 0.5, owner_u * block + before_me * CU + position, -1.0
    )
    chosen_user = iota((n * block, users), 0) == target
    pick[...] = jnp.where(chosen_user, 1.0, 0.0).astype(jnp.bfloat16)
    for a in range(stations):
        row_here = iota((n * stations, users), 0) == mef * stations + a
        weight = jnp.sum(jnp.where(row_here, serve_u, 0.0), axis=0, keepdims=True)
        weight = weight * gain_ref[a : a + 1, :]
        column = jnp.sum(jnp.where(chosen_user, weight, 0.0), axis=1, keepdims=True)
        pick_weight[a] = jnp.broadcast_to(column, (n * block, LANES))
    wide = jnp.broadcast_to(power_ref[...] * (1.0 / users), (LANES, users))
    power_wide[...] = jnp.transpose(wide)

    ring_step(0, 1)
    for q in range(pieces):
        half_copies[q].wait_recv()
        total = (half[q].astype(jnp.float32) + other[q].astype(jnp.float32)).astype(jnp.bfloat16)
        coef_b[pl.ds(q * users, users), :] = total
        chosen = jnp.dot(pick[...], total, preferred_element_type=jnp.float32)
        chosen = chosen * pick_weight[q // antennas]
        packet_send[:, q] = chosen.astype(jnp.bfloat16).reshape(n, block, 2 * TAPS)
    symbols = received_ref.shape[3]
    rows = stations * symbols
    entries = [(i, j) for i in range(antennas) for j in range(i + 1)]
    kinds = antennas * antennas
    for c in range(1, stations):
        ring_step(c, 1)
    for copy in table_copies[1:]:
        copy.wait()
    both = jnp.dot(coef_b[...], coarse[...], preferred_element_type=jnp.float32)
    for reim in range(2):
        sampled[reim] = both[:, reim * COARSE : (reim + 1) * COARSE]
    for a in range(stations):

        def body(step, sums, a=a):
            sums = list(sums)
            for w in range(2):
                row = (step * 2 + w) * 8
                scale = power_wide[pl.ds(pl.multiple_of(row, 8), 8), :]
                re, im = [], []
                for i in range(antennas):
                    at = pl.multiple_of((a * antennas + i) * users + row, 8)
                    re.append(sampled[0, pl.ds(at, 8), :])
                    im.append(sampled[1, pl.ds(at, 8), :])
                at = 0
                for i in range(antennas):
                    sre, sim = re[i] * scale, im[i] * scale
                    for j in range(i + 1):
                        sums[at] = sums[at] + (sre * re[j] + sim * im[j])
                        at += 1
                        if j < i:
                            sums[at] = sums[at] + (sim * re[j] - sre * im[j])
                            at += 1
            return tuple(sums)

        zero = jnp.zeros((8, COARSE), jnp.float32)
        sums = lax.fori_loop(0, users // 16, body, (zero,) * (antennas * antennas))
        at = 0
        for i, j in entries:
            for reim in range(1 if i == j else 2):
                value = jnp.sum(sums[at], axis=0, keepdims=True)
                if i == j:
                    value = value + noise_ref[0:1, a : a + 1]
                samples[pl.ds(at * stations + a, 1), :] = value
                at += 1
    high = samples[...].astype(jnp.bfloat16)
    low = (samples[...] - high.astype(jnp.float32)).astype(jnp.bfloat16)
    held_rows = kinds * stations // block
    for k in range(n):
        packet_send[k, pieces : pieces + held_rows] = high.reshape(held_rows, block, COARSE)
        packet_send[k, pieces + held_rows :] = low.reshape(held_rows, block, COARSE)
    parcels = packet_send.shape[1]
    mine_half = pl.ds(part * (parcels // 2), parcels // 2)
    packets = {}
    for step in range(1, steps + 1):
        for k in sorted({step, n - step}):
            peer = node(lax.rem(spot + k, n))
            copy = pltpu.make_async_remote_copy(
                src_ref=packet_send.at[peer, mine_half],
                dst_ref=packet_all.at[me, mine_half],
                send_sem=packet_send_sem.at[k],
                recv_sem=packet_recv_sem.at[k],
                device_id={"ap": peer},
                device_id_type=MESH,
            )
            copy.start()
            packets[k] = copy

    relays = {}

    def relay_start(step):
        for k in sorted({step, n - step}):
            packets[k].wait_recv()
            origin = node(lax.rem(spot + n - k, n))
            copy = pltpu.make_async_remote_copy(
                src_ref=packet_all.at[origin, mine_half],
                dst_ref=packet_all.at[origin, mine_half],
                send_sem=relay_send_sem.at[k],
                recv_sem=relay_recv_sem.at[k],
                device_id={"sc": 1 - part},
                device_id_type=MESH,
            )
            copy.start()
            relays[k] = copy

    def relay_wait(step):
        for k in sorted({step, n - step}):
            relays[k].wait_recv()

    tiles = tones // LANES
    station_of = lax.broadcasted_iota(jnp.int32, (rows, 1), 0)

    def prepare(origin, packet, signals, slot):
        high = packet[pieces : pieces + held_rows].reshape(kinds * stations, COARSE)
        low = packet[pieces + held_rows :].reshape(kinds * stations, COARSE)
        cov[slot] = jnp.dot(
            jnp.concatenate([high, high], axis=1),
            spread[...],
            preferred_element_type=jnp.float32,
        ) + jnp.dot(low, spread[:COARSE, :], preferred_element_type=jnp.float32)
        width = min(tones, 4 * LANES)
        for base in range(0, tones, width):
            lanes = slice(base, base + width)

            def entry(at):
                value = jnp.broadcast_to(
                    cov[slot, at * stations : at * stations + 1, lanes], (rows, width)
                )
                for a in range(1, stations):
                    row = jnp.broadcast_to(
                        cov[slot, at * stations + a : at * stations + a + 1, lanes], (rows, width)
                    )
                    value = jnp.where(station_of < a * symbols, value, row)
                return value

            cov_re = [[None] * antennas for _ in range(antennas)]
            cov_im = [[None] * antennas for _ in range(antennas)]
            at = 0
            for i, j in entries:
                cov_re[i][j] = entry(at)
                at += 1
                if i != j:
                    cov_im[i][j] = entry(at)
                    at += 1
            right_side = []
            for i in range(antennas):
                right_side.append(
                    tuple(
                        jnp.concatenate(
                            [
                                signals[a, i, reim, :, lanes].astype(jnp.float32)
                                for a in range(stations)
                            ],
                            axis=0,
                        )
                        for reim in range(2)
                    )
                )
            answer = hermitian_solve(cov_re, cov_im, right_side)
            for i in range(antennas):
                re, im = answer[i]
                solved[slot, i, 0, :, lanes] = re
                solved[slot, i, 1, :, lanes] = im
                solved[slot, i, 2, :, lanes] = re + im

    def combine(origin, packet, slot):
        coefs = packet[:pieces].reshape(pieces * block, 2 * TAPS)
        for l in range(tiles):
            columns = pl.ds(l * 2 * LANES, 2 * LANES)
            smooth[slot, l] = jnp.dot(coefs, table[:, columns], preferred_element_type=jnp.float32)
        here = pl.ds(pl.multiple_of(origin * block, block), block)
        for l in range(tiles):
            lanes = pl.ds(l * LANES, LANES)
            sums = [[None] * symbols for _ in range(PEER_MAX)]
            for a in range(stations):
                for i in range(antennas):
                    re, im, gap = [], [], []
                    for k in range(PEER_MAX):
                        at = (a * antennas + i) * block + k * CU
                        re.append(smooth[slot, l, pl.ds(at, CU), :LANES])
                        im.append(smooth[slot, l, pl.ds(at, CU), LANES:])
                        gap.append(re[k] - im[k])
                    for s in range(symbols):
                        row = pl.ds(a * symbols + s, 1)
                        sre = solved[slot, i, 0, row, lanes]
                        sim = solved[slot, i, 1, row, lanes]
                        ssum = solved[slot, i, 2, row, lanes]
                        for k in range(PEER_MAX):
                            new = (re[k] * sre, im[k] * sim, gap[k] * ssum)
                            old = sums[k][s]
                            if old is not None:
                                new = tuple(x + y for x, y in zip(old, new))
                            sums[k][s] = new
            for s in range(symbols):
                first = [sums[k][s][0] + sums[k][s][1] for k in range(PEER_MAX)]
                second = [
                    sums[k][s][2] - (sums[k][s][0] - sums[k][s][1]) for k in range(PEER_MAX)
                ]
                for reim, values in ((0, first), (1, second)):
                    share[s * 2 + reim, here, lanes] = jnp.concatenate(values, axis=0).astype(
                        jnp.bfloat16
                    )

    share_copies = []

    def send_share(origin):
        here = pl.ds(pl.multiple_of(origin * block, block), block)
        copy = pltpu.make_async_copy(
            share.at[:, here], share_hbm.at[:, here], share_sem.at[len(share_copies)]
        )
        copy.start()
        share_copies.append(copy)

    tasks = [(me, packet_send.at[me], received_ref, 0)]
    for step in range(1, steps + 1):
        for direction in range(2 if step <= n - 1 - n // 2 else 1):
            origin = origin_of(direction, step)
            tasks.append((origin, packet_all.at[origin], signal_all.at[origin], step))

    prepare(*tasks[0][:3], 0)
    combine(*tasks[0][:2], 0)
    send_share(me)
    for copy in gain_copies:
        copy.wait_recv()
    totals = jnp.zeros((1, users), jnp.float32)
    for p in range(n):
        for a in range(stations):
            row = serve_u[p * stations + a : p * stations + a + 1] * gains[p, a : a + 1, :]
            totals = totals + row
    scale = 1.0 / (1.0 + totals)
    held = owner_u == mef
    slot_user = iota((OWN_MAX * CU, users), 0) == jnp.where(held, rank_u * CU + position, -1.0)
    slot_rows = jnp.where(slot_user, 1.0, 0.0)
    slot_scale = jnp.sum(jnp.where(slot_user, scale, 0.0), axis=1, keepdims=True)
    scale_ref[...] = jnp.broadcast_to(slot_scale, (OWN_MAX * CU, LANES))
    hits = []
    for p in range(n):
        goal = jnp.where(
            held & (served_u[p : p + 1] > 0.5), before_u[p : p + 1] * CU + position, -1.0
        )
        hits.append(jnp.where(iota((block, users), 0) == goal, 1.0, 0.0))
    placement = exact_dot(slot_rows, jnp.concatenate(hits, axis=0), ((1,), (1,)))
    place_ref[...] = placement.astype(jnp.bfloat16)
    place_copies = []
    for source, into in ((place_ref, place_hbm), (scale_ref, scale_hbm)):
        copy = pltpu.make_async_copy(source, into, place_sem.at[1 + len(place_copies)])
        copy.start()
        place_copies.append(copy)

    def advance(step, c):
        if step <= steps:
            ring_step(c, step)

    relay_start(1)
    for c in range(stations):
        advance(2, c)
    relay_wait(1)
    prepare(*tasks[1][:3], 1)
    for t in range(1, len(tasks)):
        origin, packet, _, step = tasks[t]
        last = t + 1 == len(tasks)
        if not last and tasks[t + 1][3] > step:
            relay_start(step + 1)
            for c in range(stations):
                if step + 1 > 2:
                    advance(step + 1, c)
            relay_wait(step + 1)
        combine(origin, packet, t % 2)
        if not last:
            prepare(*tasks[t + 1][:3], (t + 1) % 2)
        send_share(origin)
    for copy in share_copies + place_copies:
        copy.wait()
    for copy in relays.values():
        copy.wait_send()
    for copy in half_copies:
        copy.wait_send()
    for copy in gain_copies:
        copy.wait_send()
    for copy in packets.values():
        copy.wait_send()
    for copy in ring_copies.values():
        copy.wait_send()


def place_kernel(
    place_hbm, scale_hbm, share_hbm, out_hbm, place_ref, scale_ref, share, lines, small_sem, in_sem, out_sem
):
    kinds, _, tones = share.shape
    smalls = []
    for source, into in ((place_hbm, place_ref), (scale_hbm, scale_ref)):
        copy = pltpu.make_async_copy(source, into, small_sem.at[len(smalls)])
        copy.start()
        smalls.append(copy)
    symbols, tiles = kinds // 2, tones // LANES
    arrivals = []
    for kind in range(kinds):
        copy = pltpu.make_async_copy(share_hbm.at[kind], share.at[kind], in_sem.at[kind])
        copy.start()
        arrivals.append(copy)
    for copy in smalls:
        copy.wait()
    copies = []
    for s in range(symbols):
        for reim in range(2):
            arrivals[s * 2 + reim].wait()
            placed = jnp.dot(
                place_ref[...], share[s * 2 + reim], preferred_element_type=jnp.float32
            )
            for l in range(tiles):
                for r in range(OWN_MAX):
                    rows = slice(r * CU, (r + 1) * CU)
                    value = placed[rows, l * LANES : (l + 1) * LANES] * scale_ref[rows]
                    lines[s, pl.ds(r * CU * 2 * tiles + l * 2 + reim, CU, stride=2 * tiles), :] = value
        height = 2 * tiles
        copy = pltpu.make_async_copy(
            lines.at[s].reshape(OWN_MAX * CU, height, LANES), out_hbm.at[:, s], out_sem.at[s]
        )
        copy.start()
        copies.append(copy)
    for copy in copies:
        copy.wait()


def ring_functions(mesh):
    n = mesh.shape["ap"]
    half = n // 2

    def plain(q):
        return q

    def node(q):
        upper = q // half
        return (1 - upper) * 2 * q + upper * (2 * (n - q) - 1)

    def place(d):
        odd = d % 2
        return (1 - odd) * (d // 2) + odd * (n - (d + 1) // 2)

    if n % 2:
        return plain, plain
    try:
        axes = list(mesh.axis_names)
        line = np.moveaxis(mesh.devices, axes.index("ap"), 0).reshape(n, -1)[:, 0]
        spots = [tuple(d.coords) for d in line]
        sizes = [max(s[x] for s in spots) + 1 for x in range(3)]

        def length(order):
            far = 0
            for q in range(n):
                one, two = spots[order(q)], spots[order((q + 1) % n)]
                far += sum(
                    min(abs(one[x] - two[x]), sizes[x] - abs(one[x] - two[x])) for x in range(3)
                )
            return far

        if length(plain) < length(node):
            return plain, plain
    except (AttributeError, TypeError):
        pass
    return node, place


def local(
    n,
    parts,
    ring_of,
    unsmoothed_link_guesses,
    received,
    user_power,
    noise_power,
    ap_gain,
    user_cluster,
    serving,
    cluster_owner,
):
    stations, antennas, _, users, tones = unsmoothed_link_guesses.shape
    symbols = received.shape[3]
    pieces = stations * antennas
    block = PEER_MAX * CU
    rows = stations * symbols
    parcels = pieces + 2 * (antennas * antennas * stations // block)
    steps = n // 2
    dma = pltpu.SemaphoreType.DMA
    bf16, f32 = jnp.bfloat16, jnp.float32
    hbm = pl.BlockSpec(memory_space=pltpu.HBM)
    tiles = tones // LANES
    slots = OWN_MAX * CU
    share, place, scale = pl.pallas_call(
        functools.partial(uplink_kernel, n, ring_of),
        out_shape=(
            jax.ShapeDtypeStruct((symbols * 2, n * block, tones), bf16),
            jax.ShapeDtypeStruct((slots, n * block), bf16),
            jax.ShapeDtypeStruct((slots, LANES), f32),
        ),
        in_specs=[hbm] * 12,
        out_specs=(hbm, hbm, hbm),
        scratch_shapes=[
            pltpu.VMEM((n, parcels, block, 2 * TAPS), bf16),
            pltpu.VMEM((n,) + received.shape, bf16),
            pltpu.VMEM(received.shape, bf16),
            pltpu.VMEM((1, users), f32),
            pltpu.VMEM((1, stations), f32),
            pltpu.VMEM((stations, users), f32),
            pltpu.VMEM((1, users), jnp.int32),
            pltpu.VMEM(serving.shape, jnp.int32),
            pltpu.VMEM((1, serving.shape[0]), jnp.int32),
            pltpu.VMEM((stations, antennas, 2, users, tones), bf16),
            pltpu.VMEM((tones, 2 * TAPS), bf16),
            pltpu.VMEM((2 * TAPS, 2 * tones), bf16),
            pltpu.VMEM((2 * TAPS, 2 * COARSE), bf16),
            pltpu.VMEM((2 * COARSE, tones), bf16),
            pltpu.VMEM((pieces, users, 2 * TAPS), bf16),
            pltpu.VMEM((pieces, users, 2 * TAPS), bf16),
            pltpu.VMEM((n, parcels, block, 2 * TAPS), bf16),
            pltpu.VMEM((pieces * users, 2 * TAPS), bf16),
            pltpu.VMEM((n, stations, users), f32),
            pltpu.VMEM((n * block, users), bf16),
            pltpu.VMEM((stations, n * block, LANES), f32),
            pltpu.VMEM((users, LANES), f32),
            pltpu.VMEM((2, pieces * users, COARSE), f32),
            pltpu.VMEM((antennas * antennas * stations, COARSE), f32),
            pltpu.VMEM((2, antennas * antennas * stations, tones), f32),
            pltpu.VMEM((2, antennas, 3, rows, tones), f32),
            pltpu.VMEM((2, tiles, pieces * block, 2 * LANES), f32),
            pltpu.VMEM((symbols * 2, n * block, tones), bf16),
            pltpu.VMEM((slots, n * block), bf16),
            pltpu.VMEM((slots, LANES), f32),
            dma((pieces,)),
            dma((4,)),
            dma((pieces,)),
            dma((pieces,)),
            dma((n,)),
            dma((n,)),
            dma((n,)),
            dma((n,)),
            dma((2, stations, steps)),
            dma((2, stations, steps)),
            dma((6,)),
            dma((n,)),
            dma((n,)),
            dma((n,)),
            dma((3,)),
        ],
        compiler_params=pltpu.CompilerParams(
            collective_id=0, has_side_effects=True, vmem_limit_bytes=VMEM_BYTES
        ),
        name="uplink",
    )(
        unsmoothed_link_guesses,
        received,
        user_power.reshape(1, users),
        noise_power.reshape(1, stations),
        ap_gain,
        user_cluster.reshape(1, users),
        serving,
        cluster_owner.reshape(1, -1),
        jnp.asarray(tap_tables(parts, tones)),
        jnp.asarray(tone_tables(parts, tones)),
        jnp.asarray(coarse_table()),
        jnp.asarray(spread_tables(parts, tones)),
    )
    placed = pl.pallas_call(
        place_kernel,
        out_shape=jax.ShapeDtypeStruct((slots, symbols, tiles * 2, LANES), f32),
        in_specs=[hbm, hbm, hbm],
        out_specs=hbm,
        scratch_shapes=[
            pltpu.VMEM((slots, n * block), bf16),
            pltpu.VMEM((slots, LANES), f32),
            pltpu.VMEM((symbols * 2, n * block, tones), bf16),
            pltpu.VMEM((symbols, slots * tiles * 2, LANES), f32),
            dma((2,)),
            dma((symbols * 2,)),
            dma((symbols,)),
        ],
        compiler_params=pltpu.CompilerParams(vmem_limit_bytes=VMEM_BYTES),
        name="place",
    )(place, scale, share)
    placed = placed.reshape(OWN_MAX, CU, symbols, tiles, 2, LANES)
    placed = jnp.transpose(placed, (0, 1, 2, 4, 3, 5))
    return placed.reshape(OWN_MAX, CU, symbols, 2, tones)


def solution(mesh):
    placed = (
        P(("cell", "ap"), None, None, None, "sc"),
        P(("cell", "ap"), None, None, None, "sc"),
        P("cell"),
        P(("cell", "ap")),
        P(("cell", "ap"), None),
        P("cell"),
        P("cell", None),
        P("cell", None),
    )
    return jax.shard_map(
        functools.partial(local, mesh.shape["ap"], mesh.shape["sc"], ring_functions(mesh)),
        mesh=mesh,
        in_specs=placed,
        out_specs=P(("cell", "ap"), None, None, None, "sc"),
        check_vma=False,
    )
```

```python
import functools
import math

import jax
import jax.numpy as jnp
import numpy as np
from jax import lax
from jax.experimental import pallas as pl
from jax.experimental.pallas import tpu as pltpu
from jax.sharding import PartitionSpec as P

TONE_NUMBER = 2048
TAPS = 64
CU = 8
OWN_MAX = 4
PEER_MAX = 2
COARSE = 2 * TAPS
MESH = pl.DeviceIdType.MESH
LANES = 128
VMEM_BYTES = 67043328


def complex_times(left_factor, right_factor):
    return (
        left_factor[0] * right_factor[0] - left_factor[1] * right_factor[1],
        left_factor[0] * right_factor[1] + left_factor[1] * right_factor[0],
    )


def times_conj(left_factor, right_factor):
    return (
        left_factor[0] * right_factor[0] + left_factor[1] * right_factor[1],
        left_factor[1] * right_factor[0] - left_factor[0] * right_factor[1],
    )


def hermitian_solve(cov_re, cov_im, right):
    dimension = len(cov_re)
    factor = {}
    inverses = []
    for j in range(dimension):
        pivot = cov_re[j][j]
        for k in range(j):
            element = factor[j, k]
            pivot = pivot - (element[0] * element[0] + element[1] * element[1])
        inverse = 1.0 / jnp.sqrt(pivot)
        inverses.append(inverse)
        for i in range(j + 1, dimension):
            running = (cov_re[i][j], cov_im[i][j])
            for k in range(j):
                product = times_conj(factor[i, k], factor[j, k])
                running = (running[0] - product[0], running[1] - product[1])
            factor[i, j] = (running[0] * inverse, running[1] * inverse)
    forward = []
    for i in range(dimension):
        running = right[i]
        for k in range(i):
            product = complex_times(factor[i, k], forward[k])
            running = (running[0] - product[0], running[1] - product[1])
        forward.append((running[0] * inverses[i], running[1] * inverses[i]))
    result = [None] * dimension
    for i in range(dimension - 1, -1, -1):
        running = forward[i]
        for k in range(i + 1, dimension):
            product = times_conj(result[k], factor[k, i])
            running = (running[0] - product[0], running[1] - product[1])
        result[i] = (running[0] * inverses[i], running[1] * inverses[i])
    return result


def angles_of(values):
    rotation = np.arange(TAPS, dtype=np.int32)[:, None] * values[None, :] % TONE_NUMBER
    return rotation.astype(np.float32) * np.float32(2.0 * math.pi / TONE_NUMBER)


def wave_table(values):
    cosine, sine = np.cos(angles_of(values)), np.sin(angles_of(values))
    return np.concatenate([cosine, sine], axis=0), np.concatenate([-sine, cosine], axis=0)


def tap_tables(parts, tones):
    made = []
    for part in range(parts):
        real, _ = wave_table(part * tones + np.arange(tones, dtype=np.int32))
        made.append(real.T)
    return np.stack(made).astype(jnp.bfloat16)


def tone_tables(parts, tones):
    made = []
    for part in range(parts):
        real, imag = wave_table(part * tones + np.arange(tones, dtype=np.int32))
        pair = np.stack(
            [real.reshape(2 * TAPS, -1, LANES), imag.reshape(2 * TAPS, -1, LANES)], axis=2
        )
        made.append(pair.reshape(2 * TAPS, 2 * tones))
    return np.stack(made).astype(jnp.bfloat16)


def coarse_table():
    step = TONE_NUMBER // COARSE
    real, imag = wave_table(step * np.arange(COARSE, dtype=np.int32))
    return np.concatenate([real, imag], axis=1).astype(jnp.bfloat16)


def spread_tables(parts, tones):
    step = TONE_NUMBER // COARSE
    made = []
    for part in range(parts):
        values = part * tones + np.arange(tones, dtype=np.int64)
        gap = values[None, :] - step * np.arange(COARSE, dtype=np.int64)[:, None]
        kernel = np.ones(gap.shape, np.float64)
        for d in range(1, COARSE // 2 + 1):
            share = 2.0 if d < COARSE // 2 else 1.0
            kernel += share * np.cos(2.0 * math.pi / TONE_NUMBER * (d * gap % TONE_NUMBER))
        kernel /= COARSE
        high = kernel.astype(np.float32).astype(jnp.bfloat16)
        low = (kernel - high.astype(np.float64)).astype(np.float32).astype(jnp.bfloat16)
        made.append(np.concatenate([high, low], axis=0))
    return np.stack(made)


def exact_dot(left, right, dims):
    return lax.dot_general(
        left.astype(jnp.bfloat16),
        right.astype(jnp.bfloat16),
        (dims, ((), ())),
        preferred_element_type=jnp.float32,
    )


def iota(shape, dim):
    return lax.broadcasted_iota(jnp.int32, shape, dim).astype(jnp.float32)


def user_tables(user_cluster, serving, owner, clusters, users, group, n):
    onehot = (iota((clusters, users), 0) == user_cluster.astype(jnp.float32)).astype(jnp.float32)
    owner_row = owner.astype(jnp.float32)
    square = (clusters, clusters)
    rows, cols = iota(square, 0), iota(square, 1)
    owner_col = jnp.sum(jnp.where(rows == cols, owner_row, 0.0), axis=1, keepdims=True)
    same = owner_col == owner_row
    earlier = jnp.where(same & (cols < rows), 1.0, 0.0)
    serve = serving.astype(jnp.float32)
    pair = jnp.where(
        jnp.floor((iota((group * n, n), 0) + 0.5) * (1.0 / group)) == iota((group * n, n), 1),
        1.0,
        0.0,
    )
    served = jnp.where(exact_dot(serve, pair, ((1,), (0,))) > 0.5, 1.0, 0.0)
    before = exact_dot(earlier, served, ((1,), (0,)))
    rank = jnp.sum(earlier, axis=1, keepdims=True)
    owner_u = jnp.sum(onehot * owner_col, axis=0, keepdims=True)
    rank_u = jnp.sum(onehot * rank, axis=0, keepdims=True)
    served_u = exact_dot(served, onehot, ((0,), (0,)))
    before_u = exact_dot(before, onehot, ((0,), (0,)))
    serve_u = exact_dot(serve, onehot, ((0,), (0,)))
    equal = exact_dot(onehot, onehot, ((0,), (0,)))
    both = (users, users)
    position = jnp.sum(
        jnp.where(iota(both, 0) < iota(both, 1), equal, 0.0), axis=0, keepdims=True
    )
    return owner_u, rank_u, served_u, before_u, serve_u, position


def uplink_kernel(
    n,
    ring_of,
    guess_hbm,
    received_hbm,
    power_hbm,
    noise_hbm,
    gain_hbm,
    cluster_hbm,
    serving_hbm,
    owner_hbm,
    taps_hbm,
    table_hbm,
    coarse_hbm,
    spread_hbm,
    share_hbm,
    place_hbm,
    scale_hbm,
    packet_all,
    sample_all,
    signal_all,
    received_ref,
    power_ref,
    noise_ref,
    gain_ref,
    cluster_ref,
    serving_ref,
    owner_ref,
    guess,
    taps,
    table,
    coarse,
    spread,
    half,
    other,
    packet_send,
    sample_send,
    coef_b,
    gains,
    pick,
    pick_weight,
    power_wide,
    sampled,
    samples,
    cov,
    solved,
    smooth,
    share,
    place_ref,
    scale_ref,
    guess_sem,
    table_sem,
    half_send_sem,
    half_recv_sem,
    gain_send_sem,
    gain_recv_sem,
    packet_send_sem,
    packet_recv_sem,
    sample_send_sem,
    sample_recv_sem,
    ring_send_sem,
    ring_recv_sem,
    small_sem,
    relay_send_sem,
    relay_recv_sem,
    share_sem,
    place_sem,
):
    stations, antennas, _, users, tones = guess.shape
    pieces = stations * antennas
    block = PEER_MAX * CU
    clusters = serving_ref.shape[0]
    me = lax.axis_index("ap")
    part = lax.axis_index("sc")
    node, place = ring_of
    spot = place(me)
    right = node(lax.rem(spot + 1, n))
    left = node(lax.rem(spot + n - 1, n))

    table_copies = []
    for source, into in (
        (taps_hbm.at[part], taps),
        (coarse_hbm, coarse),
        (spread_hbm.at[part], spread),
        (table_hbm.at[part], table),
    ):
        table_copies.append(
            pltpu.make_async_copy(source, into, table_sem.at[len(table_copies)])
        )
    small_copies = []
    for source, into in (
        (cluster_hbm, cluster_ref),
        (serving_hbm, serving_ref),
        (owner_hbm, owner_ref),
        (power_hbm, power_ref),
        (gain_hbm, gain_ref),
        (noise_hbm, noise_ref),
    ):
        copy = pltpu.make_async_copy(source, into, small_sem.at[len(small_copies)])
        copy.start()
        small_copies.append(copy)
    table_copies[0].start()
    guess_copies = []
    for q in range(pieces):
        a, i = q // antennas, q % antennas
        copy = pltpu.make_async_copy(guess_hbm.at[a, i], guess.at[a, i], guess_sem.at[q])
        guess_copies.append(copy)
    for copy in guess_copies:
        copy.start()
    received_copy = pltpu.make_async_copy(received_hbm, received_ref, place_sem.at[0])
    received_copy.start()
    for copy in table_copies[1:]:
        copy.start()

    barrier = pltpu.get_barrier_semaphore()
    pl.semaphore_signal(barrier, inc=1, device_id={"sc": 1 - part}, device_id_type=MESH)
    for k in range(1, n):
        pl.semaphore_signal(
            barrier, inc=1, device_id={"ap": lax.rem(me + k, n)}, device_id_type=MESH
        )

    for copy in small_copies:
        copy.wait()
    owner_u, rank_u, served_u, before_u, serve_u, position = user_tables(
        cluster_ref[...], serving_ref[...], owner_ref[...], clusters, users, stations, n
    )
    mef = me.astype(jnp.float32)
    mine = iota((n, users), 0) == mef
    served_me = jnp.sum(jnp.where(mine, served_u, 0.0), axis=0, keepdims=True)
    before_me = jnp.sum(jnp.where(mine, before_u, 0.0), axis=0, keepdims=True)
    target = jnp.where(
        served_me > 0.5, owner_u * block + before_me * CU + position, -1.0
    )
    chosen_user = iota((n * block, users), 0) == target
    pick[...] = jnp.where(chosen_user, 1.0, 0.0).astype(jnp.bfloat16)
    for a in range(stations):
        row_here = iota((n * stations, users), 0) == mef * stations + a
        weight = jnp.sum(jnp.where(row_here, serve_u, 0.0), axis=0, keepdims=True)
        weight = weight * gain_ref[a : a + 1, :]
        column = jnp.sum(jnp.where(chosen_user, weight, 0.0), axis=1, keepdims=True)
        pick_weight[a] = jnp.broadcast_to(column, (n * block, LANES))
    wide = jnp.broadcast_to(power_ref[...] * (1.0 / users), (LANES, users))
    power_wide[...] = jnp.transpose(wide)

    ring_copies = {}
    reach = {}
    for c in range(stations):
        far, near = n // 2, n - 1 - n // 2
        reach[c] = (far, near) if c % 2 == 0 else (near, far)
    steps = max(max(r) for r in reach.values())

    def origin_of(direction, step):
        back = lax.rem(spot + n - step, n) if direction == 0 else lax.rem(spot + step, n)
        return node(back)

    def ring_step(c, step):
        for direction in range(2):
            if step > reach[c][direction]:
                continue
            origin = origin_of(direction, step)
            source = received_ref.at[c]
            if step > 0:
                ring_copies[c, direction, step - 1].wait_recv()
                source = signal_all.at[origin, c]
            if step == reach[c][direction]:
                continue
            copy = pltpu.make_async_remote_copy(
                src_ref=source,
                dst_ref=signal_all.at[origin, c],
                send_sem=ring_send_sem.at[direction, c, step],
                recv_sem=ring_recv_sem.at[direction, c, step],
                device_id={"ap": right if direction == 0 else left},
                device_id_type=MESH,
            )
            copy.start()
            ring_copies[c, direction, step] = copy

    table_copies[0].wait()
    for copy in guess_copies:
        copy.wait()
    count = pieces * users
    lower = lax.broadcasted_iota(jnp.int32, (count, 2 * TAPS), 1) < TAPS
    products = [
        jnp.dot(
            guess[:, :, reim].reshape(count, tones), taps[...], preferred_element_type=jnp.float32
        )
        for reim in range(2)
    ]
    turned = pltpu.roll(products[1], TAPS, axis=1)
    sums = products[0] + jnp.where(lower, -turned, turned)
    half[...] = (sums * (1.0 / TONE_NUMBER)).astype(jnp.bfloat16).reshape(half.shape)
    received_copy.wait()
    pl.semaphore_wait(barrier, n)
    for c in range(stations):
        ring_step(c, 0)
    half_copies = []
    for q in range(pieces):
        copy = pltpu.make_async_remote_copy(
            src_ref=half.at[q],
            dst_ref=other.at[q],
            send_sem=half_send_sem.at[q],
            recv_sem=half_recv_sem.at[q],
            device_id={"sc": 1 - part},
            device_id_type=MESH,
        )
        copy.start()
        half_copies.append(copy)
    gain_copies = []
    for k in range(1, n):
        peer = lax.rem(me + k, n)
        copy = pltpu.make_async_remote_copy(
            src_ref=gain_ref,
            dst_ref=gains.at[me],
            send_sem=gain_send_sem.at[k],
            recv_sem=gain_recv_sem.at[n - k],
            device_id={"ap": peer},
            device_id_type=MESH,
        )
        copy.start()
        gain_copies.append(copy)
    gains[me] = gain_ref[...]
    sums = []
    for q in range(pieces):
        half_copies[q].wait_recv()
        total = (half[q].astype(jnp.float32) + other[q].astype(jnp.float32)).astype(jnp.bfloat16)
        coef_b[pl.ds(q * users, users), :] = total
        sums.append(total)
    symbols = received_ref.shape[3]
    rows = stations * symbols
    entries = [(i, j) for i in range(antennas) for j in range(i + 1)]
    kinds = antennas * antennas
    for copy in table_copies[1:]:
        copy.wait()
    both = jnp.dot(coef_b[...], coarse[...], preferred_element_type=jnp.float32)
    for reim in range(2):
        sampled[reim] = both[:, reim * COARSE : (reim + 1) * COARSE]
    chosen = jnp.dot(
        pick[...], jnp.concatenate(sums, axis=1), preferred_element_type=jnp.float32
    )
    for q in range(pieces):
        values = chosen[:, q * 2 * TAPS : (q + 1) * 2 * TAPS] * pick_weight[q // antennas]
        packet_send[:, q] = values.astype(jnp.bfloat16).reshape(n, block, 2 * TAPS)
    mine_half = pl.ds(part * (pieces // 2), pieces // 2)

    def spread_out(send, recv, window, send_sem, recv_sem, each):
        copies = {}
        for step in range(1, steps + 1):
            for k in sorted({step, n - step}):
                peer = node(lax.rem(spot + k, n))
                copy = pltpu.make_async_remote_copy(
                    src_ref=send.at[peer, window] if each else send,
                    dst_ref=recv.at[me, window] if each else recv.at[me],
                    send_sem=send_sem.at[k],
                    recv_sem=recv_sem.at[k],
                    device_id={"ap": peer},
                    device_id_type=MESH,
                )
                copy.start()
                copies[k] = copy
        return copies

    packets = spread_out(
        packet_send, packet_all, mine_half, packet_send_sem, packet_recv_sem, True
    )
    for a in range(stations):

        def body(step, sums, a=a):
            sums = list(sums)
            for w in range(2):
                row = (step * 2 + w) * 8
                scale = power_wide[pl.ds(pl.multiple_of(row, 8), 8), :]
                re, im = [], []
                for i in range(antennas):
                    at = pl.multiple_of((a * antennas + i) * users + row, 8)
                    re.append(sampled[0, pl.ds(at, 8), :])
                    im.append(sampled[1, pl.ds(at, 8), :])
                at = 0
                for i in range(antennas):
                    sre, sim = re[i] * scale, im[i] * scale
                    for j in range(i + 1):
                        sums[at] = sums[at] + (sre * re[j] + sim * im[j])
                        at += 1
                        if j < i:
                            sums[at] = sums[at] + (sim * re[j] - sre * im[j])
                            at += 1
            return tuple(sums)

        zero = jnp.zeros((8, COARSE), jnp.float32)
        sums = lax.fori_loop(0, users // 16, body, (zero,) * (antennas * antennas))
        at = 0
        for i, j in entries:
            for reim in range(1 if i == j else 2):
                value = jnp.sum(sums[at], axis=0, keepdims=True)
                if i == j:
                    value = value + noise_ref[0:1, a : a + 1]
                samples[pl.ds(at * stations + a, 1), :] = value
                at += 1
    high = samples[...].astype(jnp.bfloat16)
    low = (samples[...] - high.astype(jnp.float32)).astype(jnp.bfloat16)
    sample_send[: kinds * stations] = high
    sample_send[kinds * stations :] = low
    sample_copies = spread_out(
        sample_send, sample_all, None, sample_send_sem, sample_recv_sem, False
    )

    def sample_wait(step):
        for k in sorted({step, n - step}):
            sample_copies[k].wait_recv()

    relays = {}

    def relay_start(step):
        for k in sorted({step, n - step}):
            packets[k].wait_recv()
            origin = node(lax.rem(spot + n - k, n))
            copy = pltpu.make_async_remote_copy(
                src_ref=packet_all.at[origin, mine_half],
                dst_ref=packet_all.at[origin, mine_half],
                send_sem=relay_send_sem.at[k],
                recv_sem=relay_recv_sem.at[k],
                device_id={"sc": 1 - part},
                device_id_type=MESH,
            )
            copy.start()
            relays[k] = copy

    def relay_wait(step):
        for k in sorted({step, n - step}):
            relays[k].wait_recv()

    tiles = tones // LANES
    station_of = lax.broadcasted_iota(jnp.int32, (rows, 1), 0)

    def prepare(held, signals, slot):
        high = held[: kinds * stations, :]
        low = held[kinds * stations :, :]
        cov[slot] = jnp.dot(
            jnp.concatenate([high, high], axis=1),
            spread[...],
            preferred_element_type=jnp.float32,
        ) + jnp.dot(low, spread[:COARSE, :], preferred_element_type=jnp.float32)
        width = min(tones, 4 * LANES)
        for base in range(0, tones, width):
            lanes = slice(base, base + width)

            def entry(at):
                value = jnp.broadcast_to(
                    cov[slot, at * stations : at * stations + 1, lanes], (rows, width)
                )
                for a in range(1, stations):
                    row = jnp.broadcast_to(
                        cov[slot, at * stations + a : at * stations + a + 1, lanes], (rows, width)
                    )
                    value = jnp.where(station_of < a * symbols, value, row)
                return value

            cov_re = [[None] * antennas for _ in range(antennas)]
            cov_im = [[None] * antennas for _ in range(antennas)]
            at = 0
            for i, j in entries:
                cov_re[i][j] = entry(at)
                at += 1
                if i != j:
                    cov_im[i][j] = entry(at)
                    at += 1
            right_side = []
            for i in range(antennas):
                right_side.append(
                    tuple(
                        jnp.concatenate(
                            [
                                signals[a, i, reim, :, lanes].astype(jnp.float32)
                                for a in range(stations)
                            ],
                            axis=0,
                        )
                        for reim in range(2)
                    )
                )
            answer = hermitian_solve(cov_re, cov_im, right_side)
            for i in range(antennas):
                re, im = answer[i]
                solved[slot, i, 0, :, lanes] = re
                solved[slot, i, 1, :, lanes] = im
                solved[slot, i, 2, :, lanes] = re + im

    def combine(origin, packet, slot):
        coefs = packet[...].reshape(pieces * block, 2 * TAPS)
        for l in range(tiles):
            columns = pl.ds(l * 2 * LANES, 2 * LANES)
            smooth[slot, l] = jnp.dot(coefs, table[:, columns], preferred_element_type=jnp.float32)
        here = pl.ds(pl.multiple_of(origin * block, block), block)
        for l in range(tiles):
            lanes = pl.ds(l * LANES, LANES)
            sums = [[None] * symbols for _ in range(PEER_MAX)]
            for a in range(stations):
                for i in range(antennas):
                    re, im, gap = [], [], []
                    for k in range(PEER_MAX):
                        at = (a * antennas + i) * block + k * CU
                        re.append(smooth[slot, l, pl.ds(at, CU), :LANES])
                        im.append(smooth[slot, l, pl.ds(at, CU), LANES:])
                        gap.append(re[k] - im[k])
                    for s in range(symbols):
                        row = pl.ds(a * symbols + s, 1)
                        sre = solved[slot, i, 0, row, lanes]
                        sim = solved[slot, i, 1, row, lanes]
                        ssum = solved[slot, i, 2, row, lanes]
                        for k in range(PEER_MAX):
                            new = (re[k] * sre, im[k] * sim, gap[k] * ssum)
                            old = sums[k][s]
                            if old is not None:
                                new = tuple(x + y for x, y in zip(old, new))
                            sums[k][s] = new
            for s in range(symbols):
                first = [sums[k][s][0] + sums[k][s][1] for k in range(PEER_MAX)]
                second = [
                    sums[k][s][2] - (sums[k][s][0] - sums[k][s][1]) for k in range(PEER_MAX)
                ]
                for reim, values in ((0, first), (1, second)):
                    share[s * 2 + reim, here, lanes] = jnp.concatenate(values, axis=0).astype(
                        jnp.bfloat16
                    )

    share_copies = []

    def send_share(origin):
        here = pl.ds(pl.multiple_of(origin * block, block), block)
        copy = pltpu.make_async_copy(
            share.at[:, here], share_hbm.at[:, here], share_sem.at[len(share_copies)]
        )
        copy.start()
        share_copies.append(copy)

    tasks = [(me, packet_send.at[me], sample_send, received_ref, 0)]
    for step in range(1, steps + 1):
        for direction in range(2 if step <= n - 1 - n // 2 else 1):
            origin = origin_of(direction, step)
            tasks.append(
                (origin, packet_all.at[origin], sample_all.at[origin], signal_all.at[origin], step)
            )

    ring_step(0, 1)
    prepare(*tasks[0][2:4], 0)
    combine(*tasks[0][:2], 0)
    send_share(me)
    for c in range(1, stations):
        ring_step(c, 1)
    relay_start(1)
    for copy in gain_copies:
        copy.wait_recv()
    totals = jnp.zeros((1, users), jnp.float32)
    for p in range(n):
        for a in range(stations):
            row = serve_u[p * stations + a : p * stations + a + 1] * gains[p, a : a + 1, :]
            totals = totals + row
    scale = 1.0 / (1.0 + totals)
    held = owner_u == mef
    slot_user = iota((OWN_MAX * CU, users), 0) == jnp.where(held, rank_u * CU + position, -1.0)
    slot_rows = jnp.where(slot_user, 1.0, 0.0)
    slot_scale = jnp.sum(jnp.where(slot_user, scale, 0.0), axis=1, keepdims=True)
    scale_ref[...] = jnp.broadcast_to(slot_scale, (OWN_MAX * CU, LANES))
    hits = []
    for p in range(n):
        goal = jnp.where(
            held & (served_u[p : p + 1] > 0.5), before_u[p : p + 1] * CU + position, -1.0
        )
        hits.append(jnp.where(iota((block, users), 0) == goal, 1.0, 0.0))
    placement = exact_dot(slot_rows, jnp.concatenate(hits, axis=0), ((1,), (1,)))
    place_ref[...] = placement.astype(jnp.bfloat16)
    place_copies = []
    for source, into in ((place_ref, place_hbm), (scale_ref, scale_hbm)):
        copy = pltpu.make_async_copy(source, into, place_sem.at[1 + len(place_copies)])
        copy.start()
        place_copies.append(copy)

    sample_wait(1)
    prepare(*tasks[1][2:4], 1)
    advanced = {0: 1}
    if steps > 1:
        ring_step(0, 2)
        advanced[0] = 2
    for t in range(1, len(tasks)):
        origin, packet, _, _, step = tasks[t]
        last = t + 1 == len(tasks)
        begins = tasks[t - 1][4] < step
        after = step if last else tasks[t + 1][4]
        if begins:
            relay_wait(step)
        if after > step:
            split = after == steps
            if split:
                combine(origin, packet, t % 2)
            for c in range(stations):
                if advanced.get(c, 1) < after:
                    ring_step(c, after)
                    advanced[c] = after
            sample_wait(after)
            relay_start(after)
            if not split:
                combine(origin, packet, t % 2)
        else:
            combine(origin, packet, t % 2)
        if not last:
            prepare(*tasks[t + 1][2:4], (t + 1) % 2)
        send_share(origin)
        if begins and not last and step < steps and advanced.get(0, 1) < step + 1:
            ring_step(0, step + 1)
            advanced[0] = step + 1
    for copy in share_copies + place_copies:
        copy.wait()
    for copy in relays.values():
        copy.wait_send()
    for copy in half_copies:
        copy.wait_send()
    for copy in gain_copies:
        copy.wait_send()
    for copy in list(packets.values()) + list(sample_copies.values()):
        copy.wait_send()
    for copy in ring_copies.values():
        copy.wait_send()


def place_kernel(
    place_hbm, scale_hbm, share_hbm, out_hbm, place_ref, scale_ref, share, lines, small_sem, in_sem, out_sem
):
    kinds, _, tones = share.shape
    smalls = []
    for source, into in ((place_hbm, place_ref), (scale_hbm, scale_ref)):
        copy = pltpu.make_async_copy(source, into, small_sem.at[len(smalls)])
        copy.start()
        smalls.append(copy)
    symbols, tiles = kinds // 2, tones // LANES
    arrivals = []
    for kind in range(kinds):
        copy = pltpu.make_async_copy(share_hbm.at[kind], share.at[kind], in_sem.at[kind])
        copy.start()
        arrivals.append(copy)
    for copy in smalls:
        copy.wait()
    copies = []
    for s in range(symbols):
        for reim in range(2):
            arrivals[s * 2 + reim].wait()
            placed = jnp.dot(
                place_ref[...], share[s * 2 + reim], preferred_element_type=jnp.float32
            )
            for l in range(tiles):
                for r in range(OWN_MAX):
                    rows = slice(r * CU, (r + 1) * CU)
                    value = placed[rows, l * LANES : (l + 1) * LANES] * scale_ref[rows]
                    lines[s, pl.ds(r * CU * 2 * tiles + l * 2 + reim, CU, stride=2 * tiles), :] = value
        height = 2 * tiles
        copy = pltpu.make_async_copy(
            lines.at[s].reshape(OWN_MAX * CU, height, LANES), out_hbm.at[:, s], out_sem.at[s]
        )
        copy.start()
        copies.append(copy)
    for copy in copies:
        copy.wait()


def ring_functions(mesh):
    n = mesh.shape["ap"]
    half = n // 2

    def plain(q):
        return q

    def node(q):
        upper = q // half
        return (1 - upper) * 2 * q + upper * (2 * (n - q) - 1)

    def place(d):
        odd = d % 2
        return (1 - odd) * (d // 2) + odd * (n - (d + 1) // 2)

    if n % 2:
        return plain, plain
    try:
        axes = list(mesh.axis_names)
        line = np.moveaxis(mesh.devices, axes.index("ap"), 0).reshape(n, -1)[:, 0]
        spots = [tuple(d.coords) for d in line]
        sizes = [max(s[x] for s in spots) + 1 for x in range(3)]

        def length(order):
            far = 0
            for q in range(n):
                one, two = spots[order(q)], spots[order((q + 1) % n)]
                far += sum(
                    min(abs(one[x] - two[x]), sizes[x] - abs(one[x] - two[x])) for x in range(3)
                )
            return far

        if length(plain) < length(node):
            return plain, plain
    except (AttributeError, TypeError):
        pass
    return node, place


def local(
    n,
    parts,
    ring_of,
    unsmoothed_link_guesses,
    received,
    user_power,
    noise_power,
    ap_gain,
    user_cluster,
    serving,
    cluster_owner,
):
    stations, antennas, _, users, tones = unsmoothed_link_guesses.shape
    symbols = received.shape[3]
    pieces = stations * antennas
    block = PEER_MAX * CU
    rows = stations * symbols
    held = 2 * antennas * antennas * stations
    steps = n // 2
    dma = pltpu.SemaphoreType.DMA
    bf16, f32 = jnp.bfloat16, jnp.float32
    hbm = pl.BlockSpec(memory_space=pltpu.HBM)
    tiles = tones // LANES
    slots = OWN_MAX * CU
    share, place, scale = pl.pallas_call(
        functools.partial(uplink_kernel, n, ring_of),
        out_shape=(
            jax.ShapeDtypeStruct((symbols * 2, n * block, tones), bf16),
            jax.ShapeDtypeStruct((slots, n * block), bf16),
            jax.ShapeDtypeStruct((slots, LANES), f32),
        ),
        in_specs=[hbm] * 12,
        out_specs=(hbm, hbm, hbm),
        scratch_shapes=[
            pltpu.VMEM((n, pieces, block, 2 * TAPS), bf16),
            pltpu.VMEM((n, held, COARSE), bf16),
            pltpu.VMEM((n,) + received.shape, bf16),
            pltpu.VMEM(received.shape, bf16),
            pltpu.VMEM((1, users), f32),
            pltpu.VMEM((1, stations), f32),
            pltpu.VMEM((stations, users), f32),
            pltpu.VMEM((1, users), jnp.int32),
            pltpu.VMEM(serving.shape, jnp.int32),
            pltpu.VMEM((1, serving.shape[0]), jnp.int32),
            pltpu.VMEM((stations, antennas, 2, users, tones), bf16),
            pltpu.VMEM((tones, 2 * TAPS), bf16),
            pltpu.VMEM((2 * TAPS, 2 * tones), bf16),
            pltpu.VMEM((2 * TAPS, 2 * COARSE), bf16),
            pltpu.VMEM((2 * COARSE, tones), bf16),
            pltpu.VMEM((pieces, users, 2 * TAPS), bf16),
            pltpu.VMEM((pieces, users, 2 * TAPS), bf16),
            pltpu.VMEM((n, pieces, block, 2 * TAPS), bf16),
            pltpu.VMEM((held, COARSE), bf16),
            pltpu.VMEM((pieces * users, 2 * TAPS), bf16),
            pltpu.VMEM((n, stations, users), f32),
            pltpu.VMEM((n * block, users), bf16),
            pltpu.VMEM((stations, n * block, LANES), f32),
            pltpu.VMEM((users, LANES), f32),
            pltpu.VMEM((2, pieces * users, COARSE), f32),
            pltpu.VMEM((antennas * antennas * stations, COARSE), f32),
            pltpu.VMEM((2, antennas * antennas * stations, tones), f32),
            pltpu.VMEM((2, antennas, 3, rows, tones), f32),
            pltpu.VMEM((2, tiles, pieces * block, 2 * LANES), f32),
            pltpu.VMEM((symbols * 2, n * block, tones), bf16),
            pltpu.VMEM((slots, n * block), bf16),
            pltpu.VMEM((slots, LANES), f32),
            dma((pieces,)),
            dma((4,)),
            dma((pieces,)),
            dma((pieces,)),
            dma((n,)),
            dma((n,)),
            dma((n,)),
            dma((n,)),
            dma((n,)),
            dma((n,)),
            dma((2, stations, steps)),
            dma((2, stations, steps)),
            dma((6,)),
            dma((n,)),
            dma((n,)),
            dma((n,)),
            dma((3,)),
        ],
        compiler_params=pltpu.CompilerParams(
            collective_id=0, has_side_effects=True, vmem_limit_bytes=VMEM_BYTES
        ),
        name="uplink",
    )(
        unsmoothed_link_guesses,
        received,
        user_power.reshape(1, users),
        noise_power.reshape(1, stations),
        ap_gain,
        user_cluster.reshape(1, users),
        serving,
        cluster_owner.reshape(1, -1),
        jnp.asarray(tap_tables(parts, tones)),
        jnp.asarray(tone_tables(parts, tones)),
        jnp.asarray(coarse_table()),
        jnp.asarray(spread_tables(parts, tones)),
    )
    placed = pl.pallas_call(
        place_kernel,
        out_shape=jax.ShapeDtypeStruct((slots, symbols, tiles * 2, LANES), f32),
        in_specs=[hbm, hbm, hbm],
        out_specs=hbm,
        scratch_shapes=[
            pltpu.VMEM((slots, n * block), bf16),
            pltpu.VMEM((slots, LANES), f32),
            pltpu.VMEM((symbols * 2, n * block, tones), bf16),
            pltpu.VMEM((symbols, slots * tiles * 2, LANES), f32),
            dma((2,)),
            dma((symbols * 2,)),
            dma((symbols,)),
        ],
        compiler_params=pltpu.CompilerParams(vmem_limit_bytes=VMEM_BYTES),
        name="place",
    )(place, scale, share)
    placed = placed.reshape(OWN_MAX, CU, symbols, tiles, 2, LANES)
    placed = jnp.transpose(placed, (0, 1, 2, 4, 3, 5))
    return placed.reshape(OWN_MAX, CU, symbols, 2, tones)


def solution(mesh):
    placed = (
        P(("cell", "ap"), None, None, None, "sc"),
        P(("cell", "ap"), None, None, None, "sc"),
        P("cell"),
        P(("cell", "ap")),
        P(("cell", "ap"), None),
        P("cell"),
        P("cell", None),
        P("cell", None),
    )
    return jax.shard_map(
        functools.partial(local, mesh.shape["ap"], mesh.shape["sc"], ring_functions(mesh)),
        mesh=mesh,
        in_specs=placed,
        out_specs=P(("cell", "ap"), None, None, None, "sc"),
        check_vma=False,
    )
```

```python
import functools
import math

import jax
import jax.numpy as jnp
import numpy as np
from jax import lax
from jax.experimental import pallas as pl
from jax.experimental.pallas import tpu as pltpu
from jax.sharding import PartitionSpec as P

TONE_NUMBER = 2048
TAPS = 64
CU = 8
OWN_MAX = 4
PEER_MAX = 2
COARSE = 2 * TAPS
MESH = pl.DeviceIdType.MESH
LANES = 128
VMEM_BYTES = 67043328


def complex_times(left_factor, right_factor):
    return (
        left_factor[0] * right_factor[0] - left_factor[1] * right_factor[1],
        left_factor[0] * right_factor[1] + left_factor[1] * right_factor[0],
    )


def times_conj(left_factor, right_factor):
    return (
        left_factor[0] * right_factor[0] + left_factor[1] * right_factor[1],
        left_factor[1] * right_factor[0] - left_factor[0] * right_factor[1],
    )


def hermitian_solve(cov_re, cov_im, right):
    dimension = len(cov_re)
    factor = {}
    inverses = []
    for j in range(dimension):
        pivot = cov_re[j][j]
        for k in range(j):
            element = factor[j, k]
            pivot = pivot - (element[0] * element[0] + element[1] * element[1])
        inverse = 1.0 / jnp.sqrt(pivot)
        inverses.append(inverse)
        for i in range(j + 1, dimension):
            running = (cov_re[i][j], cov_im[i][j])
            for k in range(j):
                product = times_conj(factor[i, k], factor[j, k])
                running = (running[0] - product[0], running[1] - product[1])
            factor[i, j] = (running[0] * inverse, running[1] * inverse)
    forward = []
    for i in range(dimension):
        running = right[i]
        for k in range(i):
            product = complex_times(factor[i, k], forward[k])
            running = (running[0] - product[0], running[1] - product[1])
        forward.append((running[0] * inverses[i], running[1] * inverses[i]))
    result = [None] * dimension
    for i in range(dimension - 1, -1, -1):
        running = forward[i]
        for k in range(i + 1, dimension):
            product = times_conj(result[k], factor[k, i])
            running = (running[0] - product[0], running[1] - product[1])
        result[i] = (running[0] * inverses[i], running[1] * inverses[i])
    return result


def angles_of(values):
    rotation = np.arange(TAPS, dtype=np.int32)[:, None] * values[None, :] % TONE_NUMBER
    return rotation.astype(np.float32) * np.float32(2.0 * math.pi / TONE_NUMBER)


def wave_table(values):
    cosine, sine = np.cos(angles_of(values)), np.sin(angles_of(values))
    return np.concatenate([cosine, sine], axis=0), np.concatenate([-sine, cosine], axis=0)


def tap_tables(parts, tones):
    made = []
    for part in range(parts):
        real, _ = wave_table(part * tones + np.arange(tones, dtype=np.int32))
        made.append(real.T)
    return np.stack(made).astype(jnp.bfloat16)


def tone_tables(parts, tones):
    made = []
    for part in range(parts):
        real, imag = wave_table(part * tones + np.arange(tones, dtype=np.int32))
        pair = np.stack(
            [real.reshape(2 * TAPS, -1, LANES), imag.reshape(2 * TAPS, -1, LANES)], axis=2
        )
        made.append(pair.reshape(2 * TAPS, 2 * tones))
    return np.stack(made).astype(jnp.bfloat16)


def coarse_table():
    step = TONE_NUMBER // COARSE
    real, imag = wave_table(step * np.arange(COARSE, dtype=np.int32))
    return np.concatenate([real, imag], axis=1).astype(jnp.bfloat16)


def spread_tables(parts, tones):
    step = TONE_NUMBER // COARSE
    made = []
    for part in range(parts):
        values = part * tones + np.arange(tones, dtype=np.int64)
        gap = values[None, :] - step * np.arange(COARSE, dtype=np.int64)[:, None]
        kernel = np.ones(gap.shape, np.float64)
        for d in range(1, COARSE // 2 + 1):
            share = 2.0 if d < COARSE // 2 else 1.0
            kernel += share * np.cos(2.0 * math.pi / TONE_NUMBER * (d * gap % TONE_NUMBER))
        kernel /= COARSE
        high = kernel.astype(np.float32).astype(jnp.bfloat16)
        low = (kernel - high.astype(np.float64)).astype(np.float32).astype(jnp.bfloat16)
        made.append(np.concatenate([high, low], axis=0))
    return np.stack(made)


def exact_dot(left, right, dims):
    return lax.dot_general(
        left.astype(jnp.bfloat16),
        right.astype(jnp.bfloat16),
        (dims, ((), ())),
        preferred_element_type=jnp.float32,
    )


def iota(shape, dim):
    return lax.broadcasted_iota(jnp.int32, shape, dim).astype(jnp.float32)


def user_tables(user_cluster, serving, owner, clusters, users, group, n):
    onehot = (iota((clusters, users), 0) == user_cluster.astype(jnp.float32)).astype(jnp.float32)
    owner_row = owner.astype(jnp.float32)
    square = (clusters, clusters)
    rows, cols = iota(square, 0), iota(square, 1)
    owner_col = jnp.sum(jnp.where(rows == cols, owner_row, 0.0), axis=1, keepdims=True)
    same = owner_col == owner_row
    earlier = jnp.where(same & (cols < rows), 1.0, 0.0)
    serve = serving.astype(jnp.float32)
    pair = jnp.where(
        jnp.floor((iota((group * n, n), 0) + 0.5) * (1.0 / group)) == iota((group * n, n), 1),
        1.0,
        0.0,
    )
    served = jnp.where(exact_dot(serve, pair, ((1,), (0,))) > 0.5, 1.0, 0.0)
    before = exact_dot(earlier, served, ((1,), (0,)))
    rank = jnp.sum(earlier, axis=1, keepdims=True)
    owner_u = jnp.sum(onehot * owner_col, axis=0, keepdims=True)
    rank_u = jnp.sum(onehot * rank, axis=0, keepdims=True)
    served_u = exact_dot(served, onehot, ((0,), (0,)))
    before_u = exact_dot(before, onehot, ((0,), (0,)))
    serve_u = exact_dot(serve, onehot, ((0,), (0,)))
    equal = exact_dot(onehot, onehot, ((0,), (0,)))
    both = (users, users)
    position = jnp.sum(
        jnp.where(iota(both, 0) < iota(both, 1), equal, 0.0), axis=0, keepdims=True
    )
    return owner_u, rank_u, served_u, before_u, serve_u, position


def uplink_kernel(
    n,
    ring_of,
    guess_hbm,
    received_hbm,
    power_hbm,
    noise_hbm,
    gain_hbm,
    cluster_hbm,
    serving_hbm,
    owner_hbm,
    taps_hbm,
    table_hbm,
    coarse_hbm,
    spread_hbm,
    share_hbm,
    place_hbm,
    scale_hbm,
    packet_all,
    signal_all,
    received_ref,
    power_ref,
    noise_ref,
    gain_ref,
    cluster_ref,
    serving_ref,
    owner_ref,
    guess,
    taps,
    table,
    coarse,
    spread,
    half,
    other,
    packet_send,
    coef_b,
    gains,
    pick,
    pick_weight,
    power_wide,
    sampled,
    samples,
    cov,
    solved,
    smooth,
    share,
    place_ref,
    scale_ref,
    guess_sem,
    table_sem,
    half_send_sem,
    half_recv_sem,
    gain_send_sem,
    gain_recv_sem,
    packet_send_sem,
    packet_recv_sem,
    ring_send_sem,
    ring_recv_sem,
    small_sem,
    relay_send_sem,
    relay_recv_sem,
    share_sem,
    place_sem,
    present,
):
    stations, antennas, _, users, tones = guess.shape
    pieces = stations * antennas
    block = PEER_MAX * CU
    clusters = serving_ref.shape[0]
    me = lax.axis_index("ap")
    part = lax.axis_index("sc")
    node, place = ring_of
    spot = place(me)
    right = node(lax.rem(spot + 1, n))
    left = node(lax.rem(spot + n - 1, n))

    table_copies = []
    for source, into in (
        (taps_hbm.at[part], taps),
        (coarse_hbm, coarse),
        (spread_hbm.at[part], spread),
        (table_hbm.at[part], table),
    ):
        table_copies.append(
            pltpu.make_async_copy(source, into, table_sem.at[len(table_copies)])
        )
    received_copy = pltpu.make_async_copy(received_hbm, received_ref, place_sem.at[0])
    received_copy.start()
    small_copies = []
    for source, into in (
        (cluster_hbm, cluster_ref),
        (serving_hbm, serving_ref),
        (owner_hbm, owner_ref),
        (power_hbm, power_ref),
        (gain_hbm, gain_ref),
        (noise_hbm, noise_ref),
    ):
        copy = pltpu.make_async_copy(source, into, small_sem.at[len(small_copies)])
        copy.start()
        small_copies.append(copy)
    guess_copies = []
    for q in range(pieces):
        a, i = q // antennas, q % antennas
        copy = pltpu.make_async_copy(guess_hbm.at[a, i], guess.at[a, i], guess_sem.at[q])
        guess_copies.append(copy)

    barrier = pltpu.get_barrier_semaphore()
    pl.semaphore_signal(barrier, inc=1, device_id={"sc": 1 - part}, device_id_type=MESH)
    for peer in (left, right):
        pl.semaphore_signal(barrier, inc=1, device_id={"ap": peer}, device_id_type=MESH)
    table_copies[0].start()
    for copy in guess_copies:
        copy.start()
    for copy in table_copies[1:]:
        copy.start()
    ring_copies = {}
    reach = {}
    for c in range(stations):
        far, near = n // 2, n - 1 - n // 2
        reach[c] = (far, near) if c % 2 == 0 else (near, far)
    steps = max(max(r) for r in reach.values())

    def origin_of(direction, step):
        back = lax.rem(spot + n - step, n) if direction == 0 else lax.rem(spot + step, n)
        return node(back)

    def ring_step(c, step):
        for direction in range(2):
            if step > reach[c][direction]:
                continue
            origin = origin_of(direction, step)
            source = received_ref.at[c]
            if step > 0:
                ring_copies[c, direction, step - 1].wait_recv()
                source = signal_all.at[origin, c]
            if step == reach[c][direction]:
                continue
            copy = pltpu.make_async_remote_copy(
                src_ref=source,
                dst_ref=signal_all.at[origin, c],
                send_sem=ring_send_sem.at[direction, c, step],
                recv_sem=ring_recv_sem.at[direction, c, step],
                device_id={"ap": right if direction == 0 else left},
                device_id_type=MESH,
            )
            copy.start()
            ring_copies[c, direction, step] = copy

    received_copy.wait()
    for copy in small_copies:
        copy.wait()

    def present_send(level):
        if level < steps:
            for side, peer in ((0, right), (1, left)):
                pl.semaphore_signal(
                    present.at[side, level], inc=1, device_id={"ap": peer}, device_id_type=MESH
                )

    def present_wait(level):
        if level < steps:
            for side in range(2):
                pl.semaphore_wait(present.at[side, level], 1)
            present_send(level + 1)

    pl.semaphore_wait(barrier, 3)
    present_send(1)
    for c in range(stations):
        ring_step(c, 0)
    owner_u, rank_u, served_u, before_u, serve_u, position = user_tables(
        cluster_ref[...], serving_ref[...], owner_ref[...], clusters, users, stations, n
    )
    mef = me.astype(jnp.float32)
    mine = iota((n, users), 0) == mef
    served_me = jnp.sum(jnp.where(mine, served_u, 0.0), axis=0, keepdims=True)
    before_me = jnp.sum(jnp.where(mine, before_u, 0.0), axis=0, keepdims=True)
    target = jnp.where(
        served_me > 0.5, owner_u * block + before_me * CU + position, -1.0
    )
    chosen_user = iota((n * block, users), 0) == target
    pick[...] = jnp.where(chosen_user, 1.0, 0.0).astype(jnp.bfloat16)
    for a in range(stations):
        row_here = iota((n * stations, users), 0) == mef * stations + a
        weight = jnp.sum(jnp.where(row_here, serve_u, 0.0), axis=0, keepdims=True)
        weight = weight * gain_ref[a : a + 1, :]
        column = jnp.sum(jnp.where(chosen_user, weight, 0.0), axis=1, keepdims=True)
        pick_weight[a] = jnp.broadcast_to(column, (n * block, LANES))
    wide = jnp.broadcast_to(power_ref[...] * (1.0 / users), (LANES, users))
    power_wide[...] = jnp.transpose(wide)

    present_wait(1)
    table_copies[0].wait()
    for copy in guess_copies:
        copy.wait()
    count = pieces * users
    lower = lax.broadcasted_iota(jnp.int32, (count, 2 * TAPS), 1) < TAPS
    products = [
        jnp.dot(
            guess[:, :, reim].reshape(count, tones), taps[...], preferred_element_type=jnp.float32
        )
        for reim in range(2)
    ]
    turned = pltpu.roll(products[1], TAPS, axis=1)
    sums = products[0] + jnp.where(lower, -turned, turned)
    half[...] = (sums * (1.0 / TONE_NUMBER)).astype(jnp.bfloat16).reshape(half.shape)
    present_wait(2)
    half_copies = []
    for q in range(pieces):
        copy = pltpu.make_async_remote_copy(
            src_ref=half.at[q],
            dst_ref=other.at[q],
            send_sem=half_send_sem.at[q],
            recv_sem=half_recv_sem.at[q],
            device_id={"sc": 1 - part},
            device_id_type=MESH,
        )
        copy.start()
        half_copies.append(copy)
    sums = []
    for q in range(pieces):
        half_copies[q].wait_recv()
        total = (half[q].astype(jnp.float32) + other[q].astype(jnp.float32)).astype(jnp.bfloat16)
        coef_b[pl.ds(q * users, users), :] = total
        sums.append(total)
    symbols = received_ref.shape[3]
    rows = stations * symbols
    entries = [(i, j) for i in range(antennas) for j in range(i + 1)]
    kinds = antennas * antennas
    ring_step(0, 1)
    for copy in table_copies[1:]:
        copy.wait()
    both = jnp.dot(coef_b[...], coarse[...], preferred_element_type=jnp.float32)
    for reim in range(2):
        sampled[reim] = both[:, reim * COARSE : (reim + 1) * COARSE]
    chosen = jnp.dot(
        pick[...], jnp.concatenate(sums, axis=1), preferred_element_type=jnp.float32
    )
    for q in range(pieces):
        values = chosen[:, q * 2 * TAPS : (q + 1) * 2 * TAPS] * pick_weight[q // antennas]
        packet_send[:, q] = values.astype(jnp.bfloat16).reshape(n, block, 2 * TAPS)
    for c in range(1, stations):
        ring_step(c, 1)
    for a in range(stations):

        def body(step, sums, a=a):
            sums = list(sums)
            for w in range(2):
                row = (step * 2 + w) * 8
                scale = power_wide[pl.ds(pl.multiple_of(row, 8), 8), :]
                re, im = [], []
                for i in range(antennas):
                    at = pl.multiple_of((a * antennas + i) * users + row, 8)
                    re.append(sampled[0, pl.ds(at, 8), :])
                    im.append(sampled[1, pl.ds(at, 8), :])
                at = 0
                for i in range(antennas):
                    sre, sim = re[i] * scale, im[i] * scale
                    for j in range(i + 1):
                        sums[at] = sums[at] + (sre * re[j] + sim * im[j])
                        at += 1
                        if j < i:
                            sums[at] = sums[at] + (sim * re[j] - sre * im[j])
                            at += 1
            return tuple(sums)

        zero = jnp.zeros((8, COARSE), jnp.float32)
        sums = lax.fori_loop(0, users // 16, body, (zero,) * (antennas * antennas))
        at = 0
        for i, j in entries:
            for reim in range(1 if i == j else 2):
                value = jnp.sum(sums[at], axis=0, keepdims=True)
                if i == j:
                    value = value + noise_ref[0:1, a : a + 1]
                samples[pl.ds(at * stations + a, 1), :] = value
                at += 1
    high = samples[...].astype(jnp.bfloat16)
    low = (samples[...] - high.astype(jnp.float32)).astype(jnp.bfloat16)
    held_rows = kinds * stations // block
    for k in range(n):
        packet_send[k, pieces : pieces + held_rows] = high.reshape(held_rows, block, COARSE)
        packet_send[k, pieces + held_rows :] = low.reshape(held_rows, block, COARSE)
    parcels = packet_send.shape[1]
    mine_half = pl.ds(part * (parcels // 2), parcels // 2)
    packets = {}

    def packet_start(step):
        window = mine_half
        for k in sorted({step, n - step}):
            peer = node(lax.rem(spot + k, n))
            copy = pltpu.make_async_remote_copy(
                src_ref=packet_send.at[peer, window],
                dst_ref=packet_all.at[me, window],
                send_sem=packet_send_sem.at[k],
                recv_sem=packet_recv_sem.at[k],
                device_id={"ap": peer},
                device_id_type=MESH,
            )
            copy.start()
            packets[k] = copy

    for level in range(3, steps):
        present_wait(level)
    for step in range(1, steps + 1):
        packet_start(step)
    gain_copies = []
    for k in range(1, n):
        peer = lax.rem(me + k, n)
        copy = pltpu.make_async_remote_copy(
            src_ref=gain_ref,
            dst_ref=gains.at[me],
            send_sem=gain_send_sem.at[k],
            recv_sem=gain_recv_sem.at[n - k],
            device_id={"ap": peer},
            device_id_type=MESH,
        )
        copy.start()
        gain_copies.append(copy)
    gains[me] = gain_ref[...]
    relays = {}

    def relay_start(step):
        for k in sorted({step, n - step}):
            packets[k].wait_recv()
            origin = node(lax.rem(spot + n - k, n))
            copy = pltpu.make_async_remote_copy(
                src_ref=packet_all.at[origin, mine_half],
                dst_ref=packet_all.at[origin, mine_half],
                send_sem=relay_send_sem.at[k],
                recv_sem=relay_recv_sem.at[k],
                device_id={"sc": 1 - part},
                device_id_type=MESH,
            )
            copy.start()
            relays[k] = copy

    def relay_wait(step):
        for k in sorted({step, n - step}):
            relays[k].wait_recv()

    tiles = tones // LANES
    station_of = lax.broadcasted_iota(jnp.int32, (rows, 1), 0)

    def prepare(packet, signals, slot):
        high = packet[pieces : pieces + held_rows].reshape(kinds * stations, COARSE)
        low = packet[pieces + held_rows :].reshape(kinds * stations, COARSE)
        cov[slot] = jnp.dot(
            jnp.concatenate([high, high], axis=1),
            spread[...],
            preferred_element_type=jnp.float32,
        ) + jnp.dot(low, spread[:COARSE, :], preferred_element_type=jnp.float32)
        width = min(tones, 4 * LANES)
        for base in range(0, tones, width):
            lanes = slice(base, base + width)

            def entry(at):
                value = jnp.broadcast_to(
                    cov[slot, at * stations : at * stations + 1, lanes], (rows, width)
                )
                for a in range(1, stations):
                    row = jnp.broadcast_to(
                        cov[slot, at * stations + a : at * stations + a + 1, lanes], (rows, width)
                    )
                    value = jnp.where(station_of < a * symbols, value, row)
                return value

            cov_re = [[None] * antennas for _ in range(antennas)]
            cov_im = [[None] * antennas for _ in range(antennas)]
            at = 0
            for i, j in entries:
                cov_re[i][j] = entry(at)
                at += 1
                if i != j:
                    cov_im[i][j] = entry(at)
                    at += 1
            right_side = []
            for i in range(antennas):
                right_side.append(
                    tuple(
                        jnp.concatenate(
                            [
                                signals[a, i, reim, :, lanes].astype(jnp.float32)
                                for a in range(stations)
                            ],
                            axis=0,
                        )
                        for reim in range(2)
                    )
                )
            answer = hermitian_solve(cov_re, cov_im, right_side)
            for i in range(antennas):
                re, im = answer[i]
                solved[slot, i, 0, :, lanes] = re
                solved[slot, i, 1, :, lanes] = im
                solved[slot, i, 2, :, lanes] = re + im

    def combine(origin, packet, slot):
        coefs = packet[:pieces].reshape(pieces * block, 2 * TAPS)
        for l in range(tiles):
            columns = pl.ds(l * 2 * LANES, 2 * LANES)
            smooth[slot, l] = jnp.dot(coefs, table[:, columns], preferred_element_type=jnp.float32)
        here = pl.ds(pl.multiple_of(origin * block, block), block)
        for l in range(tiles):
            lanes = pl.ds(l * LANES, LANES)
            sums = [[None] * symbols for _ in range(PEER_MAX)]
            for a in range(stations):
                for i in range(antennas):
                    re, im, gap = [], [], []
                    for k in range(PEER_MAX):
                        at = (a * antennas + i) * block + k * CU
                        re.append(smooth[slot, l, pl.ds(at, CU), :LANES])
                        im.append(smooth[slot, l, pl.ds(at, CU), LANES:])
                        gap.append(re[k] - im[k])
                    for s in range(symbols):
                        row = pl.ds(a * symbols + s, 1)
                        sre = solved[slot, i, 0, row, lanes]
                        sim = solved[slot, i, 1, row, lanes]
                        ssum = solved[slot, i, 2, row, lanes]
                        for k in range(PEER_MAX):
                            new = (re[k] * sre, im[k] * sim, gap[k] * ssum)
                            old = sums[k][s]
                            if old is not None:
                                new = tuple(x + y for x, y in zip(old, new))
                            sums[k][s] = new
            for s in range(symbols):
                first = [sums[k][s][0] + sums[k][s][1] for k in range(PEER_MAX)]
                second = [
                    sums[k][s][2] - (sums[k][s][0] - sums[k][s][1]) for k in range(PEER_MAX)
                ]
                for reim, values in ((0, first), (1, second)):
                    share[s * 2 + reim, here, lanes] = jnp.concatenate(values, axis=0).astype(
                        jnp.bfloat16
                    )

    share_copies = []

    def send_share(origin):
        here = pl.ds(pl.multiple_of(origin * block, block), block)
        copy = pltpu.make_async_copy(
            share.at[:, here], share_hbm.at[:, here], share_sem.at[len(share_copies)]
        )
        copy.start()
        share_copies.append(copy)

    tasks = [(me, packet_send.at[me], received_ref, 0)]
    for step in range(1, steps + 1):
        for direction in range(2 if step <= n - 1 - n // 2 else 1):
            origin = origin_of(direction, step)
            tasks.append((origin, packet_all.at[origin], signal_all.at[origin], step))

    prepare(*tasks[0][1:3], 0)
    combine(*tasks[0][:2], 0)
    send_share(me)
    if steps > 1:
        ring_step(0, 2)
    relay_start(1)
    relay_wait(1)
    prepare(*tasks[1][1:3], 1)
    advanced = {(c, 1) for c in range(stations)} | {(0, 2)}

    def advance(c, step):
        if step <= steps and (c, step) not in advanced:
            ring_step(c, step)
            advanced.add((c, step))

    for c in range(1, stations):
        advance(c, 2)
    for t in range(1, len(tasks)):
        origin, packet, _, step = tasks[t]
        last = t + 1 == len(tasks)
        after = step if last else tasks[t + 1][3]
        begins = tasks[t - 1][3] < step
        combine(origin, packet, t % 2)
        if not last:
            if after > step:
                for c in range(stations):
                    advance(c, after)
                relay_wait(after)
            prepare(*tasks[t + 1][1:3], (t + 1) % 2)
        send_share(origin)
        if begins and step < steps:
            advance(0, step + 1)
            if step == 1:
                for c in range(1, stations):
                    advance(c, 2)
            relay_start(step + 1)
        if t == len(tasks) - 3:
            for copy in gain_copies:
                copy.wait_recv()
            totals = jnp.zeros((1, users), jnp.float32)
            for p in range(n):
                for a in range(stations):
                    row = serve_u[p * stations + a : p * stations + a + 1] * gains[p, a : a + 1, :]
                    totals = totals + row
            scale = 1.0 / (1.0 + totals)
            held = owner_u == mef
            slot_user = iota((OWN_MAX * CU, users), 0) == jnp.where(held, rank_u * CU + position, -1.0)
            slot_rows = jnp.where(slot_user, 1.0, 0.0)
            slot_scale = jnp.sum(jnp.where(slot_user, scale, 0.0), axis=1, keepdims=True)
            scale_ref[...] = jnp.broadcast_to(slot_scale, (OWN_MAX * CU, LANES))
            hits = []
            for p in range(n):
                goal = jnp.where(
                    held & (served_u[p : p + 1] > 0.5), before_u[p : p + 1] * CU + position, -1.0
                )
                hits.append(jnp.where(iota((block, users), 0) == goal, 1.0, 0.0))
            placement = exact_dot(slot_rows, jnp.concatenate(hits, axis=0), ((1,), (1,)))
            place_ref[...] = placement.astype(jnp.bfloat16)
            place_copies = []
            for source, into in ((place_ref, place_hbm), (scale_ref, scale_hbm)):
                copy = pltpu.make_async_copy(source, into, place_sem.at[1 + len(place_copies)])
                copy.start()
                place_copies.append(copy)

    for copy in share_copies + place_copies:
        copy.wait()
    for copy in relays.values():
        copy.wait_send()
    for copy in half_copies:
        copy.wait_send()
    for copy in gain_copies:
        copy.wait_send()
    for copy in packets.values():
        copy.wait_send()
    for copy in ring_copies.values():
        copy.wait_send()


def place_kernel(
    place_hbm, scale_hbm, share_hbm, out_hbm, place_ref, scale_ref, share, lines, small_sem, in_sem, out_sem
):
    kinds, _, tones = share.shape
    symbols, tiles = kinds // 2, tones // LANES
    arrivals = []
    for kind in range(kinds):
        arrivals.append(
            pltpu.make_async_copy(share_hbm.at[kind], share.at[kind], in_sem.at[kind])
        )
    smalls = []
    for source, into in ((place_hbm, place_ref), (scale_hbm, scale_ref)):
        copy = pltpu.make_async_copy(source, into, small_sem.at[len(smalls)])
        copy.start()
        smalls.append(copy)
    for copy in arrivals:
        copy.start()
    for copy in smalls:
        copy.wait()
    copies = []
    for s in range(symbols):
        placed = []
        for reim in range(2):
            arrivals[s * 2 + reim].wait()
            placed.append(
                jnp.dot(place_ref[...], share[s * 2 + reim], preferred_element_type=jnp.float32)
            )
        for r in range(OWN_MAX):
            rows = slice(r * CU, (r + 1) * CU)
            scale = scale_ref[rows]
            parts = [
                placed[reim][rows, l * LANES : (l + 1) * LANES] * scale
                for l in range(tiles)
                for reim in range(2)
            ]
            for first in range(0, 2 * tiles, CU):
                square = jnp.stack(parts[first : first + CU], axis=0)
                lines[s, rows, first : first + CU, :] = jnp.transpose(square, (1, 0, 2))
        copy = pltpu.make_async_copy(lines.at[s], out_hbm.at[:, s], out_sem.at[s])
        copy.start()
        copies.append(copy)
    for copy in copies:
        copy.wait()


def ring_functions(mesh):
    n = mesh.shape["ap"]
    half = n // 2

    def plain(q):
        return q

    def node(q):
        upper = q // half
        return (1 - upper) * 2 * q + upper * (2 * (n - q) - 1)

    def place(d):
        odd = d % 2
        return (1 - odd) * (d // 2) + odd * (n - (d + 1) // 2)

    if n % 2:
        return plain, plain
    try:
        axes = list(mesh.axis_names)
        line = np.moveaxis(mesh.devices, axes.index("ap"), 0).reshape(n, -1)[:, 0]
        spots = [tuple(d.coords) for d in line]
        sizes = [max(s[x] for s in spots) + 1 for x in range(3)]

        def length(order):
            far = 0
            for q in range(n):
                one, two = spots[order(q)], spots[order((q + 1) % n)]
                far += sum(
                    min(abs(one[x] - two[x]), sizes[x] - abs(one[x] - two[x])) for x in range(3)
                )
            return far

        if length(plain) < length(node):
            return plain, plain
    except (AttributeError, TypeError):
        pass
    return node, place


def local(
    n,
    parts,
    ring_of,
    unsmoothed_link_guesses,
    received,
    user_power,
    noise_power,
    ap_gain,
    user_cluster,
    serving,
    cluster_owner,
):
    stations, antennas, _, users, tones = unsmoothed_link_guesses.shape
    symbols = received.shape[3]
    pieces = stations * antennas
    block = PEER_MAX * CU
    rows = stations * symbols
    parcels = pieces + 2 * (antennas * antennas * stations // block)
    steps = n // 2
    dma = pltpu.SemaphoreType.DMA
    bf16, f32 = jnp.bfloat16, jnp.float32
    hbm = pl.BlockSpec(memory_space=pltpu.HBM)
    tiles = tones // LANES
    slots = OWN_MAX * CU
    share, place, scale = pl.pallas_call(
        functools.partial(uplink_kernel, n, ring_of),
        out_shape=(
            jax.ShapeDtypeStruct((symbols * 2, n * block, tones), bf16),
            jax.ShapeDtypeStruct((slots, n * block), bf16),
            jax.ShapeDtypeStruct((slots, LANES), f32),
        ),
        in_specs=[hbm] * 12,
        out_specs=(hbm, hbm, hbm),
        scratch_shapes=[
            pltpu.VMEM((n, parcels, block, 2 * TAPS), bf16),
            pltpu.VMEM((n,) + received.shape, bf16),
            pltpu.VMEM(received.shape, bf16),
            pltpu.VMEM((1, users), f32),
            pltpu.VMEM((1, stations), f32),
            pltpu.VMEM((stations, users), f32),
            pltpu.VMEM((1, users), jnp.int32),
            pltpu.VMEM(serving.shape, jnp.int32),
            pltpu.VMEM((1, serving.shape[0]), jnp.int32),
            pltpu.VMEM((stations, antennas, 2, users, tones), bf16),
            pltpu.VMEM((tones, 2 * TAPS), bf16),
            pltpu.VMEM((2 * TAPS, 2 * tones), bf16),
            pltpu.VMEM((2 * TAPS, 2 * COARSE), bf16),
            pltpu.VMEM((2 * COARSE, tones), bf16),
            pltpu.VMEM((pieces, users, 2 * TAPS), bf16),
            pltpu.VMEM((pieces, users, 2 * TAPS), bf16),
            pltpu.VMEM((n, parcels, block, 2 * TAPS), bf16),
            pltpu.VMEM((pieces * users, 2 * TAPS), bf16),
            pltpu.VMEM((n, stations, users), f32),
            pltpu.VMEM((n * block, users), bf16),
            pltpu.VMEM((stations, n * block, LANES), f32),
            pltpu.VMEM((users, LANES), f32),
            pltpu.VMEM((2, pieces * users, COARSE), f32),
            pltpu.VMEM((antennas * antennas * stations, COARSE), f32),
            pltpu.VMEM((2, antennas * antennas * stations, tones), f32),
            pltpu.VMEM((2, antennas, 3, rows, tones), f32),
            pltpu.VMEM((2, tiles, pieces * block, 2 * LANES), f32),
            pltpu.VMEM((symbols * 2, n * block, tones), bf16),
            pltpu.VMEM((slots, n * block), bf16),
            pltpu.VMEM((slots, LANES), f32),
            dma((pieces,)),
            dma((4,)),
            dma((pieces,)),
            dma((pieces,)),
            dma((n,)),
            dma((n,)),
            dma((n,)),
            dma((n,)),
            dma((2, stations, steps)),
            dma((2, stations, steps)),
            dma((6,)),
            dma((n,)),
            dma((n,)),
            dma((n,)),
            dma((3,)),
            pltpu.SemaphoreType.REGULAR((2, steps)),
        ],
        compiler_params=pltpu.CompilerParams(
            collective_id=0, has_side_effects=True, vmem_limit_bytes=VMEM_BYTES
        ),
        name="uplink",
    )(
        unsmoothed_link_guesses,
        received,
        user_power.reshape(1, users),
        noise_power.reshape(1, stations),
        ap_gain,
        user_cluster.reshape(1, users),
        serving,
        cluster_owner.reshape(1, -1),
        jnp.asarray(tap_tables(parts, tones)),
        jnp.asarray(tone_tables(parts, tones)),
        jnp.asarray(coarse_table()),
        jnp.asarray(spread_tables(parts, tones)),
    )
    placed = pl.pallas_call(
        place_kernel,
        out_shape=jax.ShapeDtypeStruct((slots, symbols, tiles * 2, LANES), f32),
        in_specs=[hbm, hbm, hbm],
        out_specs=hbm,
        scratch_shapes=[
            pltpu.VMEM((slots, n * block), bf16),
            pltpu.VMEM((slots, LANES), f32),
            pltpu.VMEM((symbols * 2, n * block, tones), bf16),
            pltpu.VMEM((symbols, slots, tiles * 2, LANES), f32),
            dma((2,)),
            dma((symbols * 2,)),
            dma((symbols,)),
        ],
        compiler_params=pltpu.CompilerParams(vmem_limit_bytes=VMEM_BYTES),
        name="place",
    )(place, scale, share)
    placed = placed.reshape(OWN_MAX, CU, symbols, tiles, 2, LANES)
    placed = jnp.transpose(placed, (0, 1, 2, 4, 3, 5))
    return placed.reshape(OWN_MAX, CU, symbols, 2, tones)


def solution(mesh):
    placed = (
        P(("cell", "ap"), None, None, None, "sc"),
        P(("cell", "ap"), None, None, None, "sc"),
        P("cell"),
        P(("cell", "ap")),
        P(("cell", "ap"), None),
        P("cell"),
        P("cell", None),
        P("cell", None),
    )
    return jax.shard_map(
        functools.partial(local, mesh.shape["ap"], mesh.shape["sc"], ring_functions(mesh)),
        mesh=mesh,
        in_specs=placed,
        out_specs=P(("cell", "ap"), None, None, None, "sc"),
        check_vma=False,
    )
```

```python
import functools
import math

import jax
import jax.numpy as jnp
import numpy as np
from jax import lax
from jax.experimental import pallas as pl
from jax.experimental.pallas import tpu as pltpu
from jax.sharding import PartitionSpec as P

TONE_NUMBER = 2048
TAPS = 64
CU = 8
OWN_MAX = 4
PEER_MAX = 2
COARSE = 2 * TAPS
MESH = pl.DeviceIdType.MESH
LANES = 128
VMEM_BYTES = 67043328


def complex_times(left_factor, right_factor):
    return (
        left_factor[0] * right_factor[0] - left_factor[1] * right_factor[1],
        left_factor[0] * right_factor[1] + left_factor[1] * right_factor[0],
    )


def times_conj(left_factor, right_factor):
    return (
        left_factor[0] * right_factor[0] + left_factor[1] * right_factor[1],
        left_factor[1] * right_factor[0] - left_factor[0] * right_factor[1],
    )


def hermitian_solve(cov_re, cov_im, right):
    dimension = len(cov_re)
    factor = {}
    inverses = []
    for j in range(dimension):
        pivot = cov_re[j][j]
        for k in range(j):
            element = factor[j, k]
            pivot = pivot - (element[0] * element[0] + element[1] * element[1])
        inverse = 1.0 / jnp.sqrt(pivot)
        inverses.append(inverse)
        for i in range(j + 1, dimension):
            running = (cov_re[i][j], cov_im[i][j])
            for k in range(j):
                product = times_conj(factor[i, k], factor[j, k])
                running = (running[0] - product[0], running[1] - product[1])
            factor[i, j] = (running[0] * inverse, running[1] * inverse)
    forward = []
    for i in range(dimension):
        running = right[i]
        for k in range(i):
            product = complex_times(factor[i, k], forward[k])
            running = (running[0] - product[0], running[1] - product[1])
        forward.append((running[0] * inverses[i], running[1] * inverses[i]))
    result = [None] * dimension
    for i in range(dimension - 1, -1, -1):
        running = forward[i]
        for k in range(i + 1, dimension):
            product = times_conj(result[k], factor[k, i])
            running = (running[0] - product[0], running[1] - product[1])
        result[i] = (running[0] * inverses[i], running[1] * inverses[i])
    return result


def angles_of(values):
    rotation = np.arange(TAPS, dtype=np.int32)[:, None] * values[None, :] % TONE_NUMBER
    return rotation.astype(np.float32) * np.float32(2.0 * math.pi / TONE_NUMBER)


def wave_table(values):
    cosine, sine = np.cos(angles_of(values)), np.sin(angles_of(values))
    return np.concatenate([cosine, sine], axis=0), np.concatenate([-sine, cosine], axis=0)


def tap_tables(parts, tones):
    made = []
    for part in range(parts):
        real, _ = wave_table(part * tones + np.arange(tones, dtype=np.int32))
        made.append(real.T)
    return np.stack(made).astype(jnp.bfloat16)


def tone_tables(parts, tones):
    made = []
    for part in range(parts):
        real, imag = wave_table(part * tones + np.arange(tones, dtype=np.int32))
        pair = np.stack(
            [real.reshape(2 * TAPS, -1, LANES), imag.reshape(2 * TAPS, -1, LANES)], axis=2
        )
        made.append(pair.reshape(2 * TAPS, 2 * tones))
    return np.stack(made).astype(jnp.bfloat16)


def coarse_table():
    step = TONE_NUMBER // COARSE
    real, imag = wave_table(step * np.arange(COARSE, dtype=np.int32))
    return np.concatenate([real, imag], axis=1).astype(jnp.bfloat16)


def spread_tables(parts, tones):
    step = TONE_NUMBER // COARSE
    made = []
    for part in range(parts):
        values = part * tones + np.arange(tones, dtype=np.int64)
        gap = values[None, :] - step * np.arange(COARSE, dtype=np.int64)[:, None]
        kernel = np.ones(gap.shape, np.float64)
        for d in range(1, COARSE // 2 + 1):
            share = 2.0 if d < COARSE // 2 else 1.0
            kernel += share * np.cos(2.0 * math.pi / TONE_NUMBER * (d * gap % TONE_NUMBER))
        kernel /= COARSE
        high = kernel.astype(np.float32).astype(jnp.bfloat16)
        low = (kernel - high.astype(np.float64)).astype(np.float32).astype(jnp.bfloat16)
        made.append(np.concatenate([high, low], axis=0))
    return np.stack(made)


def exact_dot(left, right, dims):
    return lax.dot_general(
        left.astype(jnp.bfloat16),
        right.astype(jnp.bfloat16),
        (dims, ((), ())),
        preferred_element_type=jnp.float32,
    )


def iota(shape, dim):
    return lax.broadcasted_iota(jnp.int32, shape, dim).astype(jnp.float32)


def user_tables(user_cluster, serving, owner, clusters, users, group, n):
    onehot = (iota((clusters, users), 0) == user_cluster.astype(jnp.float32)).astype(jnp.float32)
    owner_row = owner.astype(jnp.float32)
    square = (clusters, clusters)
    rows, cols = iota(square, 0), iota(square, 1)
    owner_col = jnp.sum(jnp.where(rows == cols, owner_row, 0.0), axis=1, keepdims=True)
    same = owner_col == owner_row
    earlier = jnp.where(same & (cols < rows), 1.0, 0.0)
    serve = serving.astype(jnp.float32)
    pair = jnp.where(
        jnp.floor((iota((group * n, n), 0) + 0.5) * (1.0 / group)) == iota((group * n, n), 1),
        1.0,
        0.0,
    )
    served = jnp.where(exact_dot(serve, pair, ((1,), (0,))) > 0.5, 1.0, 0.0)
    before = exact_dot(earlier, served, ((1,), (0,)))
    rank = jnp.sum(earlier, axis=1, keepdims=True)
    owner_u = jnp.sum(onehot * owner_col, axis=0, keepdims=True)
    rank_u = jnp.sum(onehot * rank, axis=0, keepdims=True)
    served_u = exact_dot(served, onehot, ((0,), (0,)))
    before_u = exact_dot(before, onehot, ((0,), (0,)))
    serve_u = exact_dot(serve, onehot, ((0,), (0,)))
    equal = exact_dot(onehot, onehot, ((0,), (0,)))
    both = (users, users)
    position = jnp.sum(
        jnp.where(iota(both, 0) < iota(both, 1), equal, 0.0), axis=0, keepdims=True
    )
    return owner_u, rank_u, served_u, before_u, serve_u, position


def uplink_kernel(
    n,
    ring_of,
    guess_hbm,
    received_hbm,
    power_hbm,
    noise_hbm,
    gain_hbm,
    cluster_hbm,
    serving_hbm,
    owner_hbm,
    taps_hbm,
    table_hbm,
    coarse_hbm,
    spread_hbm,
    share_hbm,
    place_hbm,
    scale_hbm,
    packet_all,
    signal_all,
    received_ref,
    power_ref,
    noise_ref,
    gain_ref,
    cluster_ref,
    serving_ref,
    owner_ref,
    guess,
    taps,
    table,
    coarse,
    spread,
    half,
    other,
    packet_send,
    coef_b,
    gains,
    pick,
    pick_weight,
    power_wide,
    sampled,
    samples,
    cov,
    solved,
    smooth,
    share,
    place_ref,
    scale_ref,
    guess_sem,
    table_sem,
    half_send_sem,
    half_recv_sem,
    gain_send_sem,
    gain_recv_sem,
    packet_send_sem,
    packet_recv_sem,
    ring_send_sem,
    ring_recv_sem,
    small_sem,
    relay_send_sem,
    relay_recv_sem,
    share_sem,
    place_sem,
    present,
):
    stations, antennas, _, users, tones = guess.shape
    pieces = stations * antennas
    block = PEER_MAX * CU
    clusters = serving_ref.shape[0]
    me = lax.axis_index("ap")
    part = lax.axis_index("sc")
    node, place = ring_of
    spot = place(me)
    right = node(lax.rem(spot + 1, n))
    left = node(lax.rem(spot + n - 1, n))

    table_copies = []
    for source, into in (
        (taps_hbm.at[part], taps),
        (coarse_hbm, coarse),
        (spread_hbm.at[part], spread),
        (table_hbm.at[part], table),
    ):
        table_copies.append(
            pltpu.make_async_copy(source, into, table_sem.at[len(table_copies)])
        )
    received_copy = pltpu.make_async_copy(received_hbm, received_ref, place_sem.at[0])
    received_copy.start()
    small_copies = []
    for source, into in (
        (cluster_hbm, cluster_ref),
        (serving_hbm, serving_ref),
        (owner_hbm, owner_ref),
        (power_hbm, power_ref),
        (gain_hbm, gain_ref),
        (noise_hbm, noise_ref),
    ):
        copy = pltpu.make_async_copy(source, into, small_sem.at[len(small_copies)])
        copy.start()
        small_copies.append(copy)
    guess_copies = []
    for q in range(pieces):
        a, i = q // antennas, q % antennas
        copy = pltpu.make_async_copy(guess_hbm.at[a, i], guess.at[a, i], guess_sem)
        guess_copies.append(copy)

    barrier = pltpu.get_barrier_semaphore()
    pl.semaphore_signal(barrier, inc=1, device_id={"sc": 1 - part}, device_id_type=MESH)
    for peer in (left, right):
        pl.semaphore_signal(barrier, inc=1, device_id={"ap": peer}, device_id_type=MESH)
    table_copies[0].start()
    for copy in guess_copies:
        copy.start()
    for copy in table_copies[1:]:
        copy.start()
    ring_copies = {}
    reach = {}
    fine = 2 * stations
    for c in range(fine):
        far, near = n // 2, n - 1 - n // 2
        reach[c] = (far, near) if c % 2 == 0 else (near, far)
    steps = max(max(r) for r in reach.values())

    def fine_part(ref, c):
        some = antennas // 2
        return ref.at[c // 2, pl.ds(c % 2 * some, some)]

    def origin_of(direction, step):
        back = lax.rem(spot + n - step, n) if direction == 0 else lax.rem(spot + step, n)
        return node(back)

    def ring_step(a, step):
        for c in range(a * fine // stations, (a + 1) * fine // stations):
            for direction in range(2):
                if step > reach[c][direction]:
                    continue
                origin = origin_of(direction, step)
                source = fine_part(received_ref, c)
                if step > 0:
                    ring_copies[c, direction, step - 1].wait_recv()
                    source = fine_part(signal_all.at[origin], c)
                if step == reach[c][direction]:
                    continue
                copy = pltpu.make_async_remote_copy(
                    src_ref=source,
                    dst_ref=fine_part(signal_all.at[origin], c),
                    send_sem=ring_send_sem,
                    recv_sem=ring_recv_sem.at[direction, c, step],
                    device_id={"ap": right if direction == 0 else left},
                    device_id_type=MESH,
                )
                copy.start()
                ring_copies[c, direction, step] = copy

    received_copy.wait()
    for copy in small_copies:
        copy.wait()

    def present_send(level):
        if level < steps:
            for side, peer in ((0, right), (1, left)):
                pl.semaphore_signal(
                    present.at[side, level], inc=1, device_id={"ap": peer}, device_id_type=MESH
                )

    def present_wait(level):
        if level < steps:
            for side in range(2):
                pl.semaphore_wait(present.at[side, level], 1)
            present_send(level + 1)

    pl.semaphore_wait(barrier, 3)
    present_send(1)
    for c in range(stations):
        ring_step(c, 0)
    owner_u, rank_u, served_u, before_u, serve_u, position = user_tables(
        cluster_ref[...], serving_ref[...], owner_ref[...], clusters, users, stations, n
    )
    mef = me.astype(jnp.float32)
    mine = iota((n, users), 0) == mef
    served_me = jnp.sum(jnp.where(mine, served_u, 0.0), axis=0, keepdims=True)
    before_me = jnp.sum(jnp.where(mine, before_u, 0.0), axis=0, keepdims=True)
    target = jnp.where(
        served_me > 0.5, owner_u * block + before_me * CU + position, -1.0
    )
    chosen_user = iota((n * block, users), 0) == target
    pick[...] = jnp.where(chosen_user, 1.0, 0.0).astype(jnp.bfloat16)
    for a in range(stations):
        row_here = iota((n * stations, users), 0) == mef * stations + a
        weight = jnp.sum(jnp.where(row_here, serve_u, 0.0), axis=0, keepdims=True)
        weight = weight * gain_ref[a : a + 1, :]
        column = jnp.sum(jnp.where(chosen_user, weight, 0.0), axis=1, keepdims=True)
        pick_weight[a] = jnp.broadcast_to(column, (n * block, LANES))
    wide = jnp.broadcast_to(power_ref[...] * (1.0 / users), (LANES, users))
    power_wide[...] = jnp.transpose(wide)

    present_wait(1)
    table_copies[0].wait()
    pltpu.make_async_copy(guess_hbm, guess, guess_sem).wait()
    count = pieces * users
    lower = lax.broadcasted_iota(jnp.int32, (count, 2 * TAPS), 1) < TAPS
    products = [
        jnp.dot(
            guess[:, :, reim].reshape(count, tones), taps[...], preferred_element_type=jnp.float32
        )
        for reim in range(2)
    ]
    turned = pltpu.roll(products[1], TAPS, axis=1)
    sums = products[0] + jnp.where(lower, -turned, turned)
    half[...] = (sums * (1.0 / TONE_NUMBER)).astype(jnp.bfloat16).reshape(half.shape)
    present_wait(2)
    half_copies = []
    for a in range(stations):
        window = pl.ds(a * antennas, antennas)
        copy = pltpu.make_async_remote_copy(
            src_ref=half.at[window],
            dst_ref=other.at[window],
            send_sem=half_send_sem.at[a],
            recv_sem=half_recv_sem.at[a],
            device_id={"sc": 1 - part},
            device_id_type=MESH,
        )
        copy.start()
        half_copies.append(copy)
    ring_step(0, 1)
    sums = []
    for q in range(pieces):
        if q % antennas == 0:
            half_copies[q // antennas].wait_recv()
        total = (half[q].astype(jnp.float32) + other[q].astype(jnp.float32)).astype(jnp.bfloat16)
        coef_b[pl.ds(q * users, users), :] = total
        sums.append(total)
    symbols = received_ref.shape[3]
    rows = stations * symbols
    entries = [(i, j) for i in range(antennas) for j in range(i + 1)]
    kinds = antennas * antennas
    for copy in table_copies[1:]:
        copy.wait()
    both = jnp.dot(coef_b[...], coarse[...], preferred_element_type=jnp.float32)
    for reim in range(2):
        sampled[reim] = both[:, reim * COARSE : (reim + 1) * COARSE]
    chosen = jnp.dot(
        pick[...], jnp.concatenate(sums, axis=1), preferred_element_type=jnp.float32
    )
    for q in range(pieces):
        values = chosen[:, q * 2 * TAPS : (q + 1) * 2 * TAPS] * pick_weight[q // antennas]
        packet_send[:, q] = values.astype(jnp.bfloat16).reshape(n, block, 2 * TAPS)
    for c in range(1, stations):
        ring_step(c, 1)
    for a in range(stations):

        def body(step, sums, a=a):
            sums = list(sums)
            for w in range(2):
                row = (step * 2 + w) * 8
                scale = power_wide[pl.ds(pl.multiple_of(row, 8), 8), :]
                re, im = [], []
                for i in range(antennas):
                    at = pl.multiple_of((a * antennas + i) * users + row, 8)
                    re.append(sampled[0, pl.ds(at, 8), :])
                    im.append(sampled[1, pl.ds(at, 8), :])
                at = 0
                for i in range(antennas):
                    sre, sim = re[i] * scale, im[i] * scale
                    for j in range(i + 1):
                        sums[at] = sums[at] + (sre * re[j] + sim * im[j])
                        at += 1
                        if j < i:
                            sums[at] = sums[at] + (sim * re[j] - sre * im[j])
                            at += 1
            return tuple(sums)

        zero = jnp.zeros((8, COARSE), jnp.float32)
        sums = lax.fori_loop(0, users // 16, body, (zero,) * (antennas * antennas))
        at = 0
        for i, j in entries:
            for reim in range(1 if i == j else 2):
                value = jnp.sum(sums[at], axis=0, keepdims=True)
                if i == j:
                    value = value + noise_ref[0:1, a : a + 1]
                samples[pl.ds(at * stations + a, 1), :] = value
                at += 1
    high = samples[...].astype(jnp.bfloat16)
    low = (samples[...] - high.astype(jnp.float32)).astype(jnp.bfloat16)
    held_rows = kinds * stations // block
    for k in range(n):
        packet_send[k, pieces : pieces + held_rows] = high.reshape(held_rows, block, COARSE)
        packet_send[k, pieces + held_rows :] = low.reshape(held_rows, block, COARSE)
    parcels = packet_send.shape[1]
    mine_half = pl.ds(part * (parcels // 2), parcels // 2)
    packets = {}

    def packet_start(step):
        window = mine_half
        for k in sorted({step, n - step}):
            peer = node(lax.rem(spot + k, n))
            copy = pltpu.make_async_remote_copy(
                src_ref=packet_send.at[peer, window],
                dst_ref=packet_all.at[me, window],
                send_sem=packet_send_sem,
                recv_sem=packet_recv_sem.at[k],
                device_id={"ap": peer},
                device_id_type=MESH,
            )
            copy.start()
            packets[k] = copy

    for level in range(3, steps):
        present_wait(level)
    for step in range(1, steps + 1):
        packet_start(step)

    def gain_all():
        return pltpu.make_async_remote_copy(
            src_ref=gains.at[pl.ds(0, n - 1)],
            dst_ref=gains.at[pl.ds(0, n - 1)],
            send_sem=gain_send_sem,
            recv_sem=gain_recv_sem,
            device_id={"ap": right},
            device_id_type=MESH,
        )

    for k in range(1, n):
        peer = lax.rem(me + k, n)
        copy = pltpu.make_async_remote_copy(
            src_ref=gain_ref,
            dst_ref=gains.at[me],
            send_sem=gain_send_sem,
            recv_sem=gain_recv_sem,
            device_id={"ap": peer},
            device_id_type=MESH,
        )
        copy.start()
    gains[me] = gain_ref[...]
    relays = {}

    def relay_start(step):
        for k in sorted({step, n - step}):
            packets[k].wait_recv()
            origin = node(lax.rem(spot + n - k, n))
            copy = pltpu.make_async_remote_copy(
                src_ref=packet_all.at[origin, mine_half],
                dst_ref=packet_all.at[origin, mine_half],
                send_sem=relay_send_sem,
                recv_sem=relay_recv_sem.at[k],
                device_id={"sc": 1 - part},
                device_id_type=MESH,
            )
            copy.start()
            relays[k] = copy

    def relay_wait(step):
        for k in sorted({step, n - step}):
            relays[k].wait_recv()

    tiles = tones // LANES
    station_of = lax.broadcasted_iota(jnp.int32, (rows, 1), 0)

    def prepare(packet, signals, slot):
        high = packet[pieces : pieces + held_rows].reshape(kinds * stations, COARSE)
        low = packet[pieces + held_rows :].reshape(kinds * stations, COARSE)
        cov[slot] = jnp.dot(
            jnp.concatenate([high, high], axis=1),
            spread[...],
            preferred_element_type=jnp.float32,
        ) + jnp.dot(low, spread[:COARSE, :], preferred_element_type=jnp.float32)
        width = min(tones, 4 * LANES)
        for base in range(0, tones, width):
            lanes = slice(base, base + width)

            def entry(at):
                value = jnp.broadcast_to(
                    cov[slot, at * stations : at * stations + 1, lanes], (rows, width)
                )
                for a in range(1, stations):
                    row = jnp.broadcast_to(
                        cov[slot, at * stations + a : at * stations + a + 1, lanes], (rows, width)
                    )
                    value = jnp.where(station_of < a * symbols, value, row)
                return value

            cov_re = [[None] * antennas for _ in range(antennas)]
            cov_im = [[None] * antennas for _ in range(antennas)]
            at = 0
            for i, j in entries:
                cov_re[i][j] = entry(at)
                at += 1
                if i != j:
                    cov_im[i][j] = entry(at)
                    at += 1
            right_side = []
            for i in range(antennas):
                right_side.append(
                    tuple(
                        jnp.concatenate(
                            [
                                signals[a, i, reim, :, lanes].astype(jnp.float32)
                                for a in range(stations)
                            ],
                            axis=0,
                        )
                        for reim in range(2)
                    )
                )
            answer = hermitian_solve(cov_re, cov_im, right_side)
            for i in range(antennas):
                re, im = answer[i]
                solved[slot, i, 0, :, lanes] = re
                solved[slot, i, 1, :, lanes] = im
                solved[slot, i, 2, :, lanes] = re + im

    def combine(origin, packet, slot):
        coefs = packet[:pieces].reshape(pieces * block, 2 * TAPS)
        for l in range(tiles):
            columns = pl.ds(l * 2 * LANES, 2 * LANES)
            smooth[slot, l] = jnp.dot(coefs, table[:, columns], preferred_element_type=jnp.float32)
        here = pl.ds(pl.multiple_of(origin * block, block), block)
        for l in range(tiles):
            lanes = pl.ds(l * LANES, LANES)
            sums = [[None] * symbols for _ in range(PEER_MAX)]
            for a in range(stations):
                for i in range(antennas):
                    re, im, gap = [], [], []
                    for k in range(PEER_MAX):
                        at = (a * antennas + i) * block + k * CU
                        re.append(smooth[slot, l, pl.ds(at, CU), :LANES])
                        im.append(smooth[slot, l, pl.ds(at, CU), LANES:])
                        gap.append(re[k] - im[k])
                    for s in range(symbols):
                        row = pl.ds(a * symbols + s, 1)
                        sre = solved[slot, i, 0, row, lanes]
                        sim = solved[slot, i, 1, row, lanes]
                        ssum = solved[slot, i, 2, row, lanes]
                        for k in range(PEER_MAX):
                            new = (re[k] * sre, im[k] * sim, gap[k] * ssum)
                            old = sums[k][s]
                            if old is not None:
                                new = tuple(x + y for x, y in zip(old, new))
                            sums[k][s] = new
            for s in range(symbols):
                first = [sums[k][s][0] + sums[k][s][1] for k in range(PEER_MAX)]
                second = [
                    sums[k][s][2] - (sums[k][s][0] - sums[k][s][1]) for k in range(PEER_MAX)
                ]
                for reim, values in ((0, first), (1, second)):
                    share[s * 2 + reim, here, lanes] = jnp.concatenate(values, axis=0).astype(
                        jnp.bfloat16
                    )

    def send_share(origin):
        here = pl.ds(pl.multiple_of(origin * block, block), block)
        copy = pltpu.make_async_copy(
            share.at[:, here], share_hbm.at[:, here], share_sem
        )
        copy.start()

    tasks = [(me, packet_send.at[me], received_ref, 0)]
    for step in range(1, steps + 1):
        for direction in range(2 if step <= n - 1 - n // 2 else 1):
            origin = origin_of(direction, step)
            tasks.append((origin, packet_all.at[origin], signal_all.at[origin], step))

    prepare(*tasks[0][1:3], 0)
    combine(*tasks[0][:2], 0)
    send_share(me)
    if steps > 1:
        ring_step(0, 2)
    relay_start(1)
    relay_wait(1)
    prepare(*tasks[1][1:3], 1)
    advanced = {(c, 1) for c in range(stations)} | {(0, 2)}

    def advance(c, step):
        if step <= steps and (c, step) not in advanced:
            ring_step(c, step)
            advanced.add((c, step))

    for c in range(1, stations):
        advance(c, 2)
    for t in range(1, len(tasks)):
        origin, packet, _, step = tasks[t]
        last = t + 1 == len(tasks)
        after = step if last else tasks[t + 1][3]
        begins = tasks[t - 1][3] < step
        combine(origin, packet, t % 2)
        if not last:
            if after > step:
                for c in range(stations):
                    advance(c, after)
                relay_wait(after)
            prepare(*tasks[t + 1][1:3], (t + 1) % 2)
        send_share(origin)
        if begins and step < steps:
            advance(0, step + 1)
            if step == 1:
                for c in range(1, stations):
                    advance(c, 2)
            relay_start(step + 1)
        if t == len(tasks) - 3:
            gain_all().wait_recv()
            totals = jnp.zeros((1, users), jnp.float32)
            for p in range(n):
                for a in range(stations):
                    row = serve_u[p * stations + a : p * stations + a + 1] * gains[p, a : a + 1, :]
                    totals = totals + row
            scale = 1.0 / (1.0 + totals)
            held = owner_u == mef
            slot_user = iota((OWN_MAX * CU, users), 0) == jnp.where(held, rank_u * CU + position, -1.0)
            slot_rows = jnp.where(slot_user, 1.0, 0.0)
            slot_scale = jnp.sum(jnp.where(slot_user, scale, 0.0), axis=1, keepdims=True)
            scale_ref[...] = jnp.broadcast_to(slot_scale, (OWN_MAX * CU, LANES))
            hits = []
            for p in range(n):
                goal = jnp.where(
                    held & (served_u[p : p + 1] > 0.5), before_u[p : p + 1] * CU + position, -1.0
                )
                hits.append(jnp.where(iota((block, users), 0) == goal, 1.0, 0.0))
            placement = exact_dot(slot_rows, jnp.concatenate(hits, axis=0), ((1,), (1,)))
            place_ref[...] = placement.astype(jnp.bfloat16)
            place_copies = []
            for source, into in ((place_ref, place_hbm), (scale_ref, scale_hbm)):
                copy = pltpu.make_async_copy(source, into, place_sem.at[1 + len(place_copies)])
                copy.start()
                place_copies.append(copy)

    pltpu.make_async_copy(share, share_hbm, share_sem).wait()
    for copy in place_copies:
        copy.wait()
    for copy in half_copies:
        copy.wait_send()
    gain_all().wait_send()
    for send_sem in (packet_send_sem, relay_send_sem):
        pltpu.make_async_remote_copy(
            src_ref=packet_all.at[pl.ds(0, n - 1), mine_half],
            dst_ref=packet_all.at[pl.ds(0, n - 1), mine_half],
            send_sem=send_sem,
            recv_sem=packet_recv_sem.at[0],
            device_id={"ap": right},
            device_id_type=MESH,
        ).wait_send()
    pltpu.make_async_remote_copy(
        src_ref=signal_all.at[pl.ds(0, n - 1)],
        dst_ref=signal_all.at[pl.ds(0, n - 1)],
        send_sem=ring_send_sem,
        recv_sem=ring_recv_sem.at[0, 0, 0],
        device_id={"ap": right},
        device_id_type=MESH,
    ).wait_send()


def place_kernel(
    place_hbm, scale_hbm, share_hbm, out_hbm, place_ref, scale_ref, share, lines, small_sem, in_sem, out_sem
):
    kinds, _, tones = share.shape
    symbols, tiles = kinds // 2, tones // LANES
    arrivals = []
    for kind in range(kinds):
        arrivals.append(
            pltpu.make_async_copy(share_hbm.at[kind], share.at[kind], in_sem.at[kind])
        )
    smalls = []
    for source, into in ((place_hbm, place_ref), (scale_hbm, scale_ref)):
        copy = pltpu.make_async_copy(source, into, small_sem.at[len(smalls)])
        copy.start()
        smalls.append(copy)
    for copy in arrivals:
        copy.start()
    for copy in smalls:
        copy.wait()
    copies = []
    for s in range(symbols):
        placed = []
        for reim in range(2):
            arrivals[s * 2 + reim].wait()
            placed.append(
                jnp.dot(place_ref[...], share[s * 2 + reim], preferred_element_type=jnp.float32)
            )
        for r in range(OWN_MAX):
            rows = slice(r * CU, (r + 1) * CU)
            scale = scale_ref[rows]
            parts = [
                placed[reim][rows, l * LANES : (l + 1) * LANES] * scale
                for l in range(tiles)
                for reim in range(2)
            ]
            for first in range(0, 2 * tiles, CU):
                square = jnp.stack(parts[first : first + CU], axis=0)
                lines[s, rows, first : first + CU, :] = jnp.transpose(square, (1, 0, 2))
        copy = pltpu.make_async_copy(lines.at[s], out_hbm.at[:, s], out_sem.at[s])
        copy.start()
        copies.append(copy)
    for copy in copies:
        copy.wait()


def ring_functions(mesh):
    n = mesh.shape["ap"]
    half = n // 2

    def plain(q):
        return q

    def node(q):
        upper = q // half
        return (1 - upper) * 2 * q + upper * (2 * (n - q) - 1)

    def place(d):
        odd = d % 2
        return (1 - odd) * (d // 2) + odd * (n - (d + 1) // 2)

    if n % 2:
        return plain, plain
    try:
        axes = list(mesh.axis_names)
        line = np.moveaxis(mesh.devices, axes.index("ap"), 0).reshape(n, -1)[:, 0]
        spots = [tuple(d.coords) for d in line]
        sizes = [max(s[x] for s in spots) + 1 for x in range(3)]

        def length(order):
            far = 0
            for q in range(n):
                one, two = spots[order(q)], spots[order((q + 1) % n)]
                far += sum(
                    min(abs(one[x] - two[x]), sizes[x] - abs(one[x] - two[x])) for x in range(3)
                )
            return far

        if length(plain) < length(node):
            return plain, plain
    except (AttributeError, TypeError):
        pass
    return node, place


def local(
    n,
    parts,
    ring_of,
    unsmoothed_link_guesses,
    received,
    user_power,
    noise_power,
    ap_gain,
    user_cluster,
    serving,
    cluster_owner,
):
    stations, antennas, _, users, tones = unsmoothed_link_guesses.shape
    symbols = received.shape[3]
    pieces = stations * antennas
    block = PEER_MAX * CU
    rows = stations * symbols
    parcels = pieces + 2 * (antennas * antennas * stations // block)
    steps = n // 2
    dma = pltpu.SemaphoreType.DMA
    bf16, f32 = jnp.bfloat16, jnp.float32
    hbm = pl.BlockSpec(memory_space=pltpu.HBM)
    tiles = tones // LANES
    slots = OWN_MAX * CU
    share, place, scale = pl.pallas_call(
        functools.partial(uplink_kernel, n, ring_of),
        out_shape=(
            jax.ShapeDtypeStruct((symbols * 2, n * block, tones), bf16),
            jax.ShapeDtypeStruct((slots, n * block), bf16),
            jax.ShapeDtypeStruct((slots, LANES), f32),
        ),
        in_specs=[hbm] * 12,
        out_specs=(hbm, hbm, hbm),
        scratch_shapes=[
            pltpu.VMEM((n, parcels, block, 2 * TAPS), bf16),
            pltpu.VMEM((n,) + received.shape, bf16),
            pltpu.VMEM(received.shape, bf16),
            pltpu.VMEM((1, users), f32),
            pltpu.VMEM((1, stations), f32),
            pltpu.VMEM((stations, users), f32),
            pltpu.VMEM((1, users), jnp.int32),
            pltpu.VMEM(serving.shape, jnp.int32),
            pltpu.VMEM((1, serving.shape[0]), jnp.int32),
            pltpu.VMEM((stations, antennas, 2, users, tones), bf16),
            pltpu.VMEM((tones, 2 * TAPS), bf16),
            pltpu.VMEM((2 * TAPS, 2 * tones), bf16),
            pltpu.VMEM((2 * TAPS, 2 * COARSE), bf16),
            pltpu.VMEM((2 * COARSE, tones), bf16),
            pltpu.VMEM((pieces, users, 2 * TAPS), bf16),
            pltpu.VMEM((pieces, users, 2 * TAPS), bf16),
            pltpu.VMEM((n, parcels, block, 2 * TAPS), bf16),
            pltpu.VMEM((pieces * users, 2 * TAPS), bf16),
            pltpu.VMEM((n, stations, users), f32),
            pltpu.VMEM((n * block, users), bf16),
            pltpu.VMEM((stations, n * block, LANES), f32),
            pltpu.VMEM((users, LANES), f32),
            pltpu.VMEM((2, pieces * users, COARSE), f32),
            pltpu.VMEM((antennas * antennas * stations, COARSE), f32),
            pltpu.VMEM((2, antennas * antennas * stations, tones), f32),
            pltpu.VMEM((2, antennas, 3, rows, tones), f32),
            pltpu.VMEM((2, tiles, pieces * block, 2 * LANES), f32),
            pltpu.VMEM((symbols * 2, n * block, tones), bf16),
            pltpu.VMEM((slots, n * block), bf16),
            pltpu.VMEM((slots, LANES), f32),
            dma,
            dma((4,)),
            dma((stations,)),
            dma((stations,)),
            dma,
            dma,
            dma,
            dma((n,)),
            dma,
            dma((2, 2 * stations, steps)),
            dma((6,)),
            dma,
            dma((n,)),
            dma,
            dma((3,)),
            pltpu.SemaphoreType.REGULAR((2, steps)),
        ],
        compiler_params=pltpu.CompilerParams(
            collective_id=0, has_side_effects=True, vmem_limit_bytes=VMEM_BYTES
        ),
        name="uplink",
    )(
        unsmoothed_link_guesses,
        received,
        user_power.reshape(1, users),
        noise_power.reshape(1, stations),
        ap_gain,
        user_cluster.reshape(1, users),
        serving,
        cluster_owner.reshape(1, -1),
        jnp.asarray(tap_tables(parts, tones)),
        jnp.asarray(tone_tables(parts, tones)),
        jnp.asarray(coarse_table()),
        jnp.asarray(spread_tables(parts, tones)),
    )
    placed = pl.pallas_call(
        place_kernel,
        out_shape=jax.ShapeDtypeStruct((slots, symbols, tiles * 2, LANES), f32),
        in_specs=[hbm, hbm, hbm],
        out_specs=hbm,
        scratch_shapes=[
            pltpu.VMEM((slots, n * block), bf16),
            pltpu.VMEM((slots, LANES), f32),
            pltpu.VMEM((symbols * 2, n * block, tones), bf16),
            pltpu.VMEM((symbols, slots, tiles * 2, LANES), f32),
            dma((2,)),
            dma((symbols * 2,)),
            dma((symbols,)),
        ],
        compiler_params=pltpu.CompilerParams(vmem_limit_bytes=VMEM_BYTES),
        name="place",
    )(place, scale, share)
    placed = placed.reshape(OWN_MAX, CU, symbols, tiles, 2, LANES)
    placed = jnp.transpose(placed, (0, 1, 2, 4, 3, 5))
    return placed.reshape(OWN_MAX, CU, symbols, 2, tones)


def solution(mesh):
    placed = (
        P(("cell", "ap"), None, None, None, "sc"),
        P(("cell", "ap"), None, None, None, "sc"),
        P("cell"),
        P(("cell", "ap")),
        P(("cell", "ap"), None),
        P("cell"),
        P("cell", None),
        P("cell", None),
    )
    return jax.shard_map(
        functools.partial(local, mesh.shape["ap"], mesh.shape["sc"], ring_functions(mesh)),
        mesh=mesh,
        in_specs=placed,
        out_specs=P(("cell", "ap"), None, None, None, "sc"),
        check_vma=False,
    )
```

```python
import functools
import math

import jax
import jax.numpy as jnp
import numpy as np
from jax import lax
from jax.experimental import pallas as pl
from jax.experimental.pallas import tpu as pltpu
from jax.sharding import PartitionSpec as P

TONE_NUMBER = 2048
TAPS = 64
CU = 8
OWN_MAX = 4
PEER_MAX = 2
COARSE = 2 * TAPS
MESH = pl.DeviceIdType.MESH
LANES = 128
VMEM_BYTES = 67043328


def complex_times(left_factor, right_factor):
    return (
        left_factor[0] * right_factor[0] - left_factor[1] * right_factor[1],
        left_factor[0] * right_factor[1] + left_factor[1] * right_factor[0],
    )


def times_conj(left_factor, right_factor):
    return (
        left_factor[0] * right_factor[0] + left_factor[1] * right_factor[1],
        left_factor[1] * right_factor[0] - left_factor[0] * right_factor[1],
    )


def hermitian_solve(cov_re, cov_im, right):
    dimension = len(cov_re)
    factor = {}
    inverses = []
    for j in range(dimension):
        pivot = cov_re[j][j]
        for k in range(j):
            element = factor[j, k]
            pivot = pivot - (element[0] * element[0] + element[1] * element[1])
        inverse = 1.0 / jnp.sqrt(pivot)
        inverses.append(inverse)
        for i in range(j + 1, dimension):
            running = (cov_re[i][j], cov_im[i][j])
            for k in range(j):
                product = times_conj(factor[i, k], factor[j, k])
                running = (running[0] - product[0], running[1] - product[1])
            factor[i, j] = (running[0] * inverse, running[1] * inverse)
    forward = []
    for i in range(dimension):
        running = right[i]
        for k in range(i):
            product = complex_times(factor[i, k], forward[k])
            running = (running[0] - product[0], running[1] - product[1])
        forward.append((running[0] * inverses[i], running[1] * inverses[i]))
    result = [None] * dimension
    for i in range(dimension - 1, -1, -1):
        running = forward[i]
        for k in range(i + 1, dimension):
            product = times_conj(result[k], factor[k, i])
            running = (running[0] - product[0], running[1] - product[1])
        result[i] = (running[0] * inverses[i], running[1] * inverses[i])
    return result


def angles_of(values):
    rotation = np.arange(TAPS, dtype=np.int32)[:, None] * values[None, :] % TONE_NUMBER
    return rotation.astype(np.float32) * np.float32(2.0 * math.pi / TONE_NUMBER)


def wave_table(values):
    cosine, sine = np.cos(angles_of(values)), np.sin(angles_of(values))
    return np.concatenate([cosine, sine], axis=0), np.concatenate([-sine, cosine], axis=0)


def tap_tables(parts, tones):
    made = []
    for part in range(parts):
        real, _ = wave_table(part * tones + np.arange(tones, dtype=np.int32))
        made.append(real.T)
    return np.stack(made).astype(jnp.bfloat16)


def tone_tables(parts, tones):
    made = []
    for part in range(parts):
        real, imag = wave_table(part * tones + np.arange(tones, dtype=np.int32))
        pair = np.stack(
            [real.reshape(2 * TAPS, -1, LANES), imag.reshape(2 * TAPS, -1, LANES)], axis=2
        )
        made.append(pair.reshape(2 * TAPS, 2 * tones))
    return np.stack(made).astype(jnp.bfloat16)


def coarse_table():
    step = TONE_NUMBER // COARSE
    real, imag = wave_table(step * np.arange(COARSE, dtype=np.int32))
    return np.concatenate([real, imag], axis=1).astype(jnp.bfloat16)


def spread_tables(parts, tones):
    step = TONE_NUMBER // COARSE
    made = []
    for part in range(parts):
        values = part * tones + np.arange(tones, dtype=np.int64)
        gap = values[None, :] - step * np.arange(COARSE, dtype=np.int64)[:, None]
        kernel = np.ones(gap.shape, np.float64)
        for d in range(1, COARSE // 2 + 1):
            share = 2.0 if d < COARSE // 2 else 1.0
            kernel += share * np.cos(2.0 * math.pi / TONE_NUMBER * (d * gap % TONE_NUMBER))
        kernel /= COARSE
        high = kernel.astype(np.float32).astype(jnp.bfloat16)
        low = (kernel - high.astype(np.float64)).astype(np.float32).astype(jnp.bfloat16)
        made.append(np.concatenate([high, low], axis=0))
    return np.stack(made)


def exact_dot(left, right, dims):
    return lax.dot_general(
        left.astype(jnp.bfloat16),
        right.astype(jnp.bfloat16),
        (dims, ((), ())),
        preferred_element_type=jnp.float32,
    )


def iota(shape, dim):
    return lax.broadcasted_iota(jnp.int32, shape, dim).astype(jnp.float32)


def user_tables(user_cluster, serving, owner, clusters, users, group, n):
    onehot = (iota((clusters, users), 0) == user_cluster.astype(jnp.float32)).astype(jnp.float32)
    owner_row = owner.astype(jnp.float32)
    square = (clusters, clusters)
    rows, cols = iota(square, 0), iota(square, 1)
    owner_col = jnp.sum(jnp.where(rows == cols, owner_row, 0.0), axis=1, keepdims=True)
    same = owner_col == owner_row
    earlier = jnp.where(same & (cols < rows), 1.0, 0.0)
    serve = serving.astype(jnp.float32)
    pair = jnp.where(
        jnp.floor((iota((group * n, n), 0) + 0.5) * (1.0 / group)) == iota((group * n, n), 1),
        1.0,
        0.0,
    )
    served = jnp.where(exact_dot(serve, pair, ((1,), (0,))) > 0.5, 1.0, 0.0)
    before = exact_dot(earlier, served, ((1,), (0,)))
    rank = jnp.sum(earlier, axis=1, keepdims=True)
    owner_u = jnp.sum(onehot * owner_col, axis=0, keepdims=True)
    rank_u = jnp.sum(onehot * rank, axis=0, keepdims=True)
    served_u = exact_dot(served, onehot, ((0,), (0,)))
    before_u = exact_dot(before, onehot, ((0,), (0,)))
    serve_u = exact_dot(serve, onehot, ((0,), (0,)))
    equal = exact_dot(onehot, onehot, ((0,), (0,)))
    both = (users, users)
    position = jnp.sum(
        jnp.where(iota(both, 0) < iota(both, 1), equal, 0.0), axis=0, keepdims=True
    )
    return owner_u, rank_u, served_u, before_u, serve_u, position


def uplink_kernel(
    n,
    ring_of,
    guess_hbm,
    received_hbm,
    power_hbm,
    noise_hbm,
    gain_hbm,
    cluster_hbm,
    serving_hbm,
    owner_hbm,
    taps_hbm,
    table_hbm,
    coarse_hbm,
    spread_hbm,
    share_hbm,
    place_hbm,
    scale_hbm,
    packet_all,
    signal_all,
    received_ref,
    power_ref,
    noise_ref,
    gain_ref,
    cluster_ref,
    serving_ref,
    owner_ref,
    guess,
    taps,
    table,
    coarse,
    spread,
    half,
    other,
    packet_send,
    coef_b,
    gains,
    pick,
    pick_weight,
    power_wide,
    sampled,
    samples,
    cov,
    solved,
    smooth,
    share,
    place_ref,
    scale_ref,
    guess_sem,
    table_sem,
    half_send_sem,
    half_recv_sem,
    gain_send_sem,
    gain_recv_sem,
    packet_send_sem,
    packet_recv_sem,
    ring_send_sem,
    ring_recv_sem,
    small_sem,
    relay_send_sem,
    relay_recv_sem,
    share_sem,
    place_sem,
    present,
):
    stations, antennas, _, users, tones = guess.shape
    pieces = stations * antennas
    block = PEER_MAX * CU
    clusters = serving_ref.shape[0]
    me = lax.axis_index("ap")
    part = lax.axis_index("sc")
    node, place = ring_of
    spot = place(me)
    right = node(lax.rem(spot + 1, n))
    left = node(lax.rem(spot + n - 1, n))

    table_copies = []
    for source, into in (
        (taps_hbm.at[part], taps),
        (coarse_hbm, coarse),
        (spread_hbm.at[part], spread),
        (table_hbm.at[part], table),
    ):
        table_copies.append(
            pltpu.make_async_copy(source, into, table_sem.at[len(table_copies)])
        )
    received_copy = pltpu.make_async_copy(received_hbm, received_ref, place_sem.at[0])
    received_copy.start()
    small_copies = []
    for source, into in (
        (cluster_hbm, cluster_ref),
        (serving_hbm, serving_ref),
        (owner_hbm, owner_ref),
        (power_hbm, power_ref),
        (gain_hbm, gain_ref),
        (noise_hbm, noise_ref),
    ):
        copy = pltpu.make_async_copy(source, into, small_sem.at[len(small_copies)])
        copy.start()
        small_copies.append(copy)
    guess_copies = []
    for q in range(pieces):
        a, i = q // antennas, q % antennas
        copy = pltpu.make_async_copy(guess_hbm.at[a, i], guess.at[a, i], guess_sem)
        guess_copies.append(copy)

    barrier = pltpu.get_barrier_semaphore()
    pl.semaphore_signal(barrier, inc=1, device_id={"sc": 1 - part}, device_id_type=MESH)
    for peer in (left, right):
        pl.semaphore_signal(barrier, inc=1, device_id={"ap": peer}, device_id_type=MESH)
    table_copies[0].start()
    for copy in guess_copies:
        copy.start()
    for copy in table_copies[1:]:
        copy.start()
    ring_copies = {}
    reach = {}
    fine = 2 * stations
    for c in range(fine):
        far, near = n // 2, n - 1 - n // 2
        reach[c] = (far, near) if c % 2 == 0 else (near, far)
    steps = max(max(r) for r in reach.values())

    def fine_part(ref, c):
        some = antennas // 2
        return ref.at[c // 2, pl.ds(c % 2 * some, some)]

    def origin_of(direction, step):
        back = lax.rem(spot + n - step, n) if direction == 0 else lax.rem(spot + step, n)
        return node(back)

    def ring_step(a, step):
        for c in range(a * fine // stations, (a + 1) * fine // stations):
            for direction in range(2):
                if step > reach[c][direction]:
                    continue
                origin = origin_of(direction, step)
                source = fine_part(received_ref, c)
                if step > 0:
                    ring_copies[c, direction, step - 1].wait_recv()
                    source = fine_part(signal_all.at[origin], c)
                if step == reach[c][direction]:
                    continue
                copy = pltpu.make_async_remote_copy(
                    src_ref=source,
                    dst_ref=fine_part(signal_all.at[origin], c),
                    send_sem=ring_send_sem,
                    recv_sem=ring_recv_sem.at[direction, c, step],
                    device_id={"ap": right if direction == 0 else left},
                    device_id_type=MESH,
                )
                copy.start()
                ring_copies[c, direction, step] = copy

    received_copy.wait()
    for copy in small_copies:
        copy.wait()

    def present_send(level):
        if level < steps:
            for side, peer in ((0, right), (1, left)):
                pl.semaphore_signal(
                    present.at[side, level], inc=1, device_id={"ap": peer}, device_id_type=MESH
                )

    def present_wait(level):
        if level < steps:
            for side in range(2):
                pl.semaphore_wait(present.at[side, level], 1)
            present_send(level + 1)

    pl.semaphore_wait(barrier, 3)
    present_send(1)
    for c in range(stations):
        ring_step(c, 0)
    owner_u, rank_u, served_u, before_u, serve_u, position = user_tables(
        cluster_ref[...], serving_ref[...], owner_ref[...], clusters, users, stations, n
    )
    mef = me.astype(jnp.float32)
    mine = iota((n, users), 0) == mef
    served_me = jnp.sum(jnp.where(mine, served_u, 0.0), axis=0, keepdims=True)
    before_me = jnp.sum(jnp.where(mine, before_u, 0.0), axis=0, keepdims=True)
    target = jnp.where(
        served_me > 0.5, owner_u * block + before_me * CU + position, -1.0
    )
    chosen_user = iota((n * block, users), 0) == target
    pick[...] = jnp.where(chosen_user, 1.0, 0.0).astype(jnp.bfloat16)
    for a in range(stations):
        row_here = iota((n * stations, users), 0) == mef * stations + a
        weight = jnp.sum(jnp.where(row_here, serve_u, 0.0), axis=0, keepdims=True)
        weight = weight * gain_ref[a : a + 1, :]
        column = jnp.sum(jnp.where(chosen_user, weight, 0.0), axis=1, keepdims=True)
        pick_weight[a] = jnp.broadcast_to(column, (n * block, LANES))
    wide = jnp.broadcast_to(power_ref[...] * (1.0 / users), (LANES, users))
    power_wide[...] = jnp.transpose(wide)

    present_wait(1)
    table_copies[0].wait()
    pltpu.make_async_copy(guess_hbm, guess, guess_sem).wait()
    count = pieces * users
    lower = lax.broadcasted_iota(jnp.int32, (count, 2 * TAPS), 1) < TAPS
    products = [
        jnp.dot(
            guess[:, :, reim].reshape(count, tones), taps[...], preferred_element_type=jnp.float32
        )
        for reim in range(2)
    ]
    turned = pltpu.roll(products[1], TAPS, axis=1)
    sums = products[0] + jnp.where(lower, -turned, turned)
    half[...] = (sums * (1.0 / TONE_NUMBER)).astype(jnp.bfloat16).reshape(half.shape)
    present_wait(2)
    half_copies = []
    for a in range(stations):
        window = pl.ds(a * antennas, antennas)
        copy = pltpu.make_async_remote_copy(
            src_ref=half.at[window],
            dst_ref=other.at[window],
            send_sem=half_send_sem.at[a],
            recv_sem=half_recv_sem.at[a],
            device_id={"sc": 1 - part},
            device_id_type=MESH,
        )
        copy.start()
        half_copies.append(copy)
    ring_step(0, 1)
    sums = []
    for q in range(pieces):
        if q % antennas == 0:
            half_copies[q // antennas].wait_recv()
        total = (half[q].astype(jnp.float32) + other[q].astype(jnp.float32)).astype(jnp.bfloat16)
        coef_b[pl.ds(q * users, users), :] = total
        sums.append(total)
    symbols = received_ref.shape[3]
    rows = stations * symbols
    entries = [(i, j) for i in range(antennas) for j in range(i + 1)]
    kinds = antennas * antennas
    for copy in table_copies[1:]:
        copy.wait()
    both = jnp.dot(coef_b[...], coarse[...], preferred_element_type=jnp.float32)
    for reim in range(2):
        sampled[reim] = both[:, reim * COARSE : (reim + 1) * COARSE]
    chosen = jnp.dot(
        pick[...], jnp.concatenate(sums, axis=1), preferred_element_type=jnp.float32
    )
    for q in range(pieces):
        values = chosen[:, q * 2 * TAPS : (q + 1) * 2 * TAPS] * pick_weight[q // antennas]
        packet_send[:, q] = values.astype(jnp.bfloat16).reshape(n, block, 2 * TAPS)
    for c in range(1, stations):
        ring_step(c, 1)
    for a in range(stations):

        def body(step, sums, a=a):
            sums = list(sums)
            for w in range(2):
                row = (step * 2 + w) * 8
                scale = power_wide[pl.ds(pl.multiple_of(row, 8), 8), :]
                re, im = [], []
                for i in range(antennas):
                    at = pl.multiple_of((a * antennas + i) * users + row, 8)
                    re.append(sampled[0, pl.ds(at, 8), :])
                    im.append(sampled[1, pl.ds(at, 8), :])
                at = 0
                for i in range(antennas):
                    sre, sim = re[i] * scale, im[i] * scale
                    for j in range(i + 1):
                        sums[at] = sums[at] + (sre * re[j] + sim * im[j])
                        at += 1
                        if j < i:
                            sums[at] = sums[at] + (sim * re[j] - sre * im[j])
                            at += 1
            return tuple(sums)

        zero = jnp.zeros((8, COARSE), jnp.float32)
        sums = lax.fori_loop(0, users // 16, body, (zero,) * (antennas * antennas))
        at = 0
        for i, j in entries:
            for reim in range(1 if i == j else 2):
                value = jnp.sum(sums[at], axis=0, keepdims=True)
                if i == j:
                    value = value + noise_ref[0:1, a : a + 1]
                samples[pl.ds(at * stations + a, 1), :] = value
                at += 1
    high = samples[...].astype(jnp.bfloat16)
    low = (samples[...] - high.astype(jnp.float32)).astype(jnp.bfloat16)
    held_rows = kinds * stations // block
    for k in range(n):
        packet_send[k, pieces : pieces + held_rows] = high.reshape(held_rows, block, COARSE)
        packet_send[k, pieces + held_rows :] = low.reshape(held_rows, block, COARSE)
    parcels = packet_send.shape[1]
    mine_half = pl.ds(part * (parcels // 2), parcels // 2)
    packets = {}

    def packet_start(step):
        window = mine_half
        for k in sorted({step, n - step}):
            peer = node(lax.rem(spot + k, n))
            copy = pltpu.make_async_remote_copy(
                src_ref=packet_send.at[peer, window],
                dst_ref=packet_all.at[me, window],
                send_sem=packet_send_sem,
                recv_sem=packet_recv_sem.at[k],
                device_id={"ap": peer},
                device_id_type=MESH,
            )
            copy.start()
            packets[k] = copy

    for level in range(3, steps):
        present_wait(level)
    for step in range(1, steps + 1):
        packet_start(step)

    def gain_all():
        return pltpu.make_async_remote_copy(
            src_ref=gains.at[pl.ds(0, n - 1)],
            dst_ref=gains.at[pl.ds(0, n - 1)],
            send_sem=gain_send_sem,
            recv_sem=gain_recv_sem,
            device_id={"ap": right},
            device_id_type=MESH,
        )

    for k in range(1, n):
        peer = lax.rem(me + k, n)
        copy = pltpu.make_async_remote_copy(
            src_ref=gain_ref,
            dst_ref=gains.at[me],
            send_sem=gain_send_sem,
            recv_sem=gain_recv_sem,
            device_id={"ap": peer},
            device_id_type=MESH,
        )
        copy.start()
    gains[me] = gain_ref[...]
    relays = {}

    def relay_start(step):
        for k in sorted({step, n - step}):
            packets[k].wait_recv()
            origin = node(lax.rem(spot + n - k, n))
            copy = pltpu.make_async_remote_copy(
                src_ref=packet_all.at[origin, mine_half],
                dst_ref=packet_all.at[origin, mine_half],
                send_sem=relay_send_sem,
                recv_sem=relay_recv_sem.at[k],
                device_id={"sc": 1 - part},
                device_id_type=MESH,
            )
            copy.start()
            relays[k] = copy

    def relay_wait(step):
        for k in sorted({step, n - step}):
            relays[k].wait_recv()

    tiles = tones // LANES
    station_of = lax.broadcasted_iota(jnp.int32, (rows, 1), 0)

    def spread_out(packet, slot):
        high = packet[pieces : pieces + held_rows].reshape(kinds * stations, COARSE)
        low = packet[pieces + held_rows :].reshape(kinds * stations, COARSE)
        cov[slot] = jnp.dot(
            jnp.concatenate([high, high], axis=1),
            spread[...],
            preferred_element_type=jnp.float32,
        ) + jnp.dot(low, spread[:COARSE, :], preferred_element_type=jnp.float32)

    def solve(signals, slot):
        width = min(tones, 4 * LANES)
        for base in range(0, tones, width):
            lanes = slice(base, base + width)

            def entry(at):
                value = jnp.broadcast_to(
                    cov[slot, at * stations : at * stations + 1, lanes], (rows, width)
                )
                for a in range(1, stations):
                    row = jnp.broadcast_to(
                        cov[slot, at * stations + a : at * stations + a + 1, lanes], (rows, width)
                    )
                    value = jnp.where(station_of < a * symbols, value, row)
                return value

            cov_re = [[None] * antennas for _ in range(antennas)]
            cov_im = [[None] * antennas for _ in range(antennas)]
            at = 0
            for i, j in entries:
                cov_re[i][j] = entry(at)
                at += 1
                if i != j:
                    cov_im[i][j] = entry(at)
                    at += 1
            right_side = []
            for i in range(antennas):
                right_side.append(
                    tuple(
                        jnp.concatenate(
                            [
                                signals[a, i, reim, :, lanes].astype(jnp.float32)
                                for a in range(stations)
                            ],
                            axis=0,
                        )
                        for reim in range(2)
                    )
                )
            answer = hermitian_solve(cov_re, cov_im, right_side)
            for i in range(antennas):
                re, im = answer[i]
                solved[slot, i, 0, :, lanes] = re
                solved[slot, i, 1, :, lanes] = im
                solved[slot, i, 2, :, lanes] = re + im

    def prepare(packet, signals, slot):
        spread_out(packet, slot)
        solve(signals, slot)

    def combine(origin, packet, slot):
        coefs = packet[:pieces].reshape(pieces * block, 2 * TAPS)
        for l in range(tiles):
            columns = pl.ds(l * 2 * LANES, 2 * LANES)
            smooth[slot, l] = jnp.dot(coefs, table[:, columns], preferred_element_type=jnp.float32)
        here = pl.ds(pl.multiple_of(origin * block, block), block)
        for l in range(tiles):
            lanes = pl.ds(l * LANES, LANES)
            sums = [[None] * symbols for _ in range(PEER_MAX)]
            for a in range(stations):
                for i in range(antennas):
                    re, im, gap = [], [], []
                    for k in range(PEER_MAX):
                        at = (a * antennas + i) * block + k * CU
                        re.append(smooth[slot, l, pl.ds(at, CU), :LANES])
                        im.append(smooth[slot, l, pl.ds(at, CU), LANES:])
                        gap.append(re[k] - im[k])
                    for s in range(symbols):
                        row = pl.ds(a * symbols + s, 1)
                        sre = solved[slot, i, 0, row, lanes]
                        sim = solved[slot, i, 1, row, lanes]
                        ssum = solved[slot, i, 2, row, lanes]
                        for k in range(PEER_MAX):
                            new = (re[k] * sre, im[k] * sim, gap[k] * ssum)
                            old = sums[k][s]
                            if old is not None:
                                new = tuple(x + y for x, y in zip(old, new))
                            sums[k][s] = new
            for s in range(symbols):
                first = [sums[k][s][0] + sums[k][s][1] for k in range(PEER_MAX)]
                second = [
                    sums[k][s][2] - (sums[k][s][0] - sums[k][s][1]) for k in range(PEER_MAX)
                ]
                for reim, values in ((0, first), (1, second)):
                    share[s * 2 + reim, here, lanes] = jnp.concatenate(values, axis=0).astype(
                        jnp.bfloat16
                    )

    def send_share(origin):
        here = pl.ds(pl.multiple_of(origin * block, block), block)
        copy = pltpu.make_async_copy(
            share.at[:, here], share_hbm.at[:, here], share_sem
        )
        copy.start()

    tasks = [(me, packet_send.at[me], received_ref, 0)]
    for step in range(1, steps + 1):
        for direction in range(2 if step <= n - 1 - n // 2 else 1):
            origin = origin_of(direction, step)
            tasks.append((origin, packet_all.at[origin], signal_all.at[origin], step))

    prepare(*tasks[0][1:3], 0)
    combine(*tasks[0][:2], 0)
    send_share(me)
    if steps > 1:
        ring_step(0, 2)
    relay_start(1)
    relay_wait(1)
    prepare(*tasks[1][1:3], 1)
    advanced = {(c, 1) for c in range(stations)} | {(0, 2)}

    def advance(c, step):
        if step <= steps and (c, step) not in advanced:
            ring_step(c, step)
            advanced.add((c, step))

    for c in range(1, stations):
        advance(c, 2)
    if steps > 1:
        relay_start(2)
    for t in range(1, len(tasks)):
        origin, packet, _, step = tasks[t]
        last = t + 1 == len(tasks)
        after = step if last else tasks[t + 1][3]
        begins = tasks[t - 1][3] < step
        if after == steps > step:
            relay_wait(after)
        combine(origin, packet, t % 2)
        if not last:
            _, following, signals, _ = tasks[t + 1]
            if after == steps > step:
                spread_out(following, (t + 1) % 2)
                for c in range(stations):
                    advance(c, after)
                solve(signals, (t + 1) % 2)
            else:
                if after > step:
                    for c in range(stations):
                        advance(c, after)
                    relay_wait(after)
                prepare(following, signals, (t + 1) % 2)
        send_share(origin)
        if step < after < steps:
            relay_start(after + 1)
        if begins and step < steps:
            advance(0, step + 1)
            if step == 1:
                for c in range(1, stations):
                    advance(c, 2)
        if t == len(tasks) - 3:
            gain_all().wait_recv()
            totals = jnp.zeros((1, users), jnp.float32)
            for p in range(n):
                for a in range(stations):
                    row = serve_u[p * stations + a : p * stations + a + 1] * gains[p, a : a + 1, :]
                    totals = totals + row
            scale = 1.0 / (1.0 + totals)
            held = owner_u == mef
            slot_user = iota((OWN_MAX * CU, users), 0) == jnp.where(held, rank_u * CU + position, -1.0)
            slot_rows = jnp.where(slot_user, 1.0, 0.0)
            slot_scale = jnp.sum(jnp.where(slot_user, scale, 0.0), axis=1, keepdims=True)
            scale_ref[...] = jnp.broadcast_to(slot_scale, (OWN_MAX * CU, LANES))
            hits = []
            for p in range(n):
                goal = jnp.where(
                    held & (served_u[p : p + 1] > 0.5), before_u[p : p + 1] * CU + position, -1.0
                )
                hits.append(jnp.where(iota((block, users), 0) == goal, 1.0, 0.0))
            placement = exact_dot(slot_rows, jnp.concatenate(hits, axis=0), ((1,), (1,)))
            place_ref[...] = placement.astype(jnp.bfloat16)
            place_copies = []
            for source, into in ((place_ref, place_hbm), (scale_ref, scale_hbm)):
                copy = pltpu.make_async_copy(source, into, place_sem.at[1 + len(place_copies)])
                copy.start()
                place_copies.append(copy)

    pltpu.make_async_copy(share, share_hbm, share_sem).wait()
    for copy in place_copies:
        copy.wait()
    for copy in half_copies:
        copy.wait_send()
    gain_all().wait_send()
    for send_sem in (packet_send_sem, relay_send_sem):
        pltpu.make_async_remote_copy(
            src_ref=packet_all.at[pl.ds(0, n - 1), mine_half],
            dst_ref=packet_all.at[pl.ds(0, n - 1), mine_half],
            send_sem=send_sem,
            recv_sem=packet_recv_sem.at[0],
            device_id={"ap": right},
            device_id_type=MESH,
        ).wait_send()
    pltpu.make_async_remote_copy(
        src_ref=signal_all.at[pl.ds(0, n - 1)],
        dst_ref=signal_all.at[pl.ds(0, n - 1)],
        send_sem=ring_send_sem,
        recv_sem=ring_recv_sem.at[0, 0, 0],
        device_id={"ap": right},
        device_id_type=MESH,
    ).wait_send()


def place_kernel(
    place_hbm, scale_hbm, share_hbm, out_hbm, place_ref, scale_ref, share, lines, small_sem, in_sem, out_sem
):
    kinds, _, tones = share.shape
    symbols, tiles = kinds // 2, tones // LANES
    arrivals = []
    for kind in range(kinds):
        arrivals.append(
            pltpu.make_async_copy(share_hbm.at[kind], share.at[kind], in_sem.at[kind])
        )
    smalls = []
    for source, into in ((place_hbm, place_ref), (scale_hbm, scale_ref)):
        copy = pltpu.make_async_copy(source, into, small_sem.at[len(smalls)])
        copy.start()
        smalls.append(copy)
    for copy in arrivals:
        copy.start()
    for copy in smalls:
        copy.wait()
    for copy in arrivals:
        copy.wait()
    copies = []
    for s in range(symbols):
        placed = [
            jnp.dot(place_ref[...], share[s * 2 + reim], preferred_element_type=jnp.float32)
            for reim in range(2)
        ]
        for r in range(OWN_MAX):
            rows = slice(r * CU, (r + 1) * CU)
            scale = scale_ref[rows]
            parts = [
                placed[reim][rows, l * LANES : (l + 1) * LANES] * scale
                for l in range(tiles)
                for reim in range(2)
            ]
            for first in range(0, 2 * tiles, CU):
                square = jnp.stack(parts[first : first + CU], axis=0)
                lines[s, rows, first : first + CU, :] = jnp.transpose(square, (1, 0, 2))
        copy = pltpu.make_async_copy(lines.at[s], out_hbm.at[:, s], out_sem.at[s])
        copy.start()
        copies.append(copy)
    for copy in copies:
        copy.wait()


def ring_functions(mesh):
    n = mesh.shape["ap"]
    half = n // 2

    def plain(q):
        return q

    def node(q):
        upper = q // half
        return (1 - upper) * 2 * q + upper * (2 * (n - q) - 1)

    def place(d):
        odd = d % 2
        return (1 - odd) * (d // 2) + odd * (n - (d + 1) // 2)

    if n % 2:
        return plain, plain
    try:
        axes = list(mesh.axis_names)
        line = np.moveaxis(mesh.devices, axes.index("ap"), 0).reshape(n, -1)[:, 0]
        spots = [tuple(d.coords) for d in line]
        sizes = [max(s[x] for s in spots) + 1 for x in range(3)]

        def length(order):
            far = 0
            for q in range(n):
                one, two = spots[order(q)], spots[order((q + 1) % n)]
                far += sum(
                    min(abs(one[x] - two[x]), sizes[x] - abs(one[x] - two[x])) for x in range(3)
                )
            return far

        if length(plain) < length(node):
            return plain, plain
    except (AttributeError, TypeError):
        pass
    return node, place


def local(
    n,
    parts,
    ring_of,
    unsmoothed_link_guesses,
    received,
    user_power,
    noise_power,
    ap_gain,
    user_cluster,
    serving,
    cluster_owner,
):
    stations, antennas, _, users, tones = unsmoothed_link_guesses.shape
    symbols = received.shape[3]
    pieces = stations * antennas
    block = PEER_MAX * CU
    rows = stations * symbols
    parcels = pieces + 2 * (antennas * antennas * stations // block)
    steps = n // 2
    dma = pltpu.SemaphoreType.DMA
    bf16, f32 = jnp.bfloat16, jnp.float32
    hbm = pl.BlockSpec(memory_space=pltpu.HBM)
    tiles = tones // LANES
    slots = OWN_MAX * CU
    share, place, scale = pl.pallas_call(
        functools.partial(uplink_kernel, n, ring_of),
        out_shape=(
            jax.ShapeDtypeStruct((symbols * 2, n * block, tones), bf16),
            jax.ShapeDtypeStruct((slots, n * block), bf16),
            jax.ShapeDtypeStruct((slots, LANES), f32),
        ),
        in_specs=[hbm] * 12,
        out_specs=(hbm, hbm, hbm),
        scratch_shapes=[
            pltpu.VMEM((n, parcels, block, 2 * TAPS), bf16),
            pltpu.VMEM((n,) + received.shape, bf16),
            pltpu.VMEM(received.shape, bf16),
            pltpu.VMEM((1, users), f32),
            pltpu.VMEM((1, stations), f32),
            pltpu.VMEM((stations, users), f32),
            pltpu.VMEM((1, users), jnp.int32),
            pltpu.VMEM(serving.shape, jnp.int32),
            pltpu.VMEM((1, serving.shape[0]), jnp.int32),
            pltpu.VMEM((stations, antennas, 2, users, tones), bf16),
            pltpu.VMEM((tones, 2 * TAPS), bf16),
            pltpu.VMEM((2 * TAPS, 2 * tones), bf16),
            pltpu.VMEM((2 * TAPS, 2 * COARSE), bf16),
            pltpu.VMEM((2 * COARSE, tones), bf16),
            pltpu.VMEM((pieces, users, 2 * TAPS), bf16),
            pltpu.VMEM((pieces, users, 2 * TAPS), bf16),
            pltpu.VMEM((n, parcels, block, 2 * TAPS), bf16),
            pltpu.VMEM((pieces * users, 2 * TAPS), bf16),
            pltpu.VMEM((n, stations, users), f32),
            pltpu.VMEM((n * block, users), bf16),
            pltpu.VMEM((stations, n * block, LANES), f32),
            pltpu.VMEM((users, LANES), f32),
            pltpu.VMEM((2, pieces * users, COARSE), f32),
            pltpu.VMEM((antennas * antennas * stations, COARSE), f32),
            pltpu.VMEM((2, antennas * antennas * stations, tones), f32),
            pltpu.VMEM((2, antennas, 3, rows, tones), f32),
            pltpu.VMEM((2, tiles, pieces * block, 2 * LANES), f32),
            pltpu.VMEM((symbols * 2, n * block, tones), bf16),
            pltpu.VMEM((slots, n * block), bf16),
            pltpu.VMEM((slots, LANES), f32),
            dma,
            dma((4,)),
            dma((stations,)),
            dma((stations,)),
            dma,
            dma,
            dma,
            dma((n,)),
            dma,
            dma((2, 2 * stations, steps)),
            dma((6,)),
            dma,
            dma((n,)),
            dma,
            dma((3,)),
            pltpu.SemaphoreType.REGULAR((2, steps)),
        ],
        compiler_params=pltpu.CompilerParams(
            collective_id=0, has_side_effects=True, vmem_limit_bytes=VMEM_BYTES
        ),
        name="uplink",
    )(
        unsmoothed_link_guesses,
        received,
        user_power.reshape(1, users),
        noise_power.reshape(1, stations),
        ap_gain,
        user_cluster.reshape(1, users),
        serving,
        cluster_owner.reshape(1, -1),
        jnp.asarray(tap_tables(parts, tones)),
        jnp.asarray(tone_tables(parts, tones)),
        jnp.asarray(coarse_table()),
        jnp.asarray(spread_tables(parts, tones)),
    )
    placed = pl.pallas_call(
        place_kernel,
        out_shape=jax.ShapeDtypeStruct((slots, symbols, tiles * 2, LANES), f32),
        in_specs=[hbm, hbm, hbm],
        out_specs=hbm,
        scratch_shapes=[
            pltpu.VMEM((slots, n * block), bf16),
            pltpu.VMEM((slots, LANES), f32),
            pltpu.VMEM((symbols * 2, n * block, tones), bf16),
            pltpu.VMEM((symbols, slots, tiles * 2, LANES), f32),
            dma((2,)),
            dma((symbols * 2,)),
            dma((symbols,)),
        ],
        compiler_params=pltpu.CompilerParams(vmem_limit_bytes=VMEM_BYTES),
        name="place",
    )(place, scale, share)
    placed = placed.reshape(OWN_MAX, CU, symbols, tiles, 2, LANES)
    placed = jnp.transpose(placed, (0, 1, 2, 4, 3, 5))
    return placed.reshape(OWN_MAX, CU, symbols, 2, tones)


def solution(mesh):
    placed = (
        P(("cell", "ap"), None, None, None, "sc"),
        P(("cell", "ap"), None, None, None, "sc"),
        P("cell"),
        P(("cell", "ap")),
        P(("cell", "ap"), None),
        P("cell"),
        P("cell", None),
        P("cell", None),
    )
    return jax.shard_map(
        functools.partial(local, mesh.shape["ap"], mesh.shape["sc"], ring_functions(mesh)),
        mesh=mesh,
        in_specs=placed,
        out_specs=P(("cell", "ap"), None, None, None, "sc"),
        check_vma=False,
    )
```
